128 devices in a mesh: row: 8 (over y, core), col: 16 (over x, z).
Axes of the slice: x: 4, y: 4, z: 4, core: 2. Of those that a mesh axis runs over, the one named last changes fastest.
Arguments:
- coords: float32 [3, 32, 256, 128], P(None, 'row', 'col'), may hold values from 0 to 256
- sources: float32 [8, 32, 256, 128], P(None, 'row', 'col'), may hold values from -6 to 6
- neighbour_mask: int32 [9, 32, 256], P(None, 'row', 'col'), may hold values 0 or 1
- compress: float32 [32, 256, 32, 128], P('row', 'col'), may hold values from -0.5 to 0.5
- expand: float32 [32, 256, 32, 128], P('row', 'col'), may hold values from -1 to 1
- row_transfer: float32 [2, 8, 16, 32, 32], P(None, 'row', 'col'), may hold values from -0.75 to 0.75
- col_transfer: float32 [2, 8, 16, 32, 32], P(None, 'row', 'col'), may hold values from -0.75 to 0.75
Outputs:
- potential: float32 [8, 32, 256, 128], P(None, 'row', 'col')
The draws below stay inside these ranges and needn't reach their ends.
All inputs are finite; a program needn't handle non-finite values. No bound on the sum of `neighbour_mask` on one device may be relied on, other than what follows from the above.
Results may differ from the reference program's by a relative error of at most 0.0003.
Values sent between devices are 32-bit elements; how exact they have to be, the bound alone decides.
No kernel may reach another device: no remote copies, remote signals or barrier semaphores. Data moves between devices by JAX's collectives and lax.ppermute only.
A program may use at most 64 MiB of HBM per device.

```python
import jax
import jax.numpy as jnp
from jax import lax

LR = 4
LC = 16
LEAF = 128
RANK = 32
NRHS = 8
NLR = 32
NLC = 256
ROW_BITS = 3
COL_BITS = 4
N_ROW = 8
N_COL = 16


def draw_coords(key, part):
    noise = jax.random.uniform(key, (3, NLR, NLC, LEAF), jnp.float32)
    leaf_rows = jnp.arange(NLR, dtype=jnp.float32)[:, None, None]
    leaf_cols = jnp.arange(NLC, dtype=jnp.float32)[None, :, None]
    height = 0.5 * noise[2]
    return jnp.stack([leaf_rows + noise[0], leaf_cols + noise[1], height])


def with_ends(entries, key, smallest, largest):
    extent = entries.shape
    index_at = [jax.random.randint(jax.random.fold_in(key, axis), (), 0, extent[axis]) for axis in range(len(extent))]
    entries = entries.at[tuple(index_at)].set(smallest)
    longest = extent.index(max(extent))
    index_at[longest] = (index_at[longest] + 1) % extent[longest]
    return entries.at[tuple(index_at)].set(largest)


def levels(rng, dims, cuts, smallest, top_value):
    loudness = 1.0
    for position, shards_of in cuts:
        heights = jax.random.uniform(jax.random.fold_in(jax.random.fold_in(rng, 6), position), (shards_of,), jnp.float32, smallest / len(cuts), top_value / len(cuts))
        loudness = loudness * jnp.repeat(jnp.exp(heights), dims[position] // shards_of).reshape((-1,) + (1,) * (len(dims) - 1 - position))
    return loudness


def normal_values(rng, dims, spread, bound, pieces=(), held_as=jnp.bfloat16):
    drawn = jax.random.normal(rng, dims, jnp.float32) * spread
    if len(pieces) > 0:
        drawn = levels(rng, dims, pieces, -0.22, 0.18) * drawn
    return jnp.clip(drawn, min=-bound, max=bound).astype(held_as)


def setup_inputs(seed: int = 0) -> dict:
    streams_of = jax.random.split(jax.random.key(seed), 8)
    coords = draw_coords(jax.random.fold_in(streams_of[7], 71), 0)
    sources = normal_values(streams_of[1], (NRHS, NLR, NLC, LEAF), 1.0, 6.0, ((1, 8), (2, 16)), jnp.float32)
    neighbour_mask = with_ends((jax.random.randint(streams_of[2], (9, NLR, NLC), 0, 4) < 3).astype(jnp.int32), jax.random.fold_in(streams_of[2], 1), 0, 1)
    compress = normal_values(streams_of[3], (NLR, NLC, RANK, LEAF), LEAF ** -0.5, 0.5, ((0, 8), (1, 16)), jnp.float32)
    expand = normal_values(streams_of[4], (NLR, NLC, RANK, LEAF), RANK ** -0.5, 1.0, ((0, 8), (1, 16)), jnp.float32)
    row_transfer = normal_values(streams_of[5], (2, N_ROW, N_COL, RANK, RANK), (2 * RANK) ** -0.5, 0.75, ((1, 8), (2, 16)), jnp.float32)
    col_transfer = normal_values(streams_of[6], (2, N_ROW, N_COL, RANK, RANK), (2 * RANK) ** -0.5, 0.75, ((1, 8), (2, 16)), jnp.float32)
    return {"coords": coords, "sources": sources, "neighbour_mask": neighbour_mask, "compress": compress, "expand": expand, "row_transfer": row_transfer, "col_transfer": col_transfer}


wave_number = 6.0
softening = 0.05
near_scale = 1.0 / 32.0
highest = lax.Precision.HIGHEST

def near_row(window, mask_row):
    leaf_cols = window.shape[2] - 2
    points = window.shape[3]
    target = window[0:3, 1, 1:leaf_cols + 1]
    accumulated = jnp.zeros((window.shape[0] - 3, leaf_cols, points), jnp.float32)
    for row_shift in range(3):
        for col_shift in range(3):
            source_leaf = window[:, row_shift, col_shift:col_shift + leaf_cols]
            distance_sq = jnp.zeros((leaf_cols, points, points), jnp.float32)
            for component in range(3):
                spacing = target[component][:, :, None] - source_leaf[component][:, None, :]
                distance_sq = distance_sq + spacing * spacing
            kernel = jnp.cos(wave_number * jnp.sqrt(distance_sq)) / jnp.sqrt(distance_sq + softening * softening)
            part_sum = jnp.einsum('cts,xcs->xct', kernel, source_leaf[3:], precision=highest)
            weight = mask_row[row_shift * 3 + col_shift].astype(jnp.float32)
            accumulated = accumulated + part_sum * weight[None, :, None]
    return near_scale * accumulated

def near_field(padded, neighbour_mask):

    def one_row(leaf_row):
        window = lax.dynamic_slice_in_dim(padded, leaf_row, 3, 1)
        mask_row = lax.dynamic_index_in_dim(neighbour_mask, leaf_row, 1, keepdims=False)
        return near_row(window, mask_row)
    rows_out = lax.map(one_row, jnp.arange(neighbour_mask.shape[1], dtype=jnp.int32))
    return jnp.transpose(rows_out, (1, 0, 2, 3))

def flip_partner(values, axis_pos, bit):
    shape = values.shape
    split = shape[:axis_pos] + (shape[axis_pos] >> bit + 1, 2, 1 << bit) + shape[axis_pos + 1:]
    return jnp.flip(values.reshape(split), axis_pos + 1).reshape(shape)

def level(coeffs, transfer, axis_pos, bit):
    partner = flip_partner(coeffs, axis_pos, bit)
    own_term = jnp.einsum('rspq,qxrlsm->pxrlsm', transfer[0], coeffs, precision=highest)
    other_term = jnp.einsum('rspq,qxrlsm->pxrlsm', transfer[1], partner, precision=highest)
    return own_term + other_term

def reference(coords, sources, neighbour_mask, compress, expand, row_transfer, col_transfer):
    stacked = jnp.concatenate([coords, sources], axis=0)
    padded = jnp.pad(stacked, ((0, 0), (1, 1), (1, 1), (0, 0)))
    near = near_field(padded, neighbour_mask)
    coeffs = jnp.einsum('lmqs,xlms->qxlm', compress, sources, precision=highest)
    coeffs = coeffs.reshape(RANK, NRHS, N_ROW, LR, N_COL, LC)
    for bit in range(ROW_BITS):
        coeffs = level(coeffs, row_transfer, 2, bit)
    for bit in range(COL_BITS):
        coeffs = level(coeffs, col_transfer, 4, bit)
    coeffs = coeffs.reshape(RANK, NRHS, NLR, NLC)
    far = jnp.einsum('lmqt,qxlm->xlmt', expand, coeffs, precision=highest)
    return near + far
```

```python
import functools

import jax
import jax.numpy as jnp
import numpy as np
from jax import lax
from jax.experimental import pallas as pl
from jax.experimental.pallas import tpu as pltpu
from jax.sharding import PartitionSpec as P

wave_number = 6.0
softening = 0.05
near_scale = 1.0 / 32.0
highest = lax.Precision.HIGHEST
f32, bf16 = jnp.float32, jnp.bfloat16

turns = wave_number / (2.0 * np.pi)
eps_sq = (softening * turns) ** 2
sine = (3.14157435, -5.16695951, 2.54064763, -0.55204997)
b0, b1, b2 = (sine[0] / sine[3], sine[1] / sine[3], sine[2] / sine[3])
half_gain = 1.0 / (2.0 * sine[3] ** 2)
near_gain = -2.0 * sine[3] ** 2 * turns * near_scale

leaf_rows, leaf_cols, points, rank, rhs = 4, 16, 128, 32, 8
leaves = leaf_rows * leaf_cols
side_cols = leaf_cols + 2
padded_leaves = (leaf_rows + 2) * side_cols
stage_items = 2
vmem = pl.BlockSpec(memory_space=pltpu.VMEM)
smem = pl.BlockSpec(memory_space=pltpu.SMEM)


def inside(i, j):
    return 0 <= i < leaf_rows and 0 <= j < leaf_cols


def slot(i, j):
    return (i + 1) * side_cols + j + 1


def offset_index(i, j, si, sj):
    return 3 * (si - i + 1) + sj - j + 1


def pack_item(source, target, both):
    (si, sj), (ti, tj) = source, target
    word = slot(si, sj) | slot(ti, tj) << 7 | offset_index(ti, tj, si, sj) << 14
    if both:
        word |= 1 << 18
    return word | 1 << 19


def interior_items():
    items = []
    for i in range(leaf_rows):
        for j in range(leaf_cols):
            items.append(pack_item((i, j), (i, j), False))
            for di, dj in ((0, 1), (1, -1), (1, 0), (1, 1)):
                if inside(i + di, j + dj):
                    items.append(pack_item((i, j), (i + di, j + dj), True))
    return items


def halo_items():
    items = []
    for i in range(-1, leaf_rows + 1):
        for j in range(-1, leaf_cols + 1):
            if inside(i, j):
                continue
            for di in (-1, 0, 1):
                for dj in (-1, 0, 1):
                    if inside(i + di, j + dj):
                        items.append(pack_item((i, j), (i + di, j + dj), False))
    return items


def item_table(items):
    step = 2 * stage_items
    idle = pack_item((0, 0), (0, 0), False) & ~(1 << 19)
    padded = items + [idle] * (-len(items) % step)
    return np.array(padded + [idle] * step, np.int32), len(padded) // step


def split(value):
    high = value.astype(bf16)
    return high, (value - high.astype(f32)).astype(bf16)


def dot(left, right):
    return jnp.dot(left, right, preferred_element_type=f32)


def dot_t(left, right):
    return lax.dot_general(left, right, (((1,), (1,)), ((), ())), preferred_element_type=f32)


def prep_kernel(coords, sources, rows, halves):
    start = [coords[pl.ds(c * padded_leaves + slot(0, 0), 1), 0:1] for c in range(3)]
    unroll = 4

    def body(step, carry):
        for k in range(unroll):
            leaf = step * unroll + k
            for c in range(3):
                row = coords[pl.ds(c * padded_leaves + leaf, 1), :]
                rows[pl.ds(leaf * 8 + c, 1), :] = (row - start[c]) * turns
            high, low = split(sources[pl.ds(leaf, rhs, stride=padded_leaves), :])
            halves[pl.ds(pl.multiple_of(leaf * 16, 16), 16), :] = jnp.concatenate([high, low], axis=0)
        return carry

    lax.fori_loop(0, padded_leaves // unroll, body, 0)


def near_kernel(trips, table, mask, rows, halves, seed, acc, splat_a, splat_b, kern_a, kern_b):
    acc[...] = seed[...]
    kern_b[...] = jnp.zeros_like(kern_b)

    def fields(at):
        word = table[at]
        return word & 127, word >> 7 & 127, word >> 14 & 15, word >> 18 & 1, word >> 19 & 1

    def spread(at, splat):
        for n in range(stage_items):
            source = fields(at + n)[0]
            for c in range(3):
                row = rows[pl.ds(source * 8 + c, 1), :]
                splat[n, c] = jnp.broadcast_to(row, (points, points)).T

    def evaluate(at, splat, kern):
        for n in range(stage_items):
            target = fields(at + n)[1]
            other = [rows[pl.ds(target * 8 + c, 1), :] for c in range(3)]
            for g in range(points // 32):
                at_rows = slice(32 * g, 32 * g + 32)
                distance_sq = None
                for c in range(3):
                    spacing = splat[n, c, at_rows] - other[c]
                    term = spacing * spacing
                    distance_sq = term if distance_sq is None else distance_sq + term
                safe = jnp.maximum(distance_sq, 1e-30)
                turn = safe * lax.rsqrt(safe)
                f = turn - jnp.round(turn)
                u = f * f
                m = f * (((u + b2) * u + b1) * u + b0)
                value = (m * m - half_gain) * lax.rsqrt(distance_sq + eps_sq)
                high, low = split(value)
                kern[n, 0, at_rows] = high
                kern[n, 1, at_rows] = low

    def mask_of(leaf_slot, k):
        i = leaf_slot // side_cols - 1
        return mask[k, jnp.clip(i, 0, leaf_rows - 1), jnp.clip(leaf_slot - (i + 1) * side_cols - 1, 0, leaf_cols - 1)]

    def apply(at, kern):
        for n in range(stage_items):
            source, target, k, both, valid = fields(at + n)
            high, low = kern[n, 0], kern[n, 1]
            left = halves[pl.ds(pl.multiple_of(source * 16, 16), 16), :]
            got = dot(left, high) + dot(left, low)
            weight = (mask_of(target, k) * valid).astype(f32)
            acc[pl.ds(target * 8, 8), :] += (got[:8] + got[8:]) * weight
            left = halves[pl.ds(pl.multiple_of(target * 16, 16), 16), :]
            got = dot_t(left, high) + dot_t(left, low)
            weight = (mask_of(source, 8 - k) * both).astype(f32)
            acc[pl.ds(source * 8, 8), :] += (got[:8] + got[8:]) * weight

    def body(trip, carry):
        a = trip * 2 * stage_items
        b = a + stage_items
        spread(b, splat_b)
        evaluate(a, splat_a, kern_a)
        apply(jnp.maximum(a - stage_items, 0), kern_b)
        spread(b + stage_items, splat_a)
        evaluate(b, splat_b, kern_b)
        apply(a, kern_a)
        return carry

    spread(0, splat_a)
    lax.fori_loop(0, trips, body, 0)
    apply(trips * 2 * stage_items - stage_items, kern_b)


def near_piece(items, mask, rows, halves, seed):
    table, trips = item_table(items)
    return pl.pallas_call(
        functools.partial(near_kernel, trips),
        out_shape=jax.ShapeDtypeStruct(seed.shape, f32),
        in_specs=[smem, smem, vmem, vmem, vmem],
        out_specs=vmem,
        scratch_shapes=[pltpu.VMEM((stage_items, 3, points, points), f32)] * 2
        + [pltpu.VMEM((stage_items, 2, points, points), bf16)] * 2,
        compiler_params=pltpu.CompilerParams(vmem_limit_bytes=24 << 20),
        cost_estimate=pl.CostEstimate(flops=len(items) * 60 * points * points, bytes_accessed=1 << 20, transcendentals=0),
        name="near",
    )(jnp.asarray(table), mask, rows, halves, seed)


def extended(value, sides, width):
    for axis, dim in sides:
        size, length = (lax.axis_size(axis), value.shape[dim])
        up = [(i, (i + 1) % size) for i in range(size - 1)]
        down = [(j, i) for i, j in up]
        last = lax.slice_in_dim(value, length - width, length, axis=dim)
        initial = lax.slice_in_dim(value, 0, width, axis=dim)
        before = lax.ppermute(last, axis, up)
        after = lax.ppermute(initial, axis, down)
        value = jnp.concatenate([before, value, after], axis=dim)
    return value


def partner_2(block, axis, distance):
    count = lax.axis_size(axis)
    route = []
    for low in range(count):
        high = low | 1 << distance
        if high != low and high < count:
            route += [(low, high), (high, low)]
    return lax.ppermute(block, axis, route)


def pair_level(blocks, coeffs, partner):
    own_term = jnp.dot(blocks[0], coeffs, precision=highest, preferred_element_type=f32)
    other_term = jnp.dot(blocks[1], partner, precision=highest, preferred_element_type=f32)
    return own_term + other_term


def shards(coords, sources, neighbour_mask, compress, expand, row_transfer, col_transfer):
    stacked = jnp.concatenate([coords, sources], axis=0)
    padded = extended(stacked, (("row", 1), ("col", 2)), 1)
    rows, halves = pl.pallas_call(
        prep_kernel,
        out_shape=(
            jax.ShapeDtypeStruct((padded_leaves * 8, points), f32),
            jax.ShapeDtypeStruct((padded_leaves * 16, points), bf16),
        ),
        in_specs=[vmem, vmem],
        out_specs=(vmem, vmem),
        compiler_params=pltpu.CompilerParams(vmem_limit_bytes=16 << 20),
        name="prep",
    )(padded[:3].reshape(-1, points), padded[3:].reshape(-1, points))
    seed = jnp.zeros((padded_leaves * 8, points), f32)
    near = near_piece(interior_items() + halo_items(), neighbour_mask, rows, halves, seed)
    near = near.reshape(leaf_rows + 2, side_cols, rhs, points)[1:-1, 1:-1] * near_gain
    near = jnp.transpose(near, (2, 0, 1, 3))
    coeffs = jnp.einsum("lmqs,xlms->qxlm", compress, sources, precision=highest)
    coeffs = coeffs.reshape(rank, rhs * leaves)
    row_blocks = row_transfer[:, 0, 0]
    for bit in range(lax.axis_size("row").bit_length() - 1):
        partner = partner_2(coeffs, "row", bit)
        coeffs = pair_level(row_blocks, coeffs, partner)
    col_blocks = col_transfer[:, 0, 0]
    for bit in range(lax.axis_size("col").bit_length() - 1):
        partner = partner_2(coeffs, "col", bit)
        coeffs = pair_level(col_blocks, coeffs, partner)
    coeffs = coeffs.reshape(rank, rhs, leaf_rows, leaf_cols)
    far = jnp.einsum("lmqt,qxlm->xlmt", expand, coeffs, precision=highest)
    return near + far


def solution(mesh):
    in_specs = (
        P(None, "row", "col", None),
        P(None, "row", "col", None),
        P(None, "row", "col"),
        P("row", "col", None, None),
        P("row", "col", None, None),
        P(None, "row", "col", None, None),
        P(None, "row", "col", None, None),
    )
    out_specs = P(None, "row", "col", None)
    return jax.shard_map(shards, mesh=mesh, in_specs=in_specs, out_specs=out_specs, check_vma=False)
```

```python
import functools

import jax
import jax.numpy as jnp
import numpy as np
from jax import lax
from jax.experimental import pallas as pl
from jax.experimental.pallas import tpu as pltpu
from jax.sharding import PartitionSpec as P

wave_number = 6.0
softening = 0.05
near_scale = 1.0 / 32.0
highest = lax.Precision.HIGHEST
f32, bf16 = jnp.float32, jnp.bfloat16

turns = wave_number / (2.0 * np.pi)
eps_sq = (softening * turns) ** 2
sine = (3.14157435, -5.16695951, 2.54064763, -0.55204997)
b0, b1, b2 = (sine[0] / sine[3], sine[1] / sine[3], sine[2] / sine[3])
half_gain = 1.0 / (2.0 * sine[3] ** 2)
near_gain = -2.0 * sine[3] ** 2 * turns * near_scale

leaf_rows, leaf_cols, points, rank, rhs = 4, 16, 128, 32, 8
leaves = leaf_rows * leaf_cols
halo_leaves = 48
group = points // rank
groups = leaves // group
batch = 4
vmem = pl.BlockSpec(memory_space=pltpu.VMEM)
smem = pl.BlockSpec(memory_space=pltpu.SMEM)


def params(mib):
    return pltpu.CompilerParams(vmem_limit_bytes=mib << 20)


def cost(cycles):
    return pl.CostEstimate(flops=int(cycles * 400_000), bytes_accessed=1 << 18, transcendentals=0)


def inside(i, j):
    return 0 <= i < leaf_rows and 0 <= j < leaf_cols


def own_slot(i, j):
    return i * leaf_cols + j


def halo_slot(i, j):
    if 0 <= j < leaf_cols:
        return j if i < 0 else leaf_cols + j
    return 2 * leaf_cols + (0 if j < 0 else leaf_rows + 2) + i + 1


def pack_item(source, target, di, dj, both):
    return source | target << 7 | (3 * (di + 1) + dj + 1) << 14 | both << 18 | 1 << 19


def interior_items():
    items = []
    for i in range(leaf_rows):
        for j in range(leaf_cols):
            here = own_slot(i, j)
            items.append(pack_item(here, here, 0, 0, 0))
            for di, dj in ((0, 1), (1, -1), (1, 0), (1, 1)):
                if inside(i + di, j + dj):
                    items.append(pack_item(here, own_slot(i + di, j + dj), -di, -dj, 1))
    return items


def halo_items():
    items = []
    for i in range(-1, leaf_rows + 1):
        for j in range(-1, leaf_cols + 1):
            if inside(i, j):
                continue
            for di in (-1, 0, 1):
                for dj in (-1, 0, 1):
                    if inside(i - di, j - dj):
                        items.append(pack_item(halo_slot(i, j), own_slot(i - di, j - dj), di, dj, 0))
    return items


def item_table(items):
    idle = pack_item(0, 0, 0, 0, 0) & ~(1 << 19)
    padded = items + [idle] * (-len(items) % batch)
    return np.array(padded + [idle] * batch, np.int32), len(padded) // batch


def split(value):
    high = value.astype(bf16)
    return high, (value - high.astype(f32)).astype(bf16)


def thirds(value):
    high = value.astype(bf16).astype(f32)
    rest = value - high
    middle = rest.astype(bf16).astype(f32)
    return high, middle, rest - middle


def dot(left, right):
    return jnp.dot(left, right, preferred_element_type=f32)


def dot_t(left, right):
    return lax.dot_general(left, right, (((1,), (1,)), ((), ())), preferred_element_type=f32)


def dot_tn(left, right):
    return lax.dot_general(left, right, (((0,), (0,)), ((), ())), preferred_element_type=f32)


def sixteen(leaf):
    return pl.ds(leaf * 16 if isinstance(leaf, int) else pl.multiple_of(leaf * 16, 16), 16)


def fill_tables(count, start, coords, sources, tall, right, heights, halves, wide):
    parts = []
    for c in range(3):
        moved = (coords[pl.ds(c * count, count), :] - start[c]) * turns
        if c == 2:
            heights[...] = moved
        else:
            parts.append(thirds(moved))
    k = lax.broadcasted_iota(jnp.int32, (16, points), 0)
    ones_x = jnp.where(k < 3, 1.0, 0.0)
    ones_y = jnp.where((k >= 3) & (k < 6), 1.0, 0.0)
    ones_t = jnp.where((k >= 6) & (k < 9), 1.0, 0.0)
    for role in range(3):
        for leaf in range(count):
            wide[pl.ds(leaf * 16, 16), :] = (ones_t, ones_x, ones_y)[role]
        for first in range(0, count, 8):
            for m in range(3):
                for c in range(2):
                    part = parts[c][m][first : first + 8]
                    if role == 0:
                        wide[pl.ds(first * 16 + 3 * c + m, 8, stride=16), :] = part
                    elif role == c + 1:
                        wide[pl.ds(first * 16 + 6 + m, 8, stride=16), :] = -part
        if role == 0:
            tall[...] = wide[...].astype(bf16)
        else:
            right[:, points * (role - 1) : points * role] = wide[...].astype(bf16)
    for leaf in range(count):
        high, low = split(sources[pl.ds(leaf, rhs, stride=count), :])
        halves[sixteen(leaf), :] = jnp.concatenate([high, low], axis=0)


def lane_block(n):
    return lax.broadcasted_iota(jnp.int32, (rhs, points), 1) // rank == n


def prep_kernel(coords, sources, compress, tall, right, heights, halves, coeffs, wide):
    start = [coords[c * leaves : c * leaves + 1, 0:1] for c in range(3)]
    fill_tables(leaves, start, coords, sources, tall, right, heights, halves, wide)
    for g in range(groups):
        high, low = split(compress[g * points : (g + 1) * points, :])
        got = dot_t(halves[g * 16 * group : (g + 1) * 16 * group, :], jnp.concatenate([high, low], axis=0))
        got = got[:, :points] + got[:, points:]
        total = jnp.zeros((rhs, points), f32)
        for n in range(group):
            total = jnp.where(lane_block(n), got[n * 16 : n * 16 + 8] + got[n * 16 + 8 : n * 16 + 16], total)
        coeffs[g * rhs : (g + 1) * rhs, :] = total


def halo_prep_kernel(start_at, coords, sources, tall, right, heights, halves, wide):
    start = [start_at[c * leaves : c * leaves + 1, 0:1] for c in range(3)]
    fill_tables(halo_leaves, start, coords, sources, tall, right, heights, halves, wide)


def near_kernel(trips, both_ways, table, mask, tall, source_heights, source_halves, right, heights, halves, seed, acc, gap, splat, kern):
    acc[...] = seed[...]
    kern[...] = jnp.zeros_like(kern)

    def fields(at):
        word = table[at]
        return word & 127, word >> 7 & 127, word >> 14 & 15, word >> 18 & 1, word >> 19 & 1

    def subtract(at, n):
        source, target = fields(at + n)[:2]
        gap[n] = dot_tn(tall[sixteen(source), :], right[sixteen(target), :])
        splat[n] = jnp.broadcast_to(source_heights[pl.ds(source, 1), :], (points, points)).T

    def evaluate(at, n):
        target = fields(at + n)[1]
        height = heights[pl.ds(target, 1), :]
        for g in range(points // 32):
            at_rows = slice(32 * g, 32 * g + 32)
            dx, dy, dz = gap[n, at_rows, :points], gap[n, at_rows, points:], splat[n, at_rows] - height
            distance_sq = dx * dx + dy * dy + dz * dz
            safe = jnp.maximum(distance_sq, 1e-30)
            turn = safe * lax.rsqrt(safe)
            f = turn - jnp.round(turn)
            u = f * f
            m = f * (((u + b2) * u + b1) * u + b0)
            value = (m * m - half_gain) * lax.rsqrt(distance_sq + eps_sq)
            high, low = split(value)
            kern[n, at_rows, :points] = high
            kern[n, at_rows, points:] = low

    def weight_of(leaf, k, on):
        return (mask[k, leaf // leaf_cols, leaf % leaf_cols] * on).astype(f32)

    def apply(at, n):
        source, target, k, both, valid = fields(at + n)
        pair = kern[n]
        got = dot(source_halves[sixteen(source), :], pair)
        got = got[:, :points] + got[:, points:]
        acc[pl.ds(target * 8, 8), :] += (got[:8] + got[8:]) * weight_of(target, k, valid)
        if both_ways:
            left = halves[sixteen(target), :]
            got = dot_t(jnp.concatenate([left, left], axis=1), pair)
            acc[pl.ds(source * 8, 8), :] += (got[:8] + got[8:]) * weight_of(source, 8 - k, both)

    def body(trip, carry):
        at = trip * batch
        for n in range(batch):
            apply(jnp.maximum(at - batch, 0), n)
            evaluate(at, n)
            subtract(at + batch, n)
        return carry

    for n in range(batch):
        subtract(0, n)
    lax.fori_loop(0, trips, body, 0)
    for n in range(batch):
        apply((trips - 1) * batch, n)


def near_piece(items, both_ways, mask, source_tables, target_tables, seed):
    table, trips = item_table(items)
    tall, _, source_heights, source_halves = source_tables
    _, right, heights, halves = target_tables
    return pl.pallas_call(
        functools.partial(near_kernel, trips, both_ways),
        out_shape=jax.ShapeDtypeStruct(seed.shape, f32),
        in_specs=[smem, smem] + [vmem] * 7,
        out_specs=vmem,
        scratch_shapes=[
            pltpu.VMEM((batch, points, 2 * points), f32),
            pltpu.VMEM((batch, points, points), f32),
            pltpu.VMEM((batch, points, 2 * points), bf16),
        ],
        compiler_params=params(16),
        cost_estimate=cost(len(items) * 110),
        name="near",
    )(jnp.asarray(table), mask, tall, source_heights, source_halves, right, heights, halves, seed)


def finish_kernel(coeffs, expand, acc, out):
    for g in range(groups):
        mine = coeffs[g * rhs : (g + 1) * rhs, :]
        rows = jnp.concatenate([jnp.where(lane_block(n), mine, 0.0) for n in range(group)], axis=0)
        high, low = split(rows)
        e_high, e_low = split(expand[g * points : (g + 1) * points, :])
        got = dot(jnp.concatenate([high, low], axis=0), jnp.concatenate([e_high, e_low], axis=1))
        got = got[:, :points] + got[:, points:]
        got = got[: group * rhs] + got[group * rhs :]
        for n in range(group):
            leaf = g * group + n
            near = acc[leaf * rhs : (leaf + 1) * rhs, :] * near_gain
            out[pl.ds(leaf, rhs, stride=leaves), :] = near + got[n * rhs : (n + 1) * rhs]


def table_shapes(count):
    return (
        jax.ShapeDtypeStruct((count * 16, points), bf16),
        jax.ShapeDtypeStruct((count * 16, 2 * points), bf16),
        jax.ShapeDtypeStruct((count, points), f32),
        jax.ShapeDtypeStruct((count * 16, points), bf16),
    )


def shifted(value, axis, up):
    size = lax.axis_size(axis)
    route = [(i, i + 1) if up else (i + 1, i) for i in range(size - 1)]
    return lax.ppermute(value, axis, route)


def partner_of(block, axis, distance):
    route = [(i, i ^ (1 << distance)) for i in range(lax.axis_size(axis))]
    return lax.ppermute(block, axis, route)


def level_blocks(transfer):
    spread = jnp.kron(jnp.eye(group, dtype=f32)[None], jnp.swapaxes(transfer[:, 0, 0], 1, 2))
    return spread


def shards(coords, sources, neighbour_mask, compress, expand, row_transfer, col_transfer):
    stacked = jnp.concatenate([coords, sources], axis=0)
    above = shifted(stacked[:, leaf_rows - 1 :], "row", True)
    below = shifted(stacked[:, :1], "row", False)
    flat_coords = coords.reshape(-1, points)
    flat_sources = sources.reshape(-1, points)
    *own, coeffs = pl.pallas_call(
        prep_kernel,
        out_shape=table_shapes(leaves) + (jax.ShapeDtypeStruct((points, points), f32),),
        in_specs=[vmem] * 3,
        out_specs=(vmem,) * 5,
        scratch_shapes=[pltpu.VMEM((leaves * 16, points), f32)],
        compiler_params=params(16),
        cost_estimate=cost(3000),
        name="prep",
    )(flat_coords, flat_sources, compress.reshape(-1, points))
    row_blocks, col_blocks = level_blocks(row_transfer), level_blocks(col_transfer)
    tall_cols = [jnp.concatenate([above[:, :, j : j + 1], stacked[:, :, j : j + 1], below[:, :, j : j + 1]], axis=1) for j in (0, leaf_cols - 1)]
    to_right = shifted(tall_cols[1], "col", True)
    to_left = shifted(tall_cols[0], "col", False)

    levels = [("row", bit, row_blocks) for bit in range(lax.axis_size("row").bit_length() - 1)]
    levels += [("col", bit, col_blocks) for bit in range(lax.axis_size("col").bit_length() - 1)]
    items = interior_items()
    pieces = len(levels) - 1
    cuts = [len(items) * n // pieces // batch * batch for n in range(pieces)] + [len(items)]
    acc = jnp.zeros((leaves * rhs, points), f32)
    for n, (axis, bit, blocks) in enumerate(levels):
        partner = partner_of(coeffs, axis, bit)
        coeffs, acc = lax.optimization_barrier((coeffs, acc))
        if n < pieces:
            acc = near_piece(items[cuts[n] : cuts[n + 1]], True, neighbour_mask, own, own, acc)
        else:
            halo = jnp.concatenate(
                [above[:, 0], below[:, 0], to_right[:, :, 0], to_left[:, :, 0], jnp.zeros((3 + rhs, 4, points), f32)], axis=1
            )
            around = pl.pallas_call(
                halo_prep_kernel,
                out_shape=table_shapes(halo_leaves),
                in_specs=[vmem] * 3,
                out_specs=(vmem,) * 4,
                scratch_shapes=[pltpu.VMEM((halo_leaves * 16, points), f32)],
                compiler_params=params(16),
                cost_estimate=cost(1000),
                name="halo_prep",
            )(flat_coords, halo[:3].reshape(-1, points), halo[3:].reshape(-1, points))
            acc = near_piece(halo_items(), False, neighbour_mask, around, own, acc)
        mine = jnp.dot(coeffs, blocks[0], precision=highest, preferred_element_type=f32)
        partner, acc = lax.optimization_barrier((partner, acc))
        coeffs = mine + jnp.dot(partner, blocks[1], precision=highest, preferred_element_type=f32)
    out = pl.pallas_call(
        finish_kernel,
        out_shape=jax.ShapeDtypeStruct((rhs * leaves, points), f32),
        in_specs=[vmem] * 3,
        out_specs=vmem,
        compiler_params=params(16),
        cost_estimate=cost(2000),
        name="finish",
    )(coeffs, expand.reshape(-1, points), acc)
    return out.reshape(rhs, leaf_rows, leaf_cols, points)


def solution(mesh):
    in_specs = (
        P(None, "row", "col", None),
        P(None, "row", "col", None),
        P(None, "row", "col"),
        P("row", "col", None, None),
        P("row", "col", None, None),
        P(None, "row", "col", None, None),
        P(None, "row", "col", None, None),
    )
    out_specs = P(None, "row", "col", None)
    return jax.shard_map(shards, mesh=mesh, in_specs=in_specs, out_specs=out_specs, check_vma=False)
```

```python
import functools

import jax
import jax.numpy as jnp
import numpy as np
from jax import lax
from jax.experimental import pallas as pl
from jax.experimental.pallas import tpu as pltpu
from jax.sharding import PartitionSpec as P

wave_number = 6.0
softening = 0.05
near_scale = 1.0 / 32.0
highest = lax.Precision.HIGHEST
f32, bf16 = jnp.float32, jnp.bfloat16

turns = wave_number / (2.0 * np.pi)
eps_sq = (softening * turns) ** 2
sine = (3.14157435, -5.16695951, 2.54064763, -0.55204997)
b0, b1, b2 = (sine[0] / sine[3], sine[1] / sine[3], sine[2] / sine[3])
half_gain = 1.0 / (2.0 * sine[3] ** 2)
near_gain = -2.0 * sine[3] ** 2 * turns * near_scale

leaf_rows, leaf_cols, points, rank, rhs = 4, 16, 128, 32, 8
leaves = leaf_rows * leaf_cols
edge_leaves = 2 * leaf_cols
side_leaves = 16
edge_rows = (3 + rhs) * leaf_cols
side_rows = 72
group = points // rank
groups = leaves // group
batch = 4
vmem = pl.BlockSpec(memory_space=pltpu.VMEM)
smem = pl.BlockSpec(memory_space=pltpu.SMEM)


def params(mib):
    return pltpu.CompilerParams(vmem_limit_bytes=mib << 20)


def cost(cycles):
    return pl.CostEstimate(flops=int(cycles * 400_000), bytes_accessed=1 << 18, transcendentals=0)


def inside(i, j):
    return 0 <= i < leaf_rows and 0 <= j < leaf_cols


def own_slot(i, j):
    return i * leaf_cols + j


def halo_slot(i, j):
    if 0 <= j < leaf_cols:
        return j if i < 0 else leaf_cols + j
    return i + 1 if j < 0 else 8 + i + 1


def pack_item(source, target, di, dj, both):
    return source | target << 7 | (3 * (di + 1) + dj + 1) << 14 | both << 18 | 1 << 19


def interior_items():
    items = []
    for i in range(leaf_rows):
        for j in range(leaf_cols):
            here = own_slot(i, j)
            items.append(pack_item(here, here, 0, 0, 0))
            for di, dj in ((0, 1), (1, -1), (1, 0), (1, 1)):
                if inside(i + di, j + dj):
                    items.append(pack_item(here, own_slot(i + di, j + dj), -di, -dj, 1))
    return items


def halo_items(sides):
    items = []
    for i in range(-1, leaf_rows + 1):
        for j in range(-1, leaf_cols + 1):
            if inside(i, j) or sides == (0 <= j < leaf_cols):
                continue
            for di in (-1, 0, 1):
                for dj in (-1, 0, 1):
                    if inside(i - di, j - dj):
                        items.append(pack_item(halo_slot(i, j), own_slot(i - di, j - dj), di, dj, 0))
    return items


def item_table(items):
    idle = pack_item(0, 0, 0, 0, 0) & ~(1 << 19)
    padded = items + [idle] * (-len(items) % (2 * batch))
    return np.array(padded + [idle] * batch, np.int32), len(padded) // (2 * batch)


def split(value):
    high = value.astype(bf16)
    return high, (value - high.astype(f32)).astype(bf16)


def thirds(value):
    high = value.astype(bf16).astype(f32)
    rest = value - high
    middle = rest.astype(bf16).astype(f32)
    return high, middle, rest - middle


def dot(left, right):
    return jnp.dot(left, right, preferred_element_type=f32)


def dot_t(left, right):
    return lax.dot_general(left, right, (((1,), (1,)), ((), ())), preferred_element_type=f32)


def sixteen(leaf):
    return pl.ds(leaf * 16 if isinstance(leaf, int) else pl.multiple_of(leaf * 16, 16), 16)


def fill_tables(count, start, coords, sources, left, right, heights, halves, wide):
    parts = []
    for c in range(3):
        moved = (coords[pl.ds(c * count, count), :] - start[c]) * turns
        if c == 2:
            heights[...] = moved
        else:
            parts.append(thirds(moved))
    k = lax.broadcasted_iota(jnp.int32, (16, points), 0)
    ones_x = jnp.where(k < 3, 1.0, 0.0)
    ones_y = jnp.where((k >= 3) & (k < 6), 1.0, 0.0)
    ones_t = jnp.where((k >= 6) & (k < 9), 1.0, 0.0)
    for role in range(3):
        for leaf in range(count):
            wide[pl.ds(leaf * 16, 16), :] = (ones_t, ones_x, ones_y)[role]
        for first in range(0, count, 8):
            for m in range(3):
                for c in range(2):
                    part = parts[c][m][first : first + 8]
                    if role == 0:
                        wide[pl.ds(first * 16 + 3 * c + m, 8, stride=16), :] = part
                    elif role == c + 1:
                        wide[pl.ds(first * 16 + 6 + m, 8, stride=16), :] = -part
        if role == 0:
            for leaf in range(count):
                left[leaf * points : (leaf + 1) * points, :] = wide[leaf * 16 : leaf * 16 + 16, :].T.astype(bf16)
        else:
            right[:, points * (role - 1) : points * role] = wide[...].astype(bf16)
    for leaf in range(count):
        high, low = split(sources[pl.ds(leaf, rhs, stride=count), :])
        halves[sixteen(leaf), :] = jnp.concatenate([high, low], axis=0)


def lane_block(n):
    return lax.broadcasted_iota(jnp.int32, (rhs, points), 1) // rank == n


def spread_blocks(transfer, blocks):
    same = lax.broadcasted_iota(jnp.int32, (points, points), 0) // rank == lax.broadcasted_iota(jnp.int32, (points, points), 1) // rank
    for n in range(2):
        wide = jnp.concatenate([transfer[n]] * group, axis=1)
        wide = jnp.where(same, jnp.concatenate([wide] * group, axis=0), 0.0)
        blocks[2 * n], blocks[2 * n + 1] = split(wide)


def prep_kernel(place, coords, sources, row_transfer, col_transfer, compress_far, left, right, heights, halves, payload, row_blocks, col_blocks, wide, compress, arrived):
    fetch = pltpu.make_async_copy(compress_far, compress, arrived)
    fetch.start()
    start = [coords[c * leaves : c * leaves + 1, 0:1] for c in range(3)]
    fill_tables(leaves, start, coords, sources, left, right, heights, halves, wide)
    spread_blocks(row_transfer, row_blocks)
    spread_blocks(col_transfer, col_blocks)
    odd = place[0] % 2
    for k in range(2):
        row = (leaf_rows - 1) * (1 - odd if k == 0 else odd)
        for c in range(3 + rhs):
            ref, at = (coords, c) if c < 3 else (sources, c - 3)
            to = points + k * edge_rows + c * leaf_cols
            payload[to : to + leaf_cols, :] = ref[pl.ds(pl.multiple_of(at * leaves + row * leaf_cols, 8), leaf_cols), :]
    fetch.wait()
    for g in range(groups):
        high, low = split(compress[g * points : (g + 1) * points, :])
        got = dot_t(halves[g * 16 * group : (g + 1) * 16 * group, :], jnp.concatenate([high, low], axis=0))
        got = got[:, :points] + got[:, points:]
        total = jnp.zeros((rhs, points), f32)
        for n in range(group):
            total = jnp.where(lane_block(n), got[n * 16 : n * 16 + 8] + got[n * 16 + 8 : n * 16 + 16], total)
        payload[g * rhs : (g + 1) * rhs, :] = total


def halo_prep_kernel(count, start_at, values, left, right, heights, halves, wide):
    start = [start_at[c * leaves : c * leaves + 1, 0:1] for c in range(3)]
    fill_tables(count, start, values.at[: 3 * count], values.at[3 * count :], left, right, heights, halves, wide)


def halo_prep(count, coords, values):
    return pl.pallas_call(
        functools.partial(halo_prep_kernel, count),
        out_shape=table_shapes(count),
        in_specs=[vmem] * 2,
        out_specs=(vmem,) * 4,
        scratch_shapes=[pltpu.VMEM((count * 16, points), f32)],
        compiler_params=params(16),
        cost_estimate=cost(1000),
        name="halo_prep",
    )(coords, values)


def level(mine, theirs, blocks):
    total = None
    for value, n in ((mine, 0), (theirs, 2)):
        high, low = split(value)
        got = dot_t(jnp.concatenate([high, low], axis=0), jnp.concatenate([blocks[n], blocks[n + 1]], axis=0))
        got = got[:, :points] + got[:, points:]
        got = got[:points] + got[points:]
        total = got if total is None else total + got
    return total


def level_kernel(forward, mine, theirs, blocks, payload):
    payload[:points, :] = level(mine[:points, :], theirs[:points, :], blocks)
    payload[points:, :] = theirs[forward:, :]


def turn_kernel(place, mine, theirs, blocks, coords, sources, first, second, payload, edges):
    payload[:points, :] = level(mine[:points, :], theirs[:points, :], blocks)
    row, col = place[0], place[1]
    odd = row % 2 == 1
    around = (row % 4 == 1) | (row % 4 == 2)
    inner = (row > 0) & (row < lax.axis_size("row") - 1)
    for c in range(3 + rhs):
        at = slice(points + c * leaf_cols, points + (c + 1) * leaf_cols)
        near = first[at, :]
        far = jnp.where(inner, jnp.where(around, second[at, :], theirs[at, :]), 0.0)
        edges[c * edge_leaves : c * edge_leaves + leaf_cols, :] = jnp.where(odd, near, far)
        edges[c * edge_leaves + leaf_cols : (c + 1) * edge_leaves, :] = jnp.where(odd, far, near)
    for k in range(2):
        j = (leaf_cols - 1) * (1 - col % 2 if k == 0 else col % 2)
        base = points + k * side_rows
        for c in range(3 + rhs):
            ref, at = (coords, c) if c < 3 else (sources, c - 3)
            payload[base + 6 * c : base + 6 * c + 1, :] = edges[pl.ds(c * edge_leaves + j, 1), :]
            for i in range(leaf_rows):
                payload[base + 6 * c + 1 + i : base + 6 * c + 2 + i, :] = ref[pl.ds(at * leaves + i * leaf_cols + j, 1), :]
            payload[base + 6 * c + 5 : base + 6 * c + 6, :] = edges[pl.ds(c * edge_leaves + leaf_cols + j, 1), :]
        payload[base + 66 : base + side_rows, :] = jnp.zeros((side_rows - 66, points), f32)


def sides_kernel(place, mine, theirs, blocks, first, second, third, coeffs, sides):
    coeffs[...] = level(mine[:points, :], theirs[:points, :], blocks)
    col = place[1]
    odd = col % 2 == 1
    inner = (col > 0) & (col < lax.axis_size("col") - 1)
    at = slice(points, points + side_rows)
    near = first[at, :]
    far = jnp.where((col % 8 == 3) | (col % 8 == 4), third[at, :], theirs[at, :])
    far = jnp.where((col % 4 == 1) | (col % 4 == 2), second[at, :], far)
    far = jnp.where(inner, far, 0.0)
    to_left, to_right = jnp.where(odd, near, far), jnp.where(odd, far, near)
    gap = jnp.zeros((2, points), f32)
    for c in range(3 + rhs):
        at = slice(6 * c, 6 * c + 6)
        sides[c * side_leaves : (c + 1) * side_leaves, :] = jnp.concatenate([to_left[at], gap, to_right[at], gap], axis=0)


def near_kernel(trips, both_ways, table, mask, left, source_heights, source_halves, right, heights, halves, seed, acc, gap_a, gap_b, splat_a, splat_b, kern_a, kern_b):
    acc[...] = seed[...]
    kern_b[...] = jnp.zeros_like(kern_b)
    buffers_a, buffers_b = (gap_a, splat_a, kern_a), (gap_b, splat_b, kern_b)

    def fields(at):
        word = table[at]
        return word & 127, word >> 7 & 127, word >> 14 & 15, word >> 18 & 1, word >> 19 & 1

    def subtract(at, n, gap, splat):
        source, target = fields(at + n)[:2]
        gap[n] = dot(left[pl.ds(pl.multiple_of(source * points, points), points), :], right[sixteen(target), :])
        splat[n] = jnp.broadcast_to(source_heights[pl.ds(source, 1), :], (points, points)).T

    def evaluate(at, n, gap, splat, kern):
        target = fields(at + n)[1]
        height = heights[pl.ds(target, 1), :]
        for g in range(points // 32):
            at_rows = slice(32 * g, 32 * g + 32)
            dx, dy, dz = gap[n, at_rows, :points], gap[n, at_rows, points:], splat[n, at_rows] - height
            distance_sq = dx * dx + dy * dy + dz * dz
            safe = jnp.maximum(distance_sq, 1e-30)
            turn = safe * lax.rsqrt(safe)
            f = turn - jnp.round(turn)
            u = f * f
            m = f * (((u + b2) * u + b1) * u + b0)
            value = (m * m - half_gain) * lax.rsqrt(distance_sq + eps_sq)
            high, low = split(value)
            kern[n, 0, at_rows] = high
            kern[n, 1, at_rows] = low

    def weight_of(leaf, k, on):
        return (mask[k, leaf // leaf_cols, leaf % leaf_cols] * on).astype(f32)

    def apply(at, n, kern):
        source, target, k, both, valid = fields(at + n)
        pair = jnp.concatenate([kern[n, 0], kern[n, 1]], axis=1)
        got = dot(source_halves[sixteen(source), :], pair)
        got = got[:, :points] + got[:, points:]
        acc[pl.ds(target * 8, 8), :] += (got[:8] + got[8:]) * weight_of(target, k, valid)
        if both_ways:
            mine = halves[sixteen(target), :]
            got = dot_t(jnp.concatenate([mine, mine], axis=1), pair)
            acc[pl.ds(source * 8, 8), :] += (got[:8] + got[8:]) * weight_of(source, 8 - k, both)

    def stage(at, here, there):
        for n in range(batch):
            apply(jnp.maximum(at - batch, 0), n, there[2])
        for n in range(batch):
            subtract(at + batch, n, *there[:2])
        for n in range(batch):
            evaluate(at, n, *here)

    def body(trip, carry):
        stage(trip * 2 * batch, buffers_a, buffers_b)
        stage(trip * 2 * batch + batch, buffers_b, buffers_a)
        return carry

    for n in range(batch):
        subtract(0, n, *buffers_a[:2])
    lax.fori_loop(0, trips, body, 0)
    for n in range(batch):
        apply(trips * 2 * batch - batch, n, buffers_b[2])


def near_piece(items, both_ways, mask, source_tables, target_tables, seed):
    table, trips = item_table(items)
    left, _, source_heights, source_halves = source_tables
    _, right, heights, halves = target_tables
    return pl.pallas_call(
        functools.partial(near_kernel, trips, both_ways),
        out_shape=jax.ShapeDtypeStruct(seed.shape, f32),
        in_specs=[smem, smem] + [vmem] * 7,
        out_specs=vmem,
        scratch_shapes=[
            shape
            for shape in (
                pltpu.VMEM((batch, points, 2 * points), f32),
                pltpu.VMEM((batch, points, points), f32),
                pltpu.VMEM((batch, 2, points, points), bf16),
            )
            for _ in range(2)
        ],
        compiler_params=params(16),
        cost_estimate=cost(len(items) * 110),
        name="near",
    )(jnp.asarray(table), mask, left, source_heights, source_halves, right, heights, halves, seed)


def finish_kernel(coeffs, expand, acc, out):
    for g in range(groups):
        mine = coeffs[g * rhs : (g + 1) * rhs, :]
        rows = jnp.concatenate([jnp.where(lane_block(n), mine, 0.0) for n in range(group)], axis=0)
        high, low = split(rows)
        e_high, e_low = split(expand[g * points : (g + 1) * points, :])
        got = dot(jnp.concatenate([high, low], axis=0), jnp.concatenate([e_high, e_low], axis=1))
        got = got[:, :points] + got[:, points:]
        got = got[: group * rhs] + got[group * rhs :]
        for n in range(group):
            leaf = g * group + n
            near = acc[leaf * rhs : (leaf + 1) * rhs, :] * near_gain
            out[pl.ds(leaf, rhs, stride=leaves), :] = near + got[n * rhs : (n + 1) * rhs]


def table_shapes(count):
    return (
        jax.ShapeDtypeStruct((count * points, 16), bf16),
        jax.ShapeDtypeStruct((count * 16, 2 * points), bf16),
        jax.ShapeDtypeStruct((count, points), f32),
        jax.ShapeDtypeStruct((count * 16, points), bf16),
    )


def partner_of(block, axis, distance):
    route = [(i, i ^ (1 << distance)) for i in range(lax.axis_size(axis))]
    return lax.ppermute(block, axis, route)


def array(*shape):
    return jax.ShapeDtypeStruct(shape, f32)


def small_call(body, name, out_shape, scalars, *operands):
    single = not isinstance(out_shape, tuple)
    return pl.pallas_call(
        body,
        out_shape=out_shape,
        in_specs=[smem] * scalars + [vmem] * (len(operands) - scalars),
        out_specs=vmem if single else (vmem,) * len(out_shape),
        compiler_params=params(16),
        cost_estimate=cost(600),
        name=name,
    )(*operands)


def shards(coords, sources, neighbour_mask, compress, expand, row_transfer, col_transfer):
    place = jnp.stack([lax.axis_index("row"), lax.axis_index("col")]).astype(jnp.int32)
    coords = coords.reshape(-1, points)
    sources = sources.reshape(-1, points)
    block_shape = jax.ShapeDtypeStruct((4, points, points), bf16)
    *own, payload, row_blocks, col_blocks = pl.pallas_call(
        prep_kernel,
        out_shape=table_shapes(leaves) + (array(points + 2 * edge_rows, points), block_shape, block_shape),
        in_specs=[smem] + [vmem] * 4 + [pl.BlockSpec(memory_space=pl.ANY)],
        out_specs=(vmem,) * 7,
        scratch_shapes=[pltpu.VMEM((leaves * 16, points), f32), pltpu.VMEM((leaves * rank, points), f32), pltpu.SemaphoreType.DMA],
        compiler_params=params(24),
        cost_estimate=cost(3000),
        name="prep",
    )(place, coords, sources, row_transfer[:, 0, 0], col_transfer[:, 0, 0], compress.reshape(-1, points))
    items = interior_items()
    row_items, col_items = halo_items(False), halo_items(True)
    row_bits, col_bits = (lax.axis_size(axis).bit_length() - 1 for axis in ("row", "col"))
    inner_pieces = row_bits + col_bits - 2
    cuts = [len(items) * n // inner_pieces // 8 * 8 for n in range(inner_pieces)] + [len(items)]
    half = len(row_items) // 2 // 8 * 8
    acc = jnp.zeros((leaves * rhs, points), f32)
    above_below = None
    received = []
    for n in range(row_bits + col_bits):
        over_row = n < row_bits
        blocks = row_blocks if over_row else col_blocks
        theirs = partner_of(payload, "row" if over_row else "col", n if over_row else n - row_bits)
        payload, acc = lax.optimization_barrier((payload, acc))
        if n < inner_pieces:
            acc = near_piece(items[cuts[n] : cuts[n + 1]], True, neighbour_mask, own, own, acc)
        else:
            some = row_items[:half] if n == inner_pieces else row_items[half:]
            acc = near_piece(some, False, neighbour_mask, above_below, own, acc)
        theirs, acc = lax.optimization_barrier((theirs, acc))
        received.append(theirs)
        if n == row_bits - 1:
            payload, edges = small_call(
                turn_kernel,
                "turn",
                (array(points + 2 * side_rows, points), array((3 + rhs) * edge_leaves, points)),
                1,
                place, payload, theirs, blocks, coords, sources, received[0], received[1],
            )
        elif n == row_bits + col_bits - 1:
            coeffs, sides = small_call(
                sides_kernel,
                "sides",
                (array(points, points), array((3 + rhs) * side_leaves, points)),
                1,
                place, payload, theirs, blocks, received[row_bits], received[row_bits + 1], received[row_bits + 2],
            )
        else:
            rows = edge_rows if over_row else side_rows
            skip = points + rows if n in (0, row_bits) else points
            payload = small_call(functools.partial(level_kernel, skip), "level", array(points + rows, points), 0, payload, theirs, blocks)
        if n == row_bits:
            above_below = halo_prep(edge_leaves, coords, edges)
    acc = near_piece(col_items, False, neighbour_mask, halo_prep(side_leaves, coords, sides), own, acc)
    out = pl.pallas_call(
        finish_kernel,
        out_shape=array(rhs * leaves, points),
        in_specs=[vmem] * 3,
        out_specs=vmem,
        compiler_params=params(16),
        cost_estimate=cost(2000),
        name="finish",
    )(coeffs, expand.reshape(-1, points), acc)
    return out.reshape(rhs, leaf_rows, leaf_cols, points)


def solution(mesh):
    in_specs = (
        P(None, "row", "col", None),
        P(None, "row", "col", None),
        P(None, "row", "col"),
        P("row", "col", None, None),
        P("row", "col", None, None),
        P(None, "row", "col", None, None),
        P(None, "row", "col", None, None),
    )
    out_specs = P(None, "row", "col", None)
    return jax.shard_map(shards, mesh=mesh, in_specs=in_specs, out_specs=out_specs, check_vma=False)
```

```python
import functools

import jax
import jax.numpy as jnp
import numpy as np
from jax import lax
from jax.experimental import pallas as pl
from jax.experimental.pallas import tpu as pltpu
from jax.sharding import PartitionSpec as P

wave_number = 6.0
softening = 0.05
near_scale = 1.0 / 32.0
highest = lax.Precision.HIGHEST
f32, bf16 = jnp.float32, jnp.bfloat16

turns = wave_number / (2.0 * np.pi)
eps_sq = (softening * turns) ** 2
sine = (3.14157435, -5.16695951, 2.54064763, -0.55204997)
b0, b1, b2 = (sine[0] / sine[3], sine[1] / sine[3], sine[2] / sine[3])
half_gain = 1.0 / (2.0 * sine[3] ** 2)
near_gain = -2.0 * sine[3] ** 2 * turns * near_scale

leaf_rows, leaf_cols, points, rank, rhs = 4, 16, 128, 32, 8
leaves = leaf_rows * leaf_cols
edge_leaves = 2 * leaf_cols
side_leaves = 16
edge_rows = (3 + rhs) * leaf_cols
side_rows = 72
group = points // rank
groups = leaves // group
batch = 4
vmem = pl.BlockSpec(memory_space=pltpu.VMEM)


def params(mib):
    return pltpu.CompilerParams(vmem_limit_bytes=mib << 20)


def cost(cycles):
    return pl.CostEstimate(flops=int(cycles * 400_000), bytes_accessed=1 << 18, transcendentals=0)


class Run:
    def __init__(self, count, skip, source, step, target, offset, both):
        self.count, self.skip, self.source, self.step, self.target = count, skip, source, step, target
        self.offset, self.both = offset, both


def interior_runs():
    across, down = leaf_rows * (leaf_cols - 1), (leaf_rows - 1) * (leaf_cols - 1)
    return [
        Run(leaves, 0, 0, 1, 0, 4, False),
        Run(across, 1, 0, 1, 1, 3, True),
        Run(leaves - leaf_cols, 0, 0, 1, leaf_cols, 1, True),
        Run(down, 1, 0, 1, leaf_cols + 1, 0, True),
        Run(down, 1, 1, 1, leaf_cols, 2, True),
    ]


def edge_runs():
    runs = []
    for first, row, di in ((0, 0, -1), (leaf_cols, leaf_rows - 1, 1)):
        for dj in (-1, 0, 1):
            start = max(0, -dj)
            at = row * leaf_cols + start
            runs.append(Run(leaf_cols - abs(dj), 0, first + start + dj, 1, at, 3 * (di + 1) + dj + 1, False))
    return runs


def side_runs():
    runs = []
    for first, column, dj in ((0, 0, -1), (8, leaf_cols - 1, 1)):
        for di in (-1, 0, 1):
            runs.append(Run(leaf_rows, 0, first + 1 + di, leaf_cols, column, 3 * (di + 1) + dj + 1, False))
    return runs


def cut_runs(runs, first, last):
    pieces, at = [], 0
    for run in runs:
        low, high = max(first - at, 0), min(last - at, run.count)
        if low < high:
            pieces.append((run, low, high))
        at += run.count
    return pieces


zero_row = 9 * leaves


def fields(pieces, at):
    found, begin = None, 0
    for run, low, high in pieces:
        q = at - begin + low
        begin += high - low
        moved = q + (q * 274 >> 12) if run.skip else q
        source, target = moved + run.source, run.step * moved + run.target
        here = [source, target, run.offset * leaves + target, (8 - run.offset) * leaves + source if run.both else zero_row]
        found = here if found is None else [jnp.where(inside_run, old, new) for old, new in zip(found, here)]
        inside_run = at < begin
    idle = [0, 0, zero_row, zero_row]
    return [jnp.where(inside_run, old, new) for old, new in zip(found, idle)]


def split(value):
    high = value.astype(bf16)
    return high, (value - high.astype(f32)).astype(bf16)


def thirds(value):
    high = value.astype(bf16).astype(f32)
    rest = value - high
    middle = rest.astype(bf16).astype(f32)
    return high, middle, rest - middle


def dot(left, right):
    return jnp.dot(left, right, preferred_element_type=f32)


def dot_t(left, right):
    return lax.dot_general(left, right, (((1,), (1,)), ((), ())), preferred_element_type=f32)


def sixteen(leaf):
    return pl.ds(leaf * 16 if isinstance(leaf, int) else pl.multiple_of(leaf * 16, 16), 16)


def fill_tables(count, start, coords, sources, left, right, heights, halves, wide):
    parts = []
    for c in range(3):
        moved = (coords[pl.ds(c * count, count), :] - start[c]) * turns
        if c == 2:
            heights[...] = moved
        else:
            parts.append(thirds(moved))
    k = lax.broadcasted_iota(jnp.int32, (16, points), 0)
    ones_x = jnp.where(k < 3, 1.0, 0.0)
    ones_y = jnp.where((k >= 3) & (k < 6), 1.0, 0.0)
    ones_t = jnp.where((k >= 6) & (k < 9), 1.0, 0.0)
    for role in range(3):
        for leaf in range(count):
            wide[pl.ds(leaf * 16, 16), :] = (ones_t, ones_x, ones_y)[role]
        for first in range(0, count, 8):
            for m in range(3):
                for c in range(2):
                    part = parts[c][m][first : first + 8]
                    if role == 0:
                        wide[pl.ds(first * 16 + 3 * c + m, 8, stride=16), :] = part
                    elif role == c + 1:
                        wide[pl.ds(first * 16 + 6 + m, 8, stride=16), :] = -part
        if role == 0:
            for leaf in range(count):
                left[leaf * points : (leaf + 1) * points, :] = wide[leaf * 16 : leaf * 16 + 16, :].T.astype(bf16)
        else:
            right[:, points * (role - 1) : points * role] = wide[...].astype(bf16)
    for leaf in range(count):
        high, low = split(sources[pl.ds(leaf, rhs, stride=count), :])
        halves[sixteen(leaf), :] = jnp.concatenate([high, low], axis=0)


def lane_block(n):
    return lax.broadcasted_iota(jnp.int32, (rhs, points), 1) // rank == n


def spread_blocks(transfer, blocks):
    same = lax.broadcasted_iota(jnp.int32, (points, points), 0) // rank == lax.broadcasted_iota(jnp.int32, (points, points), 1) // rank
    for n in range(2):
        wide = jnp.concatenate([transfer[n]] * group, axis=1)
        wide = jnp.where(same, jnp.concatenate([wide] * group, axis=0), 0.0)
        blocks[2 * n], blocks[2 * n + 1] = split(wide)


def prep_kernel(
    coords_far, sources_far, mask_far, row_far, col_far, compress_far,
    left, right, heights, halves, payload, row_blocks, col_blocks, weights,
    wide, coords, sources, mask, row_transfer, col_transfer, compress, arrived,
):
    fars = (coords_far, sources_far, compress_far, row_far, col_far, mask_far)
    heres = (coords, sources, compress, row_transfer, col_transfer, mask)
    copies = [pltpu.make_async_copy(far, here, arrived.at[n]) for n, (far, here) in enumerate(zip(fars, heres))]
    for copy in copies:
        copy.start()
    copies[0].wait()
    copies[1].wait()
    start = [coords[c * leaves : c * leaves + 1, 0:1] for c in range(3)]
    fill_tables(leaves, start, coords, sources, left, right, heights, halves, wide)
    odd = lax.axis_index("row") % 2
    for k in range(2):
        row = (leaf_rows - 1) * (1 - odd if k == 0 else odd)
        for c in range(3 + rhs):
            ref, at = (coords, c) if c < 3 else (sources, c - 3)
            to = points + k * edge_rows + c * leaf_cols
            payload[to : to + leaf_cols, :] = ref[pl.ds(pl.multiple_of(at * leaves + row * leaf_cols, 8), leaf_cols), :]
    copies[2].wait()
    for g in range(groups):
        high, low = split(compress[g * points : (g + 1) * points, :])
        got = dot_t(halves[g * 16 * group : (g + 1) * 16 * group, :], jnp.concatenate([high, low], axis=0))
        got = got[:, :points] + got[:, points:]
        total = jnp.zeros((rhs, points), f32)
        for n in range(group):
            total = jnp.where(lane_block(n), got[n * 16 : n * 16 + 8] + got[n * 16 + 8 : n * 16 + 16], total)
        payload[g * rhs : (g + 1) * rhs, :] = total
    for copy in copies[3:]:
        copy.wait()
    spread_blocks(row_transfer, row_blocks)
    spread_blocks(col_transfer, col_blocks)
    diagonal = lax.broadcasted_iota(jnp.int32, (leaf_cols, leaf_cols), 0) == lax.broadcasted_iota(jnp.int32, (leaf_cols, leaf_cols), 1)
    ones = jnp.ones((leaf_cols, points), bf16)
    for k in range(9):
        for i in range(leaf_rows):
            spread = jnp.where(diagonal, mask[k, i : i + 1, :].astype(f32), 0.0).astype(bf16)
            at = k * leaves + i * leaf_cols
            weights[at : at + leaf_cols, :] = dot(spread, ones)
    weights[zero_row : zero_row + 8, :] = jnp.zeros((8, points), f32)


def halo_prep_kernel(count, start_at, values, left, right, heights, halves, wide):
    start = [start_at[c * leaves : c * leaves + 1, 0:1] for c in range(3)]
    fill_tables(count, start, values.at[: 3 * count], values.at[3 * count :], left, right, heights, halves, wide)


def halo_prep(count, coords, values):
    return pl.pallas_call(
        functools.partial(halo_prep_kernel, count),
        out_shape=table_shapes(count),
        in_specs=[vmem] * 2,
        out_specs=(vmem,) * 4,
        scratch_shapes=[pltpu.VMEM((count * 16, points), f32)],
        compiler_params=params(16),
        cost_estimate=cost(1000),
        name="halo_prep",
    )(coords, values)


def level(mine, theirs, blocks):
    total = None
    for value, n in ((mine, 0), (theirs, 2)):
        high, low = split(value)
        got = dot_t(jnp.concatenate([high, low], axis=0), jnp.concatenate([blocks[n], blocks[n + 1]], axis=0))
        got = got[:, :points] + got[:, points:]
        got = got[:points] + got[points:]
        total = got if total is None else total + got
    return total


def level_kernel(forward, mine, theirs, blocks, payload):
    payload[:points, :] = level(mine[:points, :], theirs[:points, :], blocks)
    payload[points:, :] = theirs[forward:, :]


def turn_kernel(mine, theirs, blocks, coords, sources, first, second, payload, edges):
    payload[:points, :] = level(mine[:points, :], theirs[:points, :], blocks)
    row, col = lax.axis_index("row"), lax.axis_index("col")
    odd = row % 2 == 1
    around = (row % 4 == 1) | (row % 4 == 2)
    inner = (row > 0) & (row < lax.axis_size("row") - 1)
    for c in range(3 + rhs):
        at = slice(points + c * leaf_cols, points + (c + 1) * leaf_cols)
        near = first[at, :]
        far = jnp.where(inner, jnp.where(around, second[at, :], theirs[at, :]), 0.0)
        edges[c * edge_leaves : c * edge_leaves + leaf_cols, :] = jnp.where(odd, near, far)
        edges[c * edge_leaves + leaf_cols : (c + 1) * edge_leaves, :] = jnp.where(odd, far, near)
    for k in range(2):
        j = (leaf_cols - 1) * (1 - col % 2 if k == 0 else col % 2)
        base = points + k * side_rows
        for c in range(3 + rhs):
            ref, at = (coords, c) if c < 3 else (sources, c - 3)
            payload[base + 6 * c : base + 6 * c + 1, :] = edges[pl.ds(c * edge_leaves + j, 1), :]
            for i in range(leaf_rows):
                payload[base + 6 * c + 1 + i : base + 6 * c + 2 + i, :] = ref[pl.ds(at * leaves + i * leaf_cols + j, 1), :]
            payload[base + 6 * c + 5 : base + 6 * c + 6, :] = edges[pl.ds(c * edge_leaves + leaf_cols + j, 1), :]
        payload[base + 66 : base + side_rows, :] = jnp.zeros((side_rows - 66, points), f32)


def sides_kernel(mine, theirs, blocks, first, second, third, coeffs, sides):
    coeffs[...] = level(mine[:points, :], theirs[:points, :], blocks)
    col = lax.axis_index("col")
    odd = col % 2 == 1
    inner = (col > 0) & (col < lax.axis_size("col") - 1)
    at = slice(points, points + side_rows)
    near = first[at, :]
    far = jnp.where((col % 8 == 3) | (col % 8 == 4), third[at, :], theirs[at, :])
    far = jnp.where((col % 4 == 1) | (col % 4 == 2), second[at, :], far)
    far = jnp.where(inner, far, 0.0)
    to_left, to_right = jnp.where(odd, near, far), jnp.where(odd, far, near)
    gap = jnp.zeros((2, points), f32)
    for c in range(3 + rhs):
        at = slice(6 * c, 6 * c + 6)
        sides[c * side_leaves : (c + 1) * side_leaves, :] = jnp.concatenate([to_left[at], gap, to_right[at], gap], axis=0)


def near_kernel(pieces, trips, both_ways, weights, left, source_heights, source_halves, right, heights, halves, seed, acc, gap_a, gap_b, splat_a, splat_b, kern_a, kern_b):
    acc[...] = seed[...]
    kern_b[...] = jnp.zeros_like(kern_b)
    buffers_a, buffers_b = (gap_a, splat_a, kern_a), (gap_b, splat_b, kern_b)

    def subtract(item, n, gap, splat):
        source, target = item[:2]
        gap[n] = dot(left[pl.ds(pl.multiple_of(source * points, points), points), :], right[sixteen(target), :])
        splat[n] = jnp.broadcast_to(source_heights[pl.ds(source, 1), :], (points, points)).T

    def evaluate(item, n, gap, splat, kern):
        height = heights[pl.ds(item[1], 1), :]
        for g in range(points // 32):
            at_rows = slice(32 * g, 32 * g + 32)
            dx, dy, dz = gap[n, at_rows, :points], gap[n, at_rows, points:], splat[n, at_rows] - height
            distance_sq = dx * dx + dy * dy + dz * dz
            safe = jnp.maximum(distance_sq, 1e-30)
            turn = safe * lax.rsqrt(safe)
            f = turn - jnp.round(turn)
            u = f * f
            m = f * (((u + b2) * u + b1) * u + b0)
            value = (m * m - half_gain) * lax.rsqrt(distance_sq + eps_sq)
            high, low = split(value)
            kern[n, 0, at_rows] = high
            kern[n, 1, at_rows] = low

    def apply(item, n, kern):
        source, target, target_weight, source_weight = item
        pair = jnp.concatenate([kern[n, 0], kern[n, 1]], axis=1)
        got = dot(source_halves[sixteen(source), :], pair)
        got = got[:, :points] + got[:, points:]
        acc[pl.ds(target * 8, 8), :] += (got[:8] + got[8:]) * weights[pl.ds(target_weight, 1), :]
        if both_ways:
            mine = halves[sixteen(target), :]
            got = dot_t(jnp.concatenate([mine, mine], axis=1), pair)
            acc[pl.ds(source * 8, 8), :] += (got[:8] + got[8:]) * weights[pl.ds(source_weight, 1), :]

    def items_at(at):
        return [fields(pieces, at + n) for n in range(batch)]

    def stage(at, earlier, now, here, there):
        later = items_at(at + batch)
        for n in range(batch):
            apply(earlier[n], n, there[2])
        for n in range(batch):
            subtract(later[n], n, *there[:2])
        for n in range(batch):
            evaluate(now[n], n, *here)
        return now, later

    def body(trip, carry):
        carry = stage(trip * 2 * batch, *carry, buffers_a, buffers_b)
        return stage(trip * 2 * batch + batch, *carry, buffers_b, buffers_a)

    first = items_at(jnp.int32(0))
    for n in range(batch):
        subtract(first[n], n, *buffers_a[:2])
    nothing = [[jnp.int32(0), jnp.int32(0), jnp.int32(zero_row), jnp.int32(zero_row)]] * batch
    last, _ = lax.fori_loop(0, trips, body, (nothing, first))
    for n in range(batch):
        apply(last[n], n, buffers_b[2])


def near_piece(pieces, both_ways, weights, source_tables, target_tables, seed):
    count = sum(high - low for _, low, high in pieces)
    trips = -(-count // (2 * batch))
    left, _, source_heights, source_halves = source_tables
    _, right, heights, halves = target_tables
    return pl.pallas_call(
        functools.partial(near_kernel, pieces, trips, both_ways),
        out_shape=jax.ShapeDtypeStruct(seed.shape, f32),
        in_specs=[vmem] * 8,
        out_specs=vmem,
        scratch_shapes=[
            shape
            for shape in (
                pltpu.VMEM((batch, points, 2 * points), f32),
                pltpu.VMEM((batch, points, points), f32),
                pltpu.VMEM((batch, 2, points, points), bf16),
            )
            for _ in range(2)
        ],
        compiler_params=params(16),
        cost_estimate=cost(count * 110),
        name="near",
    )(weights, left, source_heights, source_halves, right, heights, halves, seed)


def finish_kernel(coeffs, expand, acc, out):
    for g in range(groups):
        mine = coeffs[g * rhs : (g + 1) * rhs, :]
        rows = jnp.concatenate([jnp.where(lane_block(n), mine, 0.0) for n in range(group)], axis=0)
        high, low = split(rows)
        e_high, e_low = split(expand[g * points : (g + 1) * points, :])
        got = dot(jnp.concatenate([high, low], axis=0), jnp.concatenate([e_high, e_low], axis=1))
        got = got[:, :points] + got[:, points:]
        got = got[: group * rhs] + got[group * rhs :]
        for n in range(group):
            leaf = g * group + n
            near = acc[leaf * rhs : (leaf + 1) * rhs, :] * near_gain
            out[pl.ds(leaf, rhs, stride=leaves), :] = near + got[n * rhs : (n + 1) * rhs]


def table_shapes(count):
    return (
        jax.ShapeDtypeStruct((count * points, 16), bf16),
        jax.ShapeDtypeStruct((count * 16, 2 * points), bf16),
        jax.ShapeDtypeStruct((count, points), f32),
        jax.ShapeDtypeStruct((count * 16, points), bf16),
    )


def partner_of(block, axis, distance):
    route = [(i, i ^ (1 << distance)) for i in range(lax.axis_size(axis))]
    return lax.ppermute(block, axis, route)


def array(*shape):
    return jax.ShapeDtypeStruct(shape, f32)


def small_call(body, name, out_shape, *operands):
    single = not isinstance(out_shape, tuple)
    return pl.pallas_call(
        body,
        out_shape=out_shape,
        in_specs=[vmem] * len(operands),
        out_specs=vmem if single else (vmem,) * len(out_shape),
        compiler_params=params(16),
        cost_estimate=cost(600),
        name=name,
    )(*operands)


def shards(coords, sources, neighbour_mask, compress, expand, row_transfer, col_transfer):
    coords = coords.reshape(-1, points)
    sources = sources.reshape(-1, points)
    block_shape = jax.ShapeDtypeStruct((4, points, points), bf16)
    *own, payload, row_blocks, col_blocks, weights = pl.pallas_call(
        prep_kernel,
        out_shape=table_shapes(leaves) + (array(points + 2 * edge_rows, points), block_shape, block_shape, array(zero_row + 8, points)),
        in_specs=[pl.BlockSpec(memory_space=pl.ANY)] * 6,
        out_specs=(vmem,) * 8,
        scratch_shapes=[
            pltpu.VMEM((leaves * 16, points), f32),
            pltpu.VMEM((3 * leaves, points), f32),
            pltpu.VMEM((rhs * leaves, points), f32),
            pltpu.VMEM((9, leaf_rows, leaf_cols), jnp.int32),
            pltpu.VMEM((2, rank, rank), f32),
            pltpu.VMEM((2, rank, rank), f32),
            pltpu.VMEM((leaves * rank, points), f32),
            pltpu.SemaphoreType.DMA((6,)),
        ],
        compiler_params=params(24),
        cost_estimate=cost(3000),
        name="prep",
    )(coords, sources, neighbour_mask, row_transfer[:, 0, 0], col_transfer[:, 0, 0], compress.reshape(-1, points))
    row_bits, col_bits = (lax.axis_size(axis).bit_length() - 1 for axis in ("row", "col"))
    inner_pieces = row_bits + col_bits - 2
    inner, edge, side = interior_runs(), edge_runs(), side_runs()
    counts = [sum(run.count for run in runs) for runs in (inner, edge, side)]
    cuts = [counts[0] * n // inner_pieces // 8 * 8 for n in range(inner_pieces)] + [counts[0]]
    half = counts[1] // 2 // 8 * 8
    acc = jnp.zeros((leaves * rhs, points), f32)
    above_below = None
    received = []
    for n in range(row_bits + col_bits):
        over_row = n < row_bits
        blocks = row_blocks if over_row else col_blocks
        theirs = partner_of(payload, "row" if over_row else "col", n if over_row else n - row_bits)
        payload, acc = lax.optimization_barrier((payload, acc))
        if n < inner_pieces:
            acc = near_piece(cut_runs(inner, cuts[n], cuts[n + 1]), True, weights, own, own, acc)
        else:
            some = cut_runs(edge, 0, half) if n == inner_pieces else cut_runs(edge, half, counts[1])
            acc = near_piece(some, False, weights, above_below, own, acc)
        theirs, acc = lax.optimization_barrier((theirs, acc))
        received.append(theirs)
        if n == row_bits - 1:
            payload, edges = small_call(
                turn_kernel,
                "turn",
                (array(points + 2 * side_rows, points), array((3 + rhs) * edge_leaves, points)),
                payload, theirs, blocks, coords, sources, received[0], received[1],
            )
        elif n == row_bits + col_bits - 1:
            coeffs, sides = small_call(
                sides_kernel,
                "sides",
                (array(points, points), array((3 + rhs) * side_leaves, points)),
                payload, theirs, blocks, received[row_bits], received[row_bits + 1], received[row_bits + 2],
            )
        else:
            rows = edge_rows if over_row else side_rows
            skip = points + rows if n in (0, row_bits) else points
            payload = small_call(functools.partial(level_kernel, skip), "level", array(points + rows, points), payload, theirs, blocks)
        if n == row_bits:
            above_below = halo_prep(edge_leaves, coords, edges)
    acc = near_piece(cut_runs(side, 0, counts[2]), False, weights, halo_prep(side_leaves, coords, sides), own, acc)
    out = pl.pallas_call(
        finish_kernel,
        out_shape=array(rhs * leaves, points),
        in_specs=[vmem] * 3,
        out_specs=vmem,
        compiler_params=params(16),
        cost_estimate=cost(2000),
        name="finish",
    )(coeffs, expand.reshape(-1, points), acc)
    return out.reshape(rhs, leaf_rows, leaf_cols, points)


def solution(mesh):
    in_specs = (
        P(None, "row", "col", None),
        P(None, "row", "col", None),
        P(None, "row", "col"),
        P("row", "col", None, None),
        P("row", "col", None, None),
        P(None, "row", "col", None, None),
        P(None, "row", "col", None, None),
    )
    out_specs = P(None, "row", "col", None)
    return jax.shard_map(shards, mesh=mesh, in_specs=in_specs, out_specs=out_specs, check_vma=False)
```

```python
import functools

import jax
import jax.numpy as jnp
import numpy as np
from jax import lax
from jax.experimental import pallas as pl
from jax.experimental.pallas import tpu as pltpu
from jax.sharding import PartitionSpec as P

wave_number = 6.0
softening = 0.05
near_scale = 1.0 / 32.0
highest = lax.Precision.HIGHEST
f32, bf16 = jnp.float32, jnp.bfloat16

turns = wave_number / (2.0 * np.pi)
eps_sq = (softening * turns) ** 2
sine = (3.14157435, -5.16695951, 2.54064763, -0.55204997)
b0, b1, b2 = (sine[0] / sine[3], sine[1] / sine[3], sine[2] / sine[3])
half_gain = 1.0 / (2.0 * sine[3] ** 2)
near_gain = -2.0 * sine[3] ** 2 * turns * near_scale

leaf_rows, leaf_cols, points, rank, rhs = 4, 16, 128, 32, 8
leaves = leaf_rows * leaf_cols
edge_leaves = 2 * leaf_cols
halo_leaves = edge_leaves + 16
edge_rows = (3 + rhs) * leaf_cols
side_rows = 72
group = points // rank
groups = leaves // group
batch = 4
vmem = pl.BlockSpec(memory_space=pltpu.VMEM)


def params(mib):
    return pltpu.CompilerParams(vmem_limit_bytes=mib << 20)


def cost(cycles):
    return pl.CostEstimate(flops=int(cycles * 400_000), bytes_accessed=1 << 18, transcendentals=0)


class Run:
    def __init__(self, count, skip, source, step, target, offset, both):
        self.count, self.skip, self.source, self.step, self.target = count, skip, source, step, target
        self.offset, self.both = offset, both


def interior_runs():
    across, down = leaf_rows * (leaf_cols - 1), (leaf_rows - 1) * (leaf_cols - 1)
    return [
        Run(leaves, 0, 0, 1, 0, 4, False),
        Run(across, 1, 0, 1, 1, 3, True),
        Run(leaves - leaf_cols, 0, 0, 1, leaf_cols, 1, True),
        Run(down, 1, 0, 1, leaf_cols + 1, 0, True),
        Run(down, 1, 1, 1, leaf_cols, 2, True),
    ]


def edge_runs():
    runs = []
    for first, row, di in ((0, 0, -1), (leaf_cols, leaf_rows - 1, 1)):
        for dj in (-1, 0, 1):
            start = max(0, -dj)
            at = row * leaf_cols + start
            runs.append(Run(leaf_cols - abs(dj), 0, first + start + dj, 1, at, 3 * (di + 1) + dj + 1, False))
    return runs


def side_runs():
    runs = []
    for first, column, dj in ((edge_leaves, 0, -1), (edge_leaves + 8, leaf_cols - 1, 1)):
        for di in (-1, 0, 1):
            runs.append(Run(leaf_rows, 0, first + 1 + di, leaf_cols, column, 3 * (di + 1) + dj + 1, False))
    return runs


def cut_runs(runs, first, last):
    pieces, at = [], 0
    for run in runs:
        low, high = max(first - at, 0), min(last - at, run.count)
        if low < high:
            pieces.append((run, low, high))
        at += run.count
    return pieces


zero_row = 9 * leaves


def fields(pieces, at):
    found, begin = None, 0
    for run, low, high in pieces:
        q = at - begin + low
        begin += high - low
        moved = q + (q * 274 >> 12) if run.skip else q
        source, target = moved + run.source, run.step * moved + run.target
        here = [source, target, run.offset * leaves + target, (8 - run.offset) * leaves + source if run.both else zero_row]
        found = here if found is None else [jnp.where(inside_run, old, new) for old, new in zip(found, here)]
        inside_run = at < begin
    idle = [0, 0, zero_row, zero_row]
    return [jnp.where(inside_run, old, new) for old, new in zip(found, idle)]


def split(value):
    high = value.astype(bf16)
    return high, (value - high.astype(f32)).astype(bf16)


def thirds(value):
    high = value.astype(bf16).astype(f32)
    rest = value - high
    middle = rest.astype(bf16).astype(f32)
    return high, middle, rest - middle


def dot(left, right):
    return jnp.dot(left, right, preferred_element_type=f32)


def dot_t(left, right):
    return lax.dot_general(left, right, (((1,), (1,)), ((), ())), preferred_element_type=f32)


def sixteen(leaf):
    return pl.ds(leaf * 16 if isinstance(leaf, int) else pl.multiple_of(leaf * 16, 16), 16)


def fill_tables(count, start, coords, left, right, heights, wides):
    parts = []
    for c in range(3):
        moved = (coords[pl.ds(c * count, count), :] - start[c]) * turns
        if c == 2:
            heights[...] = moved
        else:
            parts.append(thirds(moved))
    k = lax.broadcasted_iota(jnp.int32, (16, points), 0)
    ones_x = jnp.where(k < 3, 1.0, 0.0)
    ones_y = jnp.where((k >= 3) & (k < 6), 1.0, 0.0)
    ones_t = jnp.where((k >= 6) & (k < 9), 1.0, 0.0)
    for role in range(3):
        wide = wides.at[role]
        for leaf in range(count):
            wide[pl.ds(leaf * 16, 16), :] = (ones_t, ones_x, ones_y)[role]
        for first in range(0, count, 8):
            for m in range(3):
                for c in range(2):
                    part = parts[c][m][first : first + 8]
                    if role == 0:
                        wide[pl.ds(first * 16 + 3 * c + m, 8, stride=16), :] = part
                    elif role == c + 1:
                        wide[pl.ds(first * 16 + 6 + m, 8, stride=16), :] = -part
        if role == 0:
            for leaf in range(count):
                left[leaf * points : (leaf + 1) * points, :] = wide[leaf * 16 : leaf * 16 + 16, :].T.astype(bf16)
        else:
            right[:, points * (role - 1) : points * role] = wide[...].astype(bf16)


def lane_block(n):
    return lax.broadcasted_iota(jnp.int32, (rhs, points), 1) // rank == n


def spread_blocks(transfer, blocks):
    same = lax.broadcasted_iota(jnp.int32, (points, points), 0) // rank == lax.broadcasted_iota(jnp.int32, (points, points), 1) // rank
    for n in range(2):
        wide = jnp.concatenate([transfer[n]] * group, axis=1)
        wide = jnp.where(same, jnp.concatenate([wide] * group, axis=0), 0.0)
        blocks[2 * n], blocks[2 * n + 1] = split(wide)


def start_copies(fars, heres, arrived):
    copies = [pltpu.make_async_copy(far, here, arrived.at[n]) for n, (far, here) in enumerate(zip(fars, heres))]
    for copy in copies:
        copy.start()
    return copies


def compress_kernel(coords_far, sources_far, compress_far, halves, payload, outer, coords, sources, compress, arrived):
    copies = start_copies((sources_far, coords_far, compress_far), (sources, coords, compress), arrived)
    copies[0].wait()
    for leaf in range(leaves):
        high, low = split(sources[pl.ds(leaf, rhs, stride=leaves), :])
        halves[sixteen(leaf), :] = jnp.concatenate([high, low], axis=0)
    copies[1].wait()
    odd = lax.axis_index("row") % 2
    for k in range(2):
        row = (leaf_rows - 1) * (1 - odd if k == 0 else odd)
        for c in range(3 + rhs):
            ref, at = (coords, c) if c < 3 else (sources, c - 3)
            to = (payload, points + c * leaf_cols) if k == 0 else (outer, c * leaf_cols)
            to[0][to[1] : to[1] + leaf_cols, :] = ref[pl.ds(pl.multiple_of(at * leaves + row * leaf_cols, 8), leaf_cols), :]
    copies[2].wait()
    for g in range(groups):
        high, low = split(compress[g * points : (g + 1) * points, :])
        got = dot_t(halves[g * 16 * group : (g + 1) * 16 * group, :], jnp.concatenate([high, low], axis=0))
        got = got[:, :points] + got[:, points:]
        total = jnp.zeros((rhs, points), f32)
        for n in range(group):
            total = jnp.where(lane_block(n), got[n * 16 : n * 16 + 8] + got[n * 16 + 8 : n * 16 + 16], total)
        payload[g * rhs : (g + 1) * rhs, :] = total


def prep_kernel(coords_far, mask_far, row_far, col_far, left, right, heights, row_blocks, col_blocks, weights, wides, coords, mask, row_transfer, col_transfer, arrived):
    for copy in start_copies((coords_far, mask_far, row_far, col_far), (coords, mask, row_transfer, col_transfer), arrived):
        copy.wait()
    start = [coords[c * leaves : c * leaves + 1, 0:1] for c in range(3)]
    fill_tables(leaves, start, coords, left, right, heights, wides)
    spread_blocks(row_transfer, row_blocks)
    spread_blocks(col_transfer, col_blocks)
    diagonal = lax.broadcasted_iota(jnp.int32, (leaf_cols, leaf_cols), 0) == lax.broadcasted_iota(jnp.int32, (leaf_cols, leaf_cols), 1)
    ones = jnp.ones((leaf_cols, points), bf16)
    for k in range(9):
        for i in range(leaf_rows):
            spread = jnp.where(diagonal, mask[k, i : i + 1, :].astype(f32), 0.0).astype(bf16)
            at = k * leaves + i * leaf_cols
            weights[at : at + leaf_cols, :] = dot(spread, ones)
    weights[zero_row : zero_row + 8, :] = jnp.zeros((8, points), f32)


def halo_kernel(start_at, edges, first, second, left, right, heights, halves, wides, values):
    start = [start_at[c * leaves : c * leaves + 1, 0:1] for c in range(3)]
    odd = lax.axis_index("col") % 2 == 1
    near, far = first[points : points + side_rows, :], second[...]
    to_left, to_right = jnp.where(odd, near, far), jnp.where(odd, far, near)
    gap = jnp.zeros((2, points), f32)
    for c in range(3 + rhs):
        values[c * halo_leaves : c * halo_leaves + edge_leaves, :] = edges[c * edge_leaves : (c + 1) * edge_leaves, :]
        at = slice(6 * c, 6 * c + 6)
        values[c * halo_leaves + edge_leaves : (c + 1) * halo_leaves, :] = jnp.concatenate([to_left[at], gap, to_right[at], gap], axis=0)
    fill_tables(halo_leaves, start, values, left, right, heights, wides)
    for leaf in range(halo_leaves):
        high, low = split(values[pl.ds(3 * halo_leaves + leaf, rhs, stride=halo_leaves), :])
        halves[sixteen(leaf), :] = jnp.concatenate([high, low], axis=0)


def level(mine, theirs, blocks):
    total = None
    for value, n in ((mine, 0), (theirs, 2)):
        high, low = split(value)
        got = dot_t(jnp.concatenate([high, low], axis=0), jnp.concatenate([blocks[n], blocks[n + 1]], axis=0))
        got = got[:, :points] + got[:, points:]
        got = got[:points] + got[points:]
        total = got if total is None else total + got
    return total


def level_kernel(mine, theirs, blocks, payload):
    payload[...] = level(mine[:points, :], theirs[:points, :], blocks)


def turn_kernel(mine, theirs, blocks, coords, sources, first, second, payload, outer, edges):
    payload[:points, :] = level(mine[:points, :], theirs[:points, :], blocks)
    odd = lax.axis_index("row") % 2 == 1
    col = lax.axis_index("col")
    for c in range(3 + rhs):
        near = first[points + c * leaf_cols : points + (c + 1) * leaf_cols, :]
        far = second[c * leaf_cols : (c + 1) * leaf_cols, :]
        edges[c * edge_leaves : c * edge_leaves + leaf_cols, :] = jnp.where(odd, near, far)
        edges[c * edge_leaves + leaf_cols : (c + 1) * edge_leaves, :] = jnp.where(odd, far, near)
    for k in range(2):
        j = (leaf_cols - 1) * (1 - col % 2 if k == 0 else col % 2)
        to, base = (payload, points) if k == 0 else (outer, 0)
        for c in range(3 + rhs):
            ref, at = (coords, c) if c < 3 else (sources, c - 3)
            to[base + 6 * c : base + 6 * c + 1, :] = edges[pl.ds(c * edge_leaves + j, 1), :]
            for i in range(leaf_rows):
                to[base + 6 * c + 1 + i : base + 6 * c + 2 + i, :] = ref[pl.ds(at * leaves + i * leaf_cols + j, 1), :]
            to[base + 6 * c + 5 : base + 6 * c + 6, :] = edges[pl.ds(c * edge_leaves + leaf_cols + j, 1), :]
        to[base + 66 : base + side_rows, :] = jnp.zeros((side_rows - 66, points), f32)


def near_kernel(pieces, trips, both_ways, weights, left, source_heights, source_halves, right, heights, halves, seed, acc, gap_a, gap_b, splat_a, splat_b, kern_a, kern_b):
    acc[...] = seed[...]
    kern_b[...] = jnp.zeros_like(kern_b)
    buffers_a, buffers_b = (gap_a, splat_a, kern_a), (gap_b, splat_b, kern_b)

    def subtract(item, n, gap, splat):
        source, target = item[:2]
        gap[n] = dot(left[pl.ds(pl.multiple_of(source * points, points), points), :], right[sixteen(target), :])
        splat[n] = jnp.broadcast_to(source_heights[pl.ds(source, 1), :], (points, points)).T

    def evaluate(item, n, gap, splat, kern):
        height = heights[pl.ds(item[1], 1), :]
        for g in range(points // 32):
            at_rows = slice(32 * g, 32 * g + 32)
            dx, dy, dz = gap[n, at_rows, :points], gap[n, at_rows, points:], splat[n, at_rows] - height
            distance_sq = dx * dx + dy * dy + dz * dz
            safe = jnp.maximum(distance_sq, 1e-30)
            turn = safe * lax.rsqrt(safe)
            f = turn - jnp.round(turn)
            u = f * f
            m = f * (((u + b2) * u + b1) * u + b0)
            value = (m * m - half_gain) * lax.rsqrt(distance_sq + eps_sq)
            high, low = split(value)
            kern[n, 0, at_rows] = high
            kern[n, 1, at_rows] = low

    def apply(item, n, kern):
        source, target, target_weight, source_weight = item
        pair = jnp.concatenate([kern[n, 0], kern[n, 1]], axis=1)
        got = dot(source_halves[sixteen(source), :], pair)
        got = got[:, :points] + got[:, points:]
        acc[pl.ds(target * 8, 8), :] += (got[:8] + got[8:]) * weights[pl.ds(target_weight, 1), :]
        if both_ways:
            mine = halves[sixteen(target), :]
            got = dot_t(jnp.concatenate([mine, mine], axis=1), pair)
            acc[pl.ds(source * 8, 8), :] += (got[:8] + got[8:]) * weights[pl.ds(source_weight, 1), :]

    def items_at(at):
        return [fields(pieces, at + n) for n in range(batch)]

    def stage(at, earlier, now, here, there):
        later = items_at(at + batch)
        for n in range(batch):
            apply(earlier[n], n, there[2])
        for n in range(batch):
            subtract(later[n], n, *there[:2])
        for n in range(batch):
            evaluate(now[n], n, *here)
        return now, later

    def body(trip, carry):
        carry = stage(trip * 2 * batch, *carry, buffers_a, buffers_b)
        return stage(trip * 2 * batch + batch, *carry, buffers_b, buffers_a)

    first = items_at(jnp.int32(0))
    for n in range(batch):
        subtract(first[n], n, *buffers_a[:2])
    nothing = [[jnp.int32(0), jnp.int32(0), jnp.int32(zero_row), jnp.int32(zero_row)]] * batch
    last, _ = lax.fori_loop(0, trips, body, (nothing, first))
    for n in range(batch):
        apply(last[n], n, buffers_b[2])


def near_piece(pieces, both_ways, weights, source_tables, target_tables, seed):
    count = sum(high - low for _, low, high in pieces)
    trips = -(-count // (2 * batch))
    left, _, source_heights, source_halves = source_tables
    _, right, heights, halves = target_tables
    return pl.pallas_call(
        functools.partial(near_kernel, pieces, trips, both_ways),
        out_shape=jax.ShapeDtypeStruct(seed.shape, f32),
        in_specs=[vmem] * 8,
        out_specs=vmem,
        scratch_shapes=[
            shape
            for shape in (
                pltpu.VMEM((batch, points, 2 * points), f32),
                pltpu.VMEM((batch, points, points), f32),
                pltpu.VMEM((batch, 2, points, points), bf16),
            )
            for _ in range(2)
        ],
        compiler_params=params(16),
        cost_estimate=cost(count * 110),
        name="near",
    )(weights, left, source_heights, source_halves, right, heights, halves, seed)


def finish_kernel(mine, theirs, blocks, expand, acc, out):
    coeffs = level(mine[...], theirs[...], blocks)
    for g in range(groups):
        here = coeffs[g * rhs : (g + 1) * rhs]
        rows = jnp.concatenate([jnp.where(lane_block(n), here, 0.0) for n in range(group)], axis=0)
        high, low = split(rows)
        e_high, e_low = split(expand[g * points : (g + 1) * points, :])
        got = dot(jnp.concatenate([high, low], axis=0), jnp.concatenate([e_high, e_low], axis=1))
        got = got[:, :points] + got[:, points:]
        got = got[: group * rhs] + got[group * rhs :]
        for n in range(group):
            leaf = g * group + n
            near = acc[leaf * rhs : (leaf + 1) * rhs, :] * near_gain
            out[pl.ds(leaf, rhs, stride=leaves), :] = near + got[n * rhs : (n + 1) * rhs]


def table_shapes(count):
    return (
        jax.ShapeDtypeStruct((count * points, 16), bf16),
        jax.ShapeDtypeStruct((count * 16, 2 * points), bf16),
        jax.ShapeDtypeStruct((count, points), f32),
        jax.ShapeDtypeStruct((count * 16, points), bf16),
    )


def partner_of(block, axis, distance):
    route = [(i, i ^ (1 << distance)) for i in range(lax.axis_size(axis))]
    return lax.ppermute(block, axis, route)


def array(*shape):
    return jax.ShapeDtypeStruct(shape, f32)


def small_call(body, name, out_shape, *operands):
    single = not isinstance(out_shape, tuple)
    return pl.pallas_call(
        body,
        out_shape=out_shape,
        in_specs=[vmem] * len(operands),
        out_specs=vmem if single else (vmem,) * len(out_shape),
        compiler_params=params(16),
        cost_estimate=cost(600),
        name=name,
    )(*operands)


def far_call(body, name, out_shape, scratch, *operands):
    return pl.pallas_call(
        body,
        out_shape=out_shape,
        in_specs=[pl.BlockSpec(memory_space=pltpu.HBM)] * len(operands),
        out_specs=(vmem,) * len(out_shape),
        scratch_shapes=scratch + [pltpu.SemaphoreType.DMA((len(operands),))],
        compiler_params=params(24),
        cost_estimate=cost(2000),
        name=name,
    )(*[pltpu.with_memory_space_constraint(operand, pltpu.HBM) for operand in operands])


def outward(block, axis):
    size = lax.axis_size(axis)
    return lax.ppermute(block, axis, [(i, i + 1 if i % 2 else i - 1) for i in range(1, size - 1)])


def shards(coords, sources, neighbour_mask, compress, expand, row_transfer, col_transfer):
    coords = coords.reshape(-1, points)
    sources = sources.reshape(-1, points)
    halves, payload, outer = far_call(
        compress_kernel,
        "compress",
        (table_shapes(leaves)[3], array(points + edge_rows, points), array(edge_rows, points)),
        [pltpu.VMEM(shape, f32) for shape in ((3 * leaves, points), (rhs * leaves, points), (leaves * rank, points))],
        coords, sources, compress.reshape(-1, points),
    )
    row_bits, col_bits = (lax.axis_size(axis).bit_length() - 1 for axis in ("row", "col"))
    axes = ["row"] * row_bits + ["col"] * col_bits
    bits = [*range(row_bits), *range(col_bits)]
    theirs = partner_of(payload, "row", 0)
    beyond = outward(outer, "row")
    block_shape = jax.ShapeDtypeStruct((4, points, points), bf16)
    coords_later, payload = lax.optimization_barrier((coords, payload))
    left, right, heights, row_blocks, col_blocks, weights = far_call(
        prep_kernel,
        "prep",
        table_shapes(leaves)[:3] + (block_shape, block_shape, array(zero_row + 8, points)),
        [
            pltpu.VMEM((3, leaves * 16, points), f32),
            pltpu.VMEM((3 * leaves, points), f32),
            pltpu.VMEM((9, leaf_rows, leaf_cols), jnp.int32),
            pltpu.VMEM((2, rank, rank), f32),
            pltpu.VMEM((2, rank, rank), f32),
        ],
        coords_later, neighbour_mask, row_transfer[:, 0, 0], col_transfer[:, 0, 0],
    )
    own = left, right, heights, halves
    inner, around = interior_runs(), edge_runs() + side_runs()
    counts = [sum(run.count for run in runs) for runs in (inner, around)]
    windows = row_bits + col_bits - 1
    inner_windows = windows - 2
    step = 2 * batch
    cuts = [counts[0] * n // inner_windows // step * step for n in range(inner_windows)] + [counts[0]]
    half = counts[1] // 2 // step * step
    acc = jnp.zeros((leaves * rhs, points), f32)
    for n, (axis, bit) in enumerate(zip(axes, bits)):
        blocks = row_blocks if axis == "row" else col_blocks
        if n > 0:
            theirs = partner_of(payload, axis, bit)
            if n == row_bits:
                beyond = outward(outer, "col")
                first = theirs
            payload, acc = lax.optimization_barrier((payload, acc))
            if n <= inner_windows:
                acc = near_piece(cut_runs(inner, cuts[n - 1], cuts[n]), True, weights, own, own, acc)
            else:
                some = cut_runs(around, 0, half) if n == windows - 1 else cut_runs(around, half, counts[1])
                acc = near_piece(some, False, weights, halo, own, acc)
            theirs, acc = lax.optimization_barrier((theirs, acc))
            if n == row_bits:
                first = theirs
        else:
            first = theirs
        if n == row_bits - 1:
            payload, outer, edges = small_call(
                turn_kernel,
                "turn",
                (array(points + side_rows, points), array(side_rows, points), array((3 + rhs) * edge_leaves, points)),
                payload, theirs, blocks, coords, sources, first, beyond,
            )
        elif n < windows:
            payload = small_call(level_kernel, "level", array(points, points), payload, theirs, blocks)
        if n == row_bits:
            halo = pl.pallas_call(
                halo_kernel,
                out_shape=table_shapes(halo_leaves),
                in_specs=[vmem] * 4,
                out_specs=(vmem,) * 4,
                scratch_shapes=[pltpu.VMEM((3, halo_leaves * 16, points), f32), pltpu.VMEM(((3 + rhs) * halo_leaves, points), f32)],
                compiler_params=params(16),
                cost_estimate=cost(1000),
                name="halo",
            )(coords, edges, first, beyond)
    out = pl.pallas_call(
        finish_kernel,
        out_shape=array(rhs * leaves, points),
        in_specs=[vmem] * 5,
        out_specs=vmem,
        compiler_params=params(16),
        cost_estimate=cost(2000),
        name="finish",
    )(payload, theirs, blocks, expand.reshape(-1, points), acc)
    return out.reshape(rhs, leaf_rows, leaf_cols, points)


def solution(mesh):
    in_specs = (
        P(None, "row", "col", None),
        P(None, "row", "col", None),
        P(None, "row", "col"),
        P("row", "col", None, None),
        P("row", "col", None, None),
        P(None, "row", "col", None, None),
        P(None, "row", "col", None, None),
    )
    out_specs = P(None, "row", "col", None)
    return jax.shard_map(shards, mesh=mesh, in_specs=in_specs, out_specs=out_specs, check_vma=False)
```

```python
import functools

import jax
import jax.numpy as jnp
import numpy as np
from jax import lax
from jax.experimental import pallas as pl
from jax.experimental.pallas import tpu as pltpu
from jax.sharding import PartitionSpec as P

wave_number = 6.0
softening = 0.05
near_scale = 1.0 / 32.0
highest = lax.Precision.HIGHEST
f32, bf16 = jnp.float32, jnp.bfloat16

turns = wave_number / (2.0 * np.pi)
eps_sq = (softening * turns) ** 2
sine = (3.14157435, -5.16695951, 2.54064763, -0.55204997)
b0, b1, b2 = (sine[0] / sine[3], sine[1] / sine[3], sine[2] / sine[3])
half_gain = 1.0 / (2.0 * sine[3] ** 2)
near_gain = -2.0 * sine[3] ** 2 * turns * near_scale

leaf_rows, leaf_cols, points, rank, rhs = 4, 16, 128, 32, 8
leaves = leaf_rows * leaf_cols
edge_leaves = 2 * leaf_cols
side_leaves = 16
edge_rows = (3 + rhs) * leaf_cols
side_rows = 72
group = points // rank
groups = leaves // group
batch = 4
vmem = pl.BlockSpec(memory_space=pltpu.VMEM)


def params(mib):
    return pltpu.CompilerParams(vmem_limit_bytes=mib << 20)


def cost(cycles):
    return pl.CostEstimate(flops=int(cycles * 400_000), bytes_accessed=1 << 18, transcendentals=0)


class Run:
    def __init__(self, count, skip, source, step, target, offset, both):
        self.count, self.skip, self.source, self.step, self.target = count, skip, source, step, target
        self.offset, self.both = offset, both


def interior_runs():
    across, down = leaf_rows * (leaf_cols - 1), (leaf_rows - 1) * (leaf_cols - 1)
    return [
        Run(leaves, 0, 0, 1, 0, 4, False),
        Run(across, 1, 0, 1, 1, 3, True),
        Run(leaves - leaf_cols, 0, 0, 1, leaf_cols, 1, True),
        Run(down, 1, 0, 1, leaf_cols + 1, 0, True),
        Run(down, 1, 1, 1, leaf_cols, 2, True),
    ]


def edge_runs():
    runs = []
    for first, row, di in ((0, 0, -1), (leaf_cols, leaf_rows - 1, 1)):
        for dj in (-1, 0, 1):
            start = max(0, -dj)
            at = row * leaf_cols + start
            runs.append(Run(leaf_cols - abs(dj), 0, first + start + dj, 1, at, 3 * (di + 1) + dj + 1, False))
    return runs


def side_runs():
    runs = []
    for first, column, dj in ((0, 0, -1), (8, leaf_cols - 1, 1)):
        for di in (-1, 0, 1):
            runs.append(Run(leaf_rows, 0, first + 1 + di, leaf_cols, column, 3 * (di + 1) + dj + 1, False))
    return runs


def cut_runs(runs, first, last):
    pieces, at = [], 0
    for run in runs:
        low, high = max(first - at, 0), min(last - at, run.count)
        if low < high:
            pieces.append((run, low, high))
        at += run.count
    return pieces


zero_row = 9 * leaves


def fields(pieces, at):
    found, begin = None, 0
    for run, low, high in pieces:
        q = at - begin + low
        begin += high - low
        moved = q + (q * 274 >> 12) if run.skip else q
        source, target = moved + run.source, run.step * moved + run.target
        here = [source, target, run.offset * leaves + target, (8 - run.offset) * leaves + source if run.both else zero_row]
        found = here if found is None else [jnp.where(inside_run, old, new) for old, new in zip(found, here)]
        inside_run = at < begin
    idle = [0, 0, zero_row, zero_row]
    return [jnp.where(inside_run, old, new) for old, new in zip(found, idle)]


def split(value):
    high = value.astype(bf16)
    return high, (value - high.astype(f32)).astype(bf16)


def thirds(value):
    high = value.astype(bf16).astype(f32)
    rest = value - high
    middle = rest.astype(bf16).astype(f32)
    return high, middle, rest - middle


def dot(left, right):
    return jnp.dot(left, right, preferred_element_type=f32)


def dot_t(left, right):
    return lax.dot_general(left, right, (((1,), (1,)), ((), ())), preferred_element_type=f32)


def sixteen(leaf):
    return pl.ds(leaf * 16 if isinstance(leaf, int) else pl.multiple_of(leaf * 16, 16), 16)


def fill_tables(count, start, coords, left, right, heights, wides):
    parts = []
    for c in range(3):
        moved = (coords[pl.ds(c * count, count), :] - start[c]) * turns
        if c == 2:
            heights[...] = moved
        else:
            parts.append(thirds(moved))
    k = lax.broadcasted_iota(jnp.int32, (16, points), 0)
    ones_x = jnp.where(k < 3, 1.0, 0.0)
    ones_y = jnp.where((k >= 3) & (k < 6), 1.0, 0.0)
    ones_t = jnp.where((k >= 6) & (k < 9), 1.0, 0.0)
    for role in range(3):
        wide = wides.at[role]
        for leaf in range(count):
            wide[pl.ds(leaf * 16, 16), :] = (ones_t, ones_x, ones_y)[role]
        for first in range(0, count, 8):
            for m in range(3):
                for c in range(2):
                    part = parts[c][m][first : first + 8]
                    if role == 0:
                        wide[pl.ds(first * 16 + 3 * c + m, 8, stride=16), :] = part
                    elif role == c + 1:
                        wide[pl.ds(first * 16 + 6 + m, 8, stride=16), :] = -part
        if role == 0:
            for leaf in range(count):
                left[leaf * points : (leaf + 1) * points, :] = wide[leaf * 16 : leaf * 16 + 16, :].T.astype(bf16)
        else:
            right[:, points * (role - 1) : points * role] = wide[...].astype(bf16)


def lane_block(n):
    return lax.broadcasted_iota(jnp.int32, (rhs, points), 1) // rank == n


def spread_blocks(transfer, blocks):
    same = lax.broadcasted_iota(jnp.int32, (points, points), 0) // rank == lax.broadcasted_iota(jnp.int32, (points, points), 1) // rank
    for n in range(2):
        wide = jnp.concatenate([transfer[n]] * group, axis=1)
        wide = jnp.where(same, jnp.concatenate([wide] * group, axis=0), 0.0)
        blocks[2 * n], blocks[2 * n + 1] = split(wide)


def start_copies(fars, heres, arrived):
    copies = [pltpu.make_async_copy(far, here, arrived.at[n]) for n, (far, here) in enumerate(zip(fars, heres))]
    for copy in copies:
        copy.start()
    return copies


def compress_kernel(coords_far, sources_far, compress_far, halves, payload, coords, sources, compress, arrived):
    copies = start_copies((sources_far, coords_far, compress_far), (sources, coords, compress), arrived)
    copies[0].wait()
    for leaf in range(leaves):
        high, low = split(sources[pl.ds(leaf, rhs, stride=leaves), :])
        halves[sixteen(leaf), :] = jnp.concatenate([high, low], axis=0)
    copies[1].wait()
    odd = lax.axis_index("row") % 2
    for k in range(2):
        row = (leaf_rows - 1) * (1 - odd if k == 0 else odd)
        for c in range(3 + rhs):
            ref, at = (coords, c) if c < 3 else (sources, c - 3)
            to = points + k * edge_rows + c * leaf_cols
            payload[to : to + leaf_cols, :] = ref[pl.ds(pl.multiple_of(at * leaves + row * leaf_cols, 8), leaf_cols), :]
    copies[2].wait()
    for g in range(groups):
        high, low = split(compress[g * points : (g + 1) * points, :])
        got = dot_t(halves[g * 16 * group : (g + 1) * 16 * group, :], jnp.concatenate([high, low], axis=0))
        got = got[:, :points] + got[:, points:]
        total = jnp.zeros((rhs, points), f32)
        for n in range(group):
            total = jnp.where(lane_block(n), got[n * 16 : n * 16 + 8] + got[n * 16 + 8 : n * 16 + 16], total)
        payload[g * rhs : (g + 1) * rhs, :] = total


def prep_kernel(coords_far, mask_far, row_far, col_far, left, right, heights, row_blocks, col_blocks, weights, wides, coords, mask, row_transfer, col_transfer, arrived):
    for copy in start_copies((coords_far, mask_far, row_far, col_far), (coords, mask, row_transfer, col_transfer), arrived):
        copy.wait()
    start = [coords[c * leaves : c * leaves + 1, 0:1] for c in range(3)]
    fill_tables(leaves, start, coords, left, right, heights, wides)
    spread_blocks(row_transfer, row_blocks)
    spread_blocks(col_transfer, col_blocks)
    diagonal = lax.broadcasted_iota(jnp.int32, (leaf_cols, leaf_cols), 0) == lax.broadcasted_iota(jnp.int32, (leaf_cols, leaf_cols), 1)
    ones = jnp.ones((leaf_cols, points), bf16)
    for k in range(9):
        for i in range(leaf_rows):
            spread = jnp.where(diagonal, mask[k, i : i + 1, :].astype(f32), 0.0).astype(bf16)
            at = k * leaves + i * leaf_cols
            weights[at : at + leaf_cols, :] = dot(spread, ones)
    weights[zero_row : zero_row + 8, :] = jnp.zeros((8, points), f32)


def halo_tables(count, coords, values, left, right, heights, halves, wides):
    start = [coords[c * leaves : c * leaves + 1, 0:1] for c in range(3)]
    fill_tables(count, start, values, left, right, heights, wides)
    for leaf in range(count):
        high, low = split(values[pl.ds(3 * count + leaf, rhs, stride=count), :])
        halves[sixteen(leaf), :] = jnp.concatenate([high, low], axis=0)


def edges_kernel(coords, edges, left, right, heights, halves, wides):
    halo_tables(edge_leaves, coords, edges, left, right, heights, halves, wides)


def sides_kernel(coords, first, second, third, fourth, left, right, heights, halves, wides, sides):
    col = lax.axis_index("col")
    odd = col % 2 == 1
    inner = (col > 0) & (col < lax.axis_size("col") - 1)
    at = slice(points, points + side_rows)
    near = first[at, :]
    far = jnp.where((col % 8 == 3) | (col % 8 == 4), third[at, :], fourth[at, :])
    far = jnp.where((col % 4 == 1) | (col % 4 == 2), second[at, :], far)
    far = jnp.where(inner, far, 0.0)
    to_left, to_right = jnp.where(odd, near, far), jnp.where(odd, far, near)
    gap = jnp.zeros((2, points), f32)
    for c in range(3 + rhs):
        at = slice(6 * c, 6 * c + 6)
        sides[c * side_leaves : (c + 1) * side_leaves, :] = jnp.concatenate([to_left[at], gap, to_right[at], gap], axis=0)
    halo_tables(side_leaves, coords, sides, left, right, heights, halves, wides)


def level(mine, theirs, blocks):
    total = None
    for value, n in ((mine, 0), (theirs, 2)):
        high, low = split(value)
        got = dot_t(jnp.concatenate([high, low], axis=0), jnp.concatenate([blocks[n], blocks[n + 1]], axis=0))
        got = got[:, :points] + got[:, points:]
        got = got[:points] + got[points:]
        total = got if total is None else total + got
    return total


def level_kernel(forward, mine, theirs, blocks, payload):
    payload[:points, :] = level(mine[:points, :], theirs[:points, :], blocks)
    payload[points:, :] = theirs[forward:, :]


def turn_kernel(mine, theirs, blocks, coords, sources, first, second, payload, edges):
    payload[:points, :] = level(mine[:points, :], theirs[:points, :], blocks)
    row, col = lax.axis_index("row"), lax.axis_index("col")
    odd = row % 2 == 1
    around = (row % 4 == 1) | (row % 4 == 2)
    inner = (row > 0) & (row < lax.axis_size("row") - 1)
    for c in range(3 + rhs):
        at = slice(points + c * leaf_cols, points + (c + 1) * leaf_cols)
        near = first[at, :]
        far = jnp.where(inner, jnp.where(around, second[at, :], theirs[at, :]), 0.0)
        edges[c * edge_leaves : c * edge_leaves + leaf_cols, :] = jnp.where(odd, near, far)
        edges[c * edge_leaves + leaf_cols : (c + 1) * edge_leaves, :] = jnp.where(odd, far, near)
    for k in range(2):
        j = (leaf_cols - 1) * (1 - col % 2 if k == 0 else col % 2)
        base = points + k * side_rows
        for c in range(3 + rhs):
            ref, at = (coords, c) if c < 3 else (sources, c - 3)
            payload[base + 6 * c : base + 6 * c + 1, :] = edges[pl.ds(c * edge_leaves + j, 1), :]
            for i in range(leaf_rows):
                payload[base + 6 * c + 1 + i : base + 6 * c + 2 + i, :] = ref[pl.ds(at * leaves + i * leaf_cols + j, 1), :]
            payload[base + 6 * c + 5 : base + 6 * c + 6, :] = edges[pl.ds(c * edge_leaves + leaf_cols + j, 1), :]
        payload[base + 66 : base + side_rows, :] = jnp.zeros((side_rows - 66, points), f32)


def near_kernel(pieces, trips, both_ways, weights, left, source_heights, source_halves, right, heights, halves, seed, acc, gap_a, gap_b, splat_a, splat_b, kern_a, kern_b):
    acc[...] = seed[...]
    kern_b[...] = jnp.zeros_like(kern_b)
    buffers_a, buffers_b = (gap_a, splat_a, kern_a), (gap_b, splat_b, kern_b)

    def subtract(item, n, gap, splat):
        source, target = item[:2]
        gap[n] = dot(left[pl.ds(pl.multiple_of(source * points, points), points), :], right[sixteen(target), :])
        splat[n] = jnp.broadcast_to(source_heights[pl.ds(source, 1), :], (points, points)).T

    def evaluate(item, n, gap, splat, kern):
        height = heights[pl.ds(item[1], 1), :]
        for g in range(points // 32):
            at_rows = slice(32 * g, 32 * g + 32)
            dx, dy, dz = gap[n, at_rows, :points], gap[n, at_rows, points:], splat[n, at_rows] - height
            distance_sq = dx * dx + dy * dy + dz * dz
            safe = jnp.maximum(distance_sq, 1e-30)
            turn = safe * lax.rsqrt(safe)
            f = turn - jnp.round(turn)
            u = f * f
            m = f * (((u + b2) * u + b1) * u + b0)
            value = (m * m - half_gain) * lax.rsqrt(distance_sq + eps_sq)
            high, low = split(value)
            kern[n, 0, at_rows] = high
            kern[n, 1, at_rows] = low

    def apply(item, n, kern):
        source, target, target_weight, source_weight = item
        pair = jnp.concatenate([kern[n, 0], kern[n, 1]], axis=1)
        got = dot(source_halves[sixteen(source), :], pair)
        got = got[:, :points] + got[:, points:]
        acc[pl.ds(target * 8, 8), :] += (got[:8] + got[8:]) * weights[pl.ds(target_weight, 1), :]
        if both_ways:
            mine = halves[sixteen(target), :]
            got = dot_t(jnp.concatenate([mine, mine], axis=1), pair)
            acc[pl.ds(source * 8, 8), :] += (got[:8] + got[8:]) * weights[pl.ds(source_weight, 1), :]

    def items_at(at):
        return [fields(pieces, at + n) for n in range(batch)]

    def stage(at, earlier, now, here, there):
        later = items_at(at + batch)
        for n in range(batch):
            apply(earlier[n], n, there[2])
        for n in range(batch):
            subtract(later[n], n, *there[:2])
        for n in range(batch):
            evaluate(now[n], n, *here)
        return now, later

    def body(trip, carry):
        carry = stage(trip * 2 * batch, *carry, buffers_a, buffers_b)
        return stage(trip * 2 * batch + batch, *carry, buffers_b, buffers_a)

    first = items_at(jnp.int32(0))
    for n in range(batch):
        subtract(first[n], n, *buffers_a[:2])
    nothing = [[jnp.int32(0), jnp.int32(0), jnp.int32(zero_row), jnp.int32(zero_row)]] * batch
    last, _ = lax.fori_loop(0, trips, body, (nothing, first))
    for n in range(batch):
        apply(last[n], n, buffers_b[2])


def near_piece(pieces, both_ways, weights, source_tables, target_tables, seed):
    count = sum(high - low for _, low, high in pieces)
    trips = -(-count // (2 * batch))
    left, _, source_heights, source_halves = source_tables
    _, right, heights, halves = target_tables
    return pl.pallas_call(
        functools.partial(near_kernel, pieces, trips, both_ways),
        out_shape=jax.ShapeDtypeStruct(seed.shape, f32),
        in_specs=[vmem] * 8,
        out_specs=vmem,
        scratch_shapes=[
            shape
            for shape in (
                pltpu.VMEM((batch, points, 2 * points), f32),
                pltpu.VMEM((batch, points, points), f32),
                pltpu.VMEM((batch, 2, points, points), bf16),
            )
            for _ in range(2)
        ],
        compiler_params=params(16),
        cost_estimate=cost(count * 110),
        name="near",
    )(weights, left, source_heights, source_halves, right, heights, halves, seed)


def finish_kernel(mine, theirs, blocks, expand, acc, out):
    coeffs = level(mine[:points, :], theirs[:points, :], blocks)
    for g in range(groups):
        here = coeffs[g * rhs : (g + 1) * rhs]
        rows = jnp.concatenate([jnp.where(lane_block(n), here, 0.0) for n in range(group)], axis=0)
        high, low = split(rows)
        e_high, e_low = split(expand[g * points : (g + 1) * points, :])
        got = dot(jnp.concatenate([high, low], axis=0), jnp.concatenate([e_high, e_low], axis=1))
        got = got[:, :points] + got[:, points:]
        got = got[: group * rhs] + got[group * rhs :]
        for n in range(group):
            leaf = g * group + n
            near = acc[leaf * rhs : (leaf + 1) * rhs, :] * near_gain
            out[pl.ds(leaf, rhs, stride=leaves), :] = near + got[n * rhs : (n + 1) * rhs]


def table_shapes(count):
    return (
        jax.ShapeDtypeStruct((count * points, 16), bf16),
        jax.ShapeDtypeStruct((count * 16, 2 * points), bf16),
        jax.ShapeDtypeStruct((count, points), f32),
        jax.ShapeDtypeStruct((count * 16, points), bf16),
    )


def partner_of(block, axis, distance):
    route = [(i, i ^ (1 << distance)) for i in range(lax.axis_size(axis))]
    return lax.ppermute(block, axis, route)


def array(*shape):
    return jax.ShapeDtypeStruct(shape, f32)


def small_call(body, name, out_shape, *operands):
    single = not isinstance(out_shape, tuple)
    return pl.pallas_call(
        body,
        out_shape=out_shape,
        in_specs=[vmem] * len(operands),
        out_specs=vmem if single else (vmem,) * len(out_shape),
        compiler_params=params(16),
        cost_estimate=cost(600),
        name=name,
    )(*operands)


def far_call(body, name, out_shape, scratch, *operands):
    return pl.pallas_call(
        body,
        out_shape=out_shape,
        in_specs=[pl.BlockSpec(memory_space=pltpu.HBM)] * len(operands),
        out_specs=(vmem,) * len(out_shape),
        scratch_shapes=scratch + [pltpu.SemaphoreType.DMA((len(operands),))],
        compiler_params=params(24),
        cost_estimate=cost(2000),
        name=name,
    )(*[pltpu.with_memory_space_constraint(operand, pltpu.HBM) for operand in operands])


def tables_call(body, name, count, scratch, *operands):
    return pl.pallas_call(
        body,
        out_shape=table_shapes(count),
        in_specs=[vmem] * len(operands),
        out_specs=(vmem,) * 4,
        scratch_shapes=[pltpu.VMEM((3, count * 16, points), f32)] + scratch,
        compiler_params=params(16),
        cost_estimate=cost(1000),
        name=name,
    )(*operands)


def shards(coords, sources, neighbour_mask, compress, expand, row_transfer, col_transfer):
    coords = coords.reshape(-1, points)
    sources = sources.reshape(-1, points)
    halves, payload = far_call(
        compress_kernel,
        "compress",
        (table_shapes(leaves)[3], array(points + 2 * edge_rows, points)),
        [pltpu.VMEM(shape, f32) for shape in ((3 * leaves, points), (rhs * leaves, points), (leaves * rank, points))],
        coords, sources, compress.reshape(-1, points),
    )
    row_bits, col_bits = (lax.axis_size(axis).bit_length() - 1 for axis in ("row", "col"))
    axes = ["row"] * row_bits + ["col"] * col_bits
    bits = [*range(row_bits), *range(col_bits)]
    theirs = partner_of(payload, "row", 0)
    block_shape = jax.ShapeDtypeStruct((4, points, points), bf16)
    coords_later, payload = lax.optimization_barrier((coords, payload))
    left, right, heights, row_blocks, col_blocks, weights = far_call(
        prep_kernel,
        "prep",
        table_shapes(leaves)[:3] + (block_shape, block_shape, array(zero_row + 8, points)),
        [
            pltpu.VMEM((3, leaves * 16, points), f32),
            pltpu.VMEM((3 * leaves, points), f32),
            pltpu.VMEM((9, leaf_rows, leaf_cols), jnp.int32),
            pltpu.VMEM((2, rank, rank), f32),
            pltpu.VMEM((2, rank, rank), f32),
        ],
        coords_later, neighbour_mask, row_transfer[:, 0, 0], col_transfer[:, 0, 0],
    )
    own = left, right, heights, halves
    inner, edge, side = interior_runs(), edge_runs(), side_runs()
    counts = [sum(run.count for run in runs) for runs in (inner, edge, side)]
    step = 2 * batch
    windows = row_bits + col_bits - 1
    edge_windows = (row_bits, row_bits + 2)
    inner_windows = [n for n in range(1, windows + 1) if n not in edge_windows]
    cuts = [counts[0] * k // len(inner_windows) // step * step for k in range(len(inner_windows))] + [counts[0]]
    half = -(-counts[1] // 2 // step) * step
    acc = jnp.zeros((leaves * rhs, points), f32)
    received = [theirs]
    for n, (axis, bit) in enumerate(zip(axes, bits)):
        blocks = row_blocks if axis == "row" else col_blocks
        if n > 0:
            theirs = partner_of(payload, axis, bit)
            payload, acc = lax.optimization_barrier((payload, acc))
            if n == row_bits:
                edges, acc = lax.optimization_barrier((edges, acc))
                edge_tables = tables_call(edges_kernel, "edges", edge_leaves, [], coords, edges)
            if n in edge_windows:
                some = cut_runs(edge, 0, half) if n == row_bits else cut_runs(edge, half, counts[1])
                acc = near_piece(some, False, weights, edge_tables, own, acc)
            else:
                k = inner_windows.index(n)
                acc = near_piece(cut_runs(inner, cuts[k], cuts[k + 1]), True, weights, own, own, acc)
            theirs, acc = lax.optimization_barrier((theirs, acc))
            received.append(theirs)
        if n == row_bits - 1:
            payload, edges = small_call(
                turn_kernel,
                "turn",
                (array(points + 2 * side_rows, points), array((3 + rhs) * edge_leaves, points)),
                payload, theirs, blocks, coords, sources, received[0], received[1],
            )
        elif n < windows:
            rows = edge_rows if axis == "row" else side_rows
            skip = points + rows if bit == 0 else points
            payload = small_call(functools.partial(level_kernel, skip), "level", array(points + rows, points), payload, theirs, blocks)
    side_tables = tables_call(sides_kernel, "sides", side_leaves, [pltpu.VMEM(((3 + rhs) * side_leaves, points), f32)], coords, *received[row_bits:])
    acc = near_piece(cut_runs(side, 0, counts[2]), False, weights, side_tables, own, acc)
    out = pl.pallas_call(
        finish_kernel,
        out_shape=array(rhs * leaves, points),
        in_specs=[vmem] * 5,
        out_specs=vmem,
        compiler_params=params(16),
        cost_estimate=cost(2000),
        name="finish",
    )(payload, theirs, blocks, expand.reshape(-1, points), acc)
    return out.reshape(rhs, leaf_rows, leaf_cols, points)


def solution(mesh):
    in_specs = (
        P(None, "row", "col", None),
        P(None, "row", "col", None),
        P(None, "row", "col"),
        P("row", "col", None, None),
        P("row", "col", None, None),
        P(None, "row", "col", None, None),
        P(None, "row", "col", None, None),
    )
    out_specs = P(None, "row", "col", None)
    return jax.shard_map(shards, mesh=mesh, in_specs=in_specs, out_specs=out_specs, check_vma=False)
```

```python
import functools

import jax
import jax.numpy as jnp
import numpy as np
from jax import lax
from jax.experimental import pallas as pl
from jax.experimental.pallas import tpu as pltpu
from jax.sharding import PartitionSpec as P

wave_number = 6.0
softening = 0.05
near_scale = 1.0 / 32.0
highest = lax.Precision.HIGHEST
f32, bf16 = jnp.float32, jnp.bfloat16

turns = wave_number / (2.0 * np.pi)
eps_sq = (softening * turns) ** 2
sine = (3.14157435, -5.16695951, 2.54064763, -0.55204997)
b0, b1, b2 = (sine[0] / sine[3], sine[1] / sine[3], sine[2] / sine[3])
half_gain = 1.0 / (2.0 * sine[3] ** 2)
near_gain = -2.0 * sine[3] ** 2 * turns * near_scale

leaf_rows, leaf_cols, points, rank, rhs = 4, 16, 128, 32, 8
leaves = leaf_rows * leaf_cols
edge_leaves = 2 * leaf_cols
side_leaves = 16
edge_rows = (3 + rhs) * leaf_cols
side_rows = 72
group = points // rank
groups = leaves // group
batch = 4
step = 2 * batch
unroll = 2
vmem = pl.BlockSpec(memory_space=pltpu.VMEM)


def params(mib):
    return pltpu.CompilerParams(vmem_limit_bytes=mib << 20)


def cost(cycles):
    return pl.CostEstimate(flops=int(cycles * 400_000), bytes_accessed=1 << 18, transcendentals=0)


class Run:
    def __init__(self, count, skip, source, step, target, offset, both):
        self.count, self.skip, self.source, self.step, self.target = count, skip, source, step, target
        self.offset, self.both = offset, both


def interior_runs():
    across, down = leaf_rows * (leaf_cols - 1), (leaf_rows - 1) * (leaf_cols - 1)
    return [
        Run(leaves, 0, 0, 1, 0, 4, False),
        Run(across, 1, 0, 1, 1, 3, True),
        Run(leaves - leaf_cols, 0, 0, 1, leaf_cols, 1, True),
        Run(down, 1, 0, 1, leaf_cols + 1, 0, True),
        Run(down, 1, 1, 1, leaf_cols, 2, True),
    ]


def edge_runs():
    runs = []
    for first, row, di in ((0, 0, -1), (leaf_cols, leaf_rows - 1, 1)):
        for dj in (-1, 0, 1):
            start = max(0, -dj)
            at = row * leaf_cols + start
            runs.append(Run(leaf_cols - abs(dj), 0, first + start + dj, 1, at, 3 * (di + 1) + dj + 1, False))
    return runs


def side_runs():
    runs = []
    for first, column, dj in ((0, 0, -1), (8, leaf_cols - 1, 1)):
        for di in (-1, 0, 1):
            runs.append(Run(leaf_rows, 0, first + 1 + di, leaf_cols, column, 3 * (di + 1) + dj + 1, False))
    return runs


def cut_runs(runs, first, last):
    pieces, at = [], 0
    for run in runs:
        low, high = max(first - at, 0), min(last - at, run.count)
        if low < high:
            pieces.append((run, low, high))
        at += run.count
    return pieces


zero_row = 9 * leaves


def fields(pieces, at):
    found, begin = None, 0
    for run, low, high in pieces:
        q = at - begin + low
        begin += high - low
        moved = q + (q * 274 >> 12) if run.skip else q
        source, target = moved + run.source, run.step * moved + run.target
        here = [source, target, run.offset * leaves + target, (8 - run.offset) * leaves + source if run.both else zero_row]
        found = here if found is None else [jnp.where(inside_run, old, new) for old, new in zip(found, here)]
        inside_run = at < begin
    idle = [0, 0, zero_row, zero_row]
    return [jnp.where(inside_run, old, new) for old, new in zip(found, idle)]


def split(value):
    high = value.astype(bf16)
    return high, (value - high.astype(f32)).astype(bf16)


def thirds(value):
    high = value.astype(bf16).astype(f32)
    rest = value - high
    middle = rest.astype(bf16).astype(f32)
    return high, middle, rest - middle


def dot(left, right):
    return jnp.dot(left, right, preferred_element_type=f32)


def dot_t(left, right):
    return lax.dot_general(left, right, (((1,), (1,)), ((), ())), preferred_element_type=f32)


def sixteen(leaf):
    return pl.ds(leaf * 16 if isinstance(leaf, int) else pl.multiple_of(leaf * 16, 16), 16)


def fill_tables(count, start, coords, left, right, heights, wides):
    parts = []
    for c in range(3):
        moved = (coords[pl.ds(c * count, count), :] - start[c]) * turns
        if c == 2:
            heights[...] = moved
        else:
            parts.append(thirds(moved))
    k = lax.broadcasted_iota(jnp.int32, (16, points), 0)
    ones_x = jnp.where(k < 3, 1.0, 0.0)
    ones_y = jnp.where((k >= 3) & (k < 6), 1.0, 0.0)
    ones_t = jnp.where((k >= 6) & (k < 9), 1.0, 0.0)
    for role in range(3):
        wide = wides.at[role]
        for leaf in range(count):
            wide[pl.ds(leaf * 16, 16), :] = (ones_t, ones_x, ones_y)[role]
        for first in range(0, count, 8):
            for m in range(3):
                for c in range(2):
                    part = parts[c][m][first : first + 8]
                    if role == 0:
                        wide[pl.ds(first * 16 + 3 * c + m, 8, stride=16), :] = part
                    elif role == c + 1:
                        wide[pl.ds(first * 16 + 6 + m, 8, stride=16), :] = -part
        if role == 0:
            for leaf in range(count):
                left[leaf * points : (leaf + 1) * points, :] = wide[leaf * 16 : leaf * 16 + 16, :].T.astype(bf16)
        else:
            right[:, points * (role - 1) : points * role] = wide[...].astype(bf16)


def lane_block(n):
    return lax.broadcasted_iota(jnp.int32, (rhs, points), 1) // rank == n


def spread_blocks(transfer, blocks):
    same = lax.broadcasted_iota(jnp.int32, (points, points), 0) // rank == lax.broadcasted_iota(jnp.int32, (points, points), 1) // rank
    for n in range(2):
        wide = jnp.concatenate([transfer[n]] * group, axis=1)
        wide = jnp.where(same, jnp.concatenate([wide] * group, axis=0), 0.0)
        blocks[2 * n], blocks[2 * n + 1] = split(wide)


def start_copies(fars, heres, arrived):
    copies = [pltpu.make_async_copy(far, here, arrived.at[n]) for n, (far, here) in enumerate(zip(fars, heres))]
    for copy in copies:
        copy.start()
    return copies


def compress_kernel(coords_far, sources_far, compress_far, halves, payload, coords, sources, compress, arrived):
    copies = start_copies((sources_far, coords_far, compress_far), (sources, coords, compress), arrived)
    copies[0].wait()
    for leaf in range(leaves):
        high, low = split(sources[pl.ds(leaf, rhs, stride=leaves), :])
        halves[sixteen(leaf), :] = jnp.concatenate([high, low], axis=0)
    copies[1].wait()
    odd = lax.axis_index("row") % 2
    for k in range(2):
        row = (leaf_rows - 1) * (1 - odd if k == 0 else odd)
        for c in range(3 + rhs):
            ref, at = (coords, c) if c < 3 else (sources, c - 3)
            to = points + k * edge_rows + c * leaf_cols
            payload[to : to + leaf_cols, :] = ref[pl.ds(pl.multiple_of(at * leaves + row * leaf_cols, 8), leaf_cols), :]
    copies[2].wait()
    for g in range(groups):
        high, low = split(compress[g * points : (g + 1) * points, :])
        got = dot_t(halves[g * 16 * group : (g + 1) * 16 * group, :], jnp.concatenate([high, low], axis=0))
        got = got[:, :points] + got[:, points:]
        total = jnp.zeros((rhs, points), f32)
        for n in range(group):
            total = jnp.where(lane_block(n), got[n * 16 : n * 16 + 8] + got[n * 16 + 8 : n * 16 + 16], total)
        payload[g * rhs : (g + 1) * rhs, :] = total


def prep_kernel(coords, mask, row_transfer, col_transfer, left, right, heights, row_blocks, col_blocks, weights, wides):
    start = [coords[c * leaves : c * leaves + 1, 0:1] for c in range(3)]
    fill_tables(leaves, start, coords, left, right, heights, wides)
    spread_blocks(row_transfer, row_blocks)
    spread_blocks(col_transfer, col_blocks)
    diagonal = lax.broadcasted_iota(jnp.int32, (leaf_cols, leaf_cols), 0) == lax.broadcasted_iota(jnp.int32, (leaf_cols, leaf_cols), 1)
    ones = jnp.ones((leaf_cols, points), bf16)
    for k in range(9):
        for i in range(leaf_rows):
            spread = jnp.where(diagonal, mask[k, i : i + 1, :].astype(f32), 0.0).astype(bf16)
            at = k * leaves + i * leaf_cols
            weights[at : at + leaf_cols, :] = dot(spread, ones)
    weights[zero_row : zero_row + 8, :] = jnp.zeros((8, points), f32)


def halo_tables(count, coords, values, left, right, heights, halves, wides):
    start = [coords[c * leaves : c * leaves + 1, 0:1] for c in range(3)]
    fill_tables(count, start, values, left, right, heights, wides)
    for leaf in range(count):
        high, low = split(values[pl.ds(3 * count + leaf, rhs, stride=count), :])
        halves[sixteen(leaf), :] = jnp.concatenate([high, low], axis=0)


def edges_kernel(coords, edges, left, right, heights, halves, wides):
    halo_tables(edge_leaves, coords, edges, left, right, heights, halves, wides)


def sides_kernel(coords, first, second, third, fourth, left, right, heights, halves, wides, sides):
    col = lax.axis_index("col")
    odd = col % 2 == 1
    inner = (col > 0) & (col < lax.axis_size("col") - 1)
    at = slice(points, points + side_rows)
    near = first[at, :]
    far = jnp.where((col % 8 == 3) | (col % 8 == 4), third[at, :], fourth[at, :])
    far = jnp.where((col % 4 == 1) | (col % 4 == 2), second[at, :], far)
    far = jnp.where(inner, far, 0.0)
    to_left, to_right = jnp.where(odd, near, far), jnp.where(odd, far, near)
    gap = jnp.zeros((2, points), f32)
    for c in range(3 + rhs):
        at = slice(6 * c, 6 * c + 6)
        sides[c * side_leaves : (c + 1) * side_leaves, :] = jnp.concatenate([to_left[at], gap, to_right[at], gap], axis=0)
    halo_tables(side_leaves, coords, sides, left, right, heights, halves, wides)


def level(mine, theirs, blocks):
    total = None
    for value, n in ((mine, 0), (theirs, 2)):
        high, low = split(value)
        got = dot_t(jnp.concatenate([high, low], axis=0), jnp.concatenate([blocks[n], blocks[n + 1]], axis=0))
        got = got[:, :points] + got[:, points:]
        got = got[:points] + got[points:]
        total = got if total is None else total + got
    return total


def level_kernel(forward, mine, theirs, blocks, payload):
    payload[:points, :] = level(mine[:points, :], theirs[:points, :], blocks)
    payload[points:, :] = theirs[forward:, :]


def turn_kernel(mine, theirs, blocks, coords, sources, first, second, payload, edges):
    payload[:points, :] = level(mine[:points, :], theirs[:points, :], blocks)
    row, col = lax.axis_index("row"), lax.axis_index("col")
    odd = row % 2 == 1
    around = (row % 4 == 1) | (row % 4 == 2)
    inner = (row > 0) & (row < lax.axis_size("row") - 1)
    for c in range(3 + rhs):
        at = slice(points + c * leaf_cols, points + (c + 1) * leaf_cols)
        near = first[at, :]
        far = jnp.where(inner, jnp.where(around, second[at, :], theirs[at, :]), 0.0)
        edges[c * edge_leaves : c * edge_leaves + leaf_cols, :] = jnp.where(odd, near, far)
        edges[c * edge_leaves + leaf_cols : (c + 1) * edge_leaves, :] = jnp.where(odd, far, near)
    for k in range(2):
        j = (leaf_cols - 1) * (1 - col % 2 if k == 0 else col % 2)
        base = points + k * side_rows
        for c in range(3 + rhs):
            ref, at = (coords, c) if c < 3 else (sources, c - 3)
            payload[base + 6 * c : base + 6 * c + 1, :] = edges[pl.ds(c * edge_leaves + j, 1), :]
            for i in range(leaf_rows):
                payload[base + 6 * c + 1 + i : base + 6 * c + 2 + i, :] = ref[pl.ds(at * leaves + i * leaf_cols + j, 1), :]
            payload[base + 6 * c + 5 : base + 6 * c + 6, :] = edges[pl.ds(c * edge_leaves + leaf_cols + j, 1), :]
        payload[base + 66 : base + side_rows, :] = jnp.zeros((side_rows - 66, points), f32)


def near_kernel(pieces, pairs, both_ways, weights, left, source_heights, source_halves, right, heights, halves, seed, acc, gap_a, gap_b, splat_a, splat_b, kern_a, kern_b):
    acc[...] = seed[...]
    kern_b[...] = jnp.zeros_like(kern_b)
    buffers_a, buffers_b = (gap_a, splat_a, kern_a), (gap_b, splat_b, kern_b)

    def subtract(item, n, gap, splat):
        source, target = item[:2]
        gap[n] = dot(left[pl.ds(pl.multiple_of(source * points, points), points), :], right[sixteen(target), :])
        splat[n] = jnp.broadcast_to(source_heights[pl.ds(source, 1), :], (points, points)).T

    def evaluate(item, n, gap, splat, kern):
        height = heights[pl.ds(item[1], 1), :]
        for g in range(points // 32):
            at_rows = slice(32 * g, 32 * g + 32)
            dx, dy, dz = gap[n, at_rows, :points], gap[n, at_rows, points:], splat[n, at_rows] - height
            distance_sq = dx * dx + dy * dy + dz * dz
            safe = jnp.maximum(distance_sq, 1e-30)
            turn = safe * lax.rsqrt(safe)
            f = turn - jnp.round(turn)
            u = f * f
            m = f * (((u + b2) * u + b1) * u + b0)
            value = (m * m - half_gain) * lax.rsqrt(distance_sq + eps_sq)
            high, low = split(value)
            kern[n, 0, at_rows] = high
            kern[n, 1, at_rows] = low

    def apply(item, n, kern):
        source, target, target_weight, source_weight = item
        pair = jnp.concatenate([kern[n, 0], kern[n, 1]], axis=1)
        got = dot(source_halves[sixteen(source), :], pair)
        got = got[:, :points] + got[:, points:]
        acc[pl.ds(target * 8, 8), :] += (got[:8] + got[8:]) * weights[pl.ds(target_weight, 1), :]
        if both_ways:
            mine = halves[sixteen(target), :]
            got = dot_t(jnp.concatenate([mine, mine], axis=1), pair)
            acc[pl.ds(source * 8, 8), :] += (got[:8] + got[8:]) * weights[pl.ds(source_weight, 1), :]

    def items_at(at):
        return [fields(pieces, at + n) for n in range(batch)]

    def stage(at, earlier, now, here, there):
        later = items_at(at + batch)
        for n in range(batch):
            apply(earlier[n], n, there[2])
        for n in range(batch):
            subtract(later[n], n, *there[:2])
        for n in range(batch):
            evaluate(now[n], n, *here)
        return now, later

    def pair(at, carry):
        carry = stage(at, *carry, buffers_a, buffers_b)
        return stage(at + batch, *carry, buffers_b, buffers_a)

    def body(trip, carry):
        for k in range(unroll):
            carry = pair(trip * step * unroll + k * step, carry)
        return carry

    first = items_at(jnp.int32(0))
    for n in range(batch):
        subtract(first[n], n, *buffers_a[:2])
    nothing = [[jnp.int32(0), jnp.int32(0), jnp.int32(zero_row), jnp.int32(zero_row)]] * batch
    carry = lax.fori_loop(0, pairs // unroll, body, (nothing, first))
    for k in range(pairs // unroll * unroll, pairs):
        carry = pair(jnp.int32(k * step), carry)
    last = carry[0]
    for n in range(batch):
        apply(last[n], n, buffers_b[2])


def near_piece(pieces, both_ways, weights, source_tables, target_tables, seed):
    count = sum(high - low for _, low, high in pieces)
    pairs = -(-count // step)
    left, _, source_heights, source_halves = source_tables
    _, right, heights, halves = target_tables
    return pl.pallas_call(
        functools.partial(near_kernel, pieces, pairs, both_ways),
        out_shape=jax.ShapeDtypeStruct(seed.shape, f32),
        in_specs=[vmem] * 8,
        out_specs=vmem,
        scratch_shapes=[
            shape
            for shape in (
                pltpu.VMEM((batch, points, 2 * points), f32),
                pltpu.VMEM((batch, points, points), f32),
                pltpu.VMEM((batch, 2, points, points), bf16),
            )
            for _ in range(2)
        ],
        compiler_params=params(16),
        cost_estimate=cost(count * 110),
        name="near",
    )(weights, left, source_heights, source_halves, right, heights, halves, seed)


def finish_kernel(mine, theirs, blocks, expand, acc, out):
    coeffs = level(mine[:points, :], theirs[:points, :], blocks)
    for g in range(groups):
        here = coeffs[g * rhs : (g + 1) * rhs]
        rows = jnp.concatenate([jnp.where(lane_block(n), here, 0.0) for n in range(group)], axis=0)
        high, low = split(rows)
        e_high, e_low = split(expand[g * points : (g + 1) * points, :])
        got = dot(jnp.concatenate([high, low], axis=0), jnp.concatenate([e_high, e_low], axis=1))
        got = got[:, :points] + got[:, points:]
        got = got[: group * rhs] + got[group * rhs :]
        for n in range(group):
            leaf = g * group + n
            near = acc[leaf * rhs : (leaf + 1) * rhs, :] * near_gain
            out[pl.ds(leaf, rhs, stride=leaves), :] = near + got[n * rhs : (n + 1) * rhs]


def table_shapes(count):
    return (
        jax.ShapeDtypeStruct((count * points, 16), bf16),
        jax.ShapeDtypeStruct((count * 16, 2 * points), bf16),
        jax.ShapeDtypeStruct((count, points), f32),
        jax.ShapeDtypeStruct((count * 16, points), bf16),
    )


def partner_of(block, axis, distance):
    route = [(i, i ^ (1 << distance)) for i in range(lax.axis_size(axis))]
    return lax.ppermute(block, axis, route)


def array(*shape):
    return jax.ShapeDtypeStruct(shape, f32)


def small_call(body, name, out_shape, *operands):
    single = not isinstance(out_shape, tuple)
    return pl.pallas_call(
        body,
        out_shape=out_shape,
        in_specs=[vmem] * len(operands),
        out_specs=vmem if single else (vmem,) * len(out_shape),
        compiler_params=params(16),
        cost_estimate=cost(600),
        name=name,
    )(*operands)


def far_call(body, name, out_shape, scratch, *operands):
    return pl.pallas_call(
        body,
        out_shape=out_shape,
        in_specs=[pl.BlockSpec(memory_space=pltpu.HBM)] * len(operands),
        out_specs=(vmem,) * len(out_shape),
        scratch_shapes=scratch + [pltpu.SemaphoreType.DMA((len(operands),))],
        compiler_params=params(24),
        cost_estimate=cost(2000),
        name=name,
    )(*[pltpu.with_memory_space_constraint(operand, pltpu.HBM) for operand in operands])


def tables_call(body, name, count, scratch, *operands):
    return pl.pallas_call(
        body,
        out_shape=table_shapes(count),
        in_specs=[vmem] * len(operands),
        out_specs=(vmem,) * 4,
        scratch_shapes=[pltpu.VMEM((3, count * 16, points), f32)] + scratch,
        compiler_params=params(16),
        cost_estimate=cost(1000),
        name=name,
    )(*operands)


def shards(coords, sources, neighbour_mask, compress, expand, row_transfer, col_transfer):
    coords = coords.reshape(-1, points)
    sources = sources.reshape(-1, points)
    halves, payload = far_call(
        compress_kernel,
        "compress",
        (table_shapes(leaves)[3], array(points + 2 * edge_rows, points)),
        [pltpu.VMEM(shape, f32) for shape in ((3 * leaves, points), (rhs * leaves, points), (leaves * rank, points))],
        coords, sources, compress.reshape(-1, points),
    )
    row_bits, col_bits = (lax.axis_size(axis).bit_length() - 1 for axis in ("row", "col"))
    axes = ["row"] * row_bits + ["col"] * col_bits
    bits = [*range(row_bits), *range(col_bits)]
    theirs = partner_of(payload, "row", 0)
    block_shape = jax.ShapeDtypeStruct((4, points, points), bf16)
    coords_later, payload = lax.optimization_barrier((coords, payload))
    left, right, heights, row_blocks, col_blocks, weights = pl.pallas_call(
        prep_kernel,
        out_shape=table_shapes(leaves)[:3] + (block_shape, block_shape, array(zero_row + 8, points)),
        in_specs=[vmem] * 4,
        out_specs=(vmem,) * 6,
        scratch_shapes=[pltpu.VMEM((3, leaves * 16, points), f32)],
        compiler_params=params(16),
        cost_estimate=cost(2000),
        name="prep",
    )(coords_later, neighbour_mask, row_transfer[:, 0, 0], col_transfer[:, 0, 0])
    own = left, right, heights, halves
    inner, edge, side = interior_runs(), edge_runs(), side_runs()
    counts = [sum(run.count for run in runs) for runs in (inner, edge, side)]
    windows = row_bits + col_bits - 1
    edge_windows = (row_bits, row_bits + 2)
    inner_windows = [n for n in range(1, windows + 1) if n not in edge_windows]
    cuts = [counts[0] * k // len(inner_windows) // step * step for k in range(len(inner_windows))] + [counts[0]]
    half = -(-counts[1] // 2 // step) * step
    acc = jnp.zeros((leaves * rhs, points), f32)
    received = [theirs]
    for n, (axis, bit) in enumerate(zip(axes, bits)):
        blocks = row_blocks if axis == "row" else col_blocks
        if n > 0:
            theirs = partner_of(payload, axis, bit)
            payload, acc = lax.optimization_barrier((payload, acc))
            if n == row_bits:
                edges, acc = lax.optimization_barrier((edges, acc))
                edge_tables = tables_call(edges_kernel, "edges", edge_leaves, [], coords, edges)
            if n in edge_windows:
                some = cut_runs(edge, 0, half) if n == row_bits else cut_runs(edge, half, counts[1])
                acc = near_piece(some, False, weights, edge_tables, own, acc)
            else:
                k = inner_windows.index(n)
                acc = near_piece(cut_runs(inner, cuts[k], cuts[k + 1]), True, weights, own, own, acc)
            theirs, acc = lax.optimization_barrier((theirs, acc))
            received.append(theirs)
        if n == row_bits - 1:
            payload, edges = small_call(
                turn_kernel,
                "turn",
                (array(points + 2 * side_rows, points), array((3 + rhs) * edge_leaves, points)),
                payload, theirs, blocks, coords, sources, received[0], received[1],
            )
        elif n < windows:
            rows = edge_rows if axis == "row" else side_rows
            skip = points + rows if bit == 0 else points
            payload = small_call(functools.partial(level_kernel, skip), "level", array(points + rows, points), payload, theirs, blocks)
    side_tables = tables_call(sides_kernel, "sides", side_leaves, [pltpu.VMEM(((3 + rhs) * side_leaves, points), f32)], coords, *received[row_bits:])
    acc = near_piece(cut_runs(side, 0, counts[2]), False, weights, side_tables, own, acc)
    out = pl.pallas_call(
        finish_kernel,
        out_shape=array(rhs * leaves, points),
        in_specs=[vmem] * 5,
        out_specs=vmem,
        compiler_params=params(16),
        cost_estimate=cost(2000),
        name="finish",
    )(payload, theirs, blocks, expand.reshape(-1, points), acc)
    return out.reshape(rhs, leaf_rows, leaf_cols, points)


def solution(mesh):
    in_specs = (
        P(None, "row", "col", None),
        P(None, "row", "col", None),
        P(None, "row", "col"),
        P("row", "col", None, None),
        P("row", "col", None, None),
        P(None, "row", "col", None, None),
        P(None, "row", "col", None, None),
    )
    out_specs = P(None, "row", "col", None)
    return jax.shard_map(shards, mesh=mesh, in_specs=in_specs, out_specs=out_specs, check_vma=False)
```

```python
import functools

import jax
import jax.numpy as jnp
import numpy as np
from jax import lax
from jax.experimental import pallas as pl
from jax.experimental.pallas import tpu as pltpu
from jax.sharding import PartitionSpec as P

wave_number = 6.0
softening = 0.05
near_scale = 1.0 / 32.0
highest = lax.Precision.HIGHEST
f32, bf16 = jnp.float32, jnp.bfloat16

turns = wave_number / (2.0 * np.pi)
eps_sq = (softening * turns) ** 2
sine = (3.14157435, -5.16695951, 2.54064763, -0.55204997)
b0, b1, b2 = (sine[0] / sine[3], sine[1] / sine[3], sine[2] / sine[3])
half_gain = 1.0 / (2.0 * sine[3] ** 2)
near_gain = -2.0 * sine[3] ** 2 * turns * near_scale

leaf_rows, leaf_cols, points, rank, rhs = 4, 16, 128, 32, 8
leaves = leaf_rows * leaf_cols
edge_leaves = 2 * leaf_cols
side_leaves = 16
edge_rows = (3 + rhs) * leaf_cols
side_rows = 72
group = points // rank
groups = leaves // group
ring = 2
vmem = pl.BlockSpec(memory_space=pltpu.VMEM)


def params(mib):
    return pltpu.CompilerParams(vmem_limit_bytes=mib << 20)


def cost(cycles):
    return pl.CostEstimate(flops=int(cycles * 400_000), bytes_accessed=1 << 18, transcendentals=0)


class Run:
    def __init__(self, count, skip, source, step, target, offset, both):
        self.count, self.skip, self.source, self.step, self.target = count, skip, source, step, target
        self.offset, self.both = offset, both


def interior_runs():
    across, down = leaf_rows * (leaf_cols - 1), (leaf_rows - 1) * (leaf_cols - 1)
    return [
        Run(leaves, 0, 0, 1, 0, 4, False),
        Run(across, 1, 0, 1, 1, 3, True),
        Run(leaves - leaf_cols, 0, 0, 1, leaf_cols, 1, True),
        Run(down, 1, 0, 1, leaf_cols + 1, 0, True),
        Run(down, 1, 1, 1, leaf_cols, 2, True),
    ]


def edge_runs():
    runs = []
    for first, row, di in ((0, 0, -1), (leaf_cols, leaf_rows - 1, 1)):
        for dj in (-1, 0, 1):
            start = max(0, -dj)
            at = row * leaf_cols + start
            runs.append(Run(leaf_cols - abs(dj), 0, first + start + dj, 1, at, 3 * (di + 1) + dj + 1, False))
    return runs


def side_runs():
    runs = []
    for first, column, dj in ((0, 0, -1), (8, leaf_cols - 1, 1)):
        for di in (-1, 0, 1):
            runs.append(Run(leaf_rows, 0, first + 1 + di, leaf_cols, column, 3 * (di + 1) + dj + 1, False))
    return runs


def cut_runs(runs, first, last):
    pieces, at = [], 0
    for run in runs:
        low, high = max(first - at, 0), min(last - at, run.count)
        if low < high:
            pieces.append((run, low, high))
        at += run.count
    return pieces


zero_row = 9 * leaves


def listed(pieces):
    items = []
    for run, low, high in pieces:
        for q in range(low, high):
            moved = q + run.skip * (q // (leaf_cols - 1))
            source, target = moved + run.source, run.step * moved + run.target
            back = (8 - run.offset) * leaves + source if run.both else None
            items.append((source, target, run.offset * leaves + target, back))
    return items


def split(value):
    high = value.astype(bf16)
    return high, (value - high.astype(f32)).astype(bf16)


def thirds(value):
    high = value.astype(bf16).astype(f32)
    rest = value - high
    middle = rest.astype(bf16).astype(f32)
    return high, middle, rest - middle


def dot(left, right):
    return jnp.dot(left, right, preferred_element_type=f32)


def dot_t(left, right):
    return lax.dot_general(left, right, (((1,), (1,)), ((), ())), preferred_element_type=f32)


def sixteen(leaf):
    return pl.ds(leaf * 16 if isinstance(leaf, int) else pl.multiple_of(leaf * 16, 16), 16)


def fill_tables(count, start, coords, left, right, heights, wides):
    parts = []
    for c in range(3):
        moved = (coords[pl.ds(c * count, count), :] - start[c]) * turns
        if c == 2:
            heights[...] = moved
        else:
            parts.append(thirds(moved))
    k = lax.broadcasted_iota(jnp.int32, (16, points), 0)
    ones_x = jnp.where(k < 3, 1.0, 0.0)
    ones_y = jnp.where((k >= 3) & (k < 6), 1.0, 0.0)
    ones_t = jnp.where((k >= 6) & (k < 9), 1.0, 0.0)
    for role in range(3):
        wide = wides.at[role]
        for leaf in range(count):
            wide[pl.ds(leaf * 16, 16), :] = (ones_t, ones_x, ones_y)[role]
        for first in range(0, count, 8):
            for m in range(3):
                for c in range(2):
                    part = parts[c][m][first : first + 8]
                    if role == 0:
                        wide[pl.ds(first * 16 + 3 * c + m, 8, stride=16), :] = part
                    elif role == c + 1:
                        wide[pl.ds(first * 16 + 6 + m, 8, stride=16), :] = -part
        if role == 0:
            for leaf in range(count):
                left[leaf * points : (leaf + 1) * points, :] = wide[leaf * 16 : leaf * 16 + 16, :].T.astype(bf16)
        else:
            right[:, points * (role - 1) : points * role] = wide[...].astype(bf16)


def lane_block(n):
    return lax.broadcasted_iota(jnp.int32, (rhs, points), 1) // rank == n


def spread_blocks(transfer, blocks):
    same = lax.broadcasted_iota(jnp.int32, (points, points), 0) // rank == lax.broadcasted_iota(jnp.int32, (points, points), 1) // rank
    for n in range(2):
        wide = jnp.concatenate([transfer[n]] * group, axis=1)
        wide = jnp.where(same, jnp.concatenate([wide] * group, axis=0), 0.0)
        blocks[2 * n], blocks[2 * n + 1] = split(wide)


def start_copies(fars, heres, arrived):
    copies = [pltpu.make_async_copy(far, here, arrived.at[n]) for n, (far, here) in enumerate(zip(fars, heres))]
    for copy in copies:
        copy.start()
    return copies


def compress_kernel(coords_far, sources_far, compress_far, halves, payload, coords, sources, compress, arrived):
    copies = start_copies((sources_far, coords_far, compress_far), (sources, coords, compress), arrived)
    copies[0].wait()
    for leaf in range(leaves):
        high, low = split(sources[pl.ds(leaf, rhs, stride=leaves), :])
        halves[sixteen(leaf), :] = jnp.concatenate([high, low], axis=0)
    copies[1].wait()
    odd = lax.axis_index("row") % 2
    for k in range(2):
        row = (leaf_rows - 1) * (1 - odd if k == 0 else odd)
        for c in range(3 + rhs):
            ref, at = (coords, c) if c < 3 else (sources, c - 3)
            to = points + k * edge_rows + c * leaf_cols
            payload[to : to + leaf_cols, :] = ref[pl.ds(pl.multiple_of(at * leaves + row * leaf_cols, 8), leaf_cols), :]
    copies[2].wait()
    for g in range(groups):
        high, low = split(compress[g * points : (g + 1) * points, :])
        got = dot_t(halves[g * 16 * group : (g + 1) * 16 * group, :], jnp.concatenate([high, low], axis=0))
        got = got[:, :points] + got[:, points:]
        total = jnp.zeros((rhs, points), f32)
        for n in range(group):
            total = jnp.where(lane_block(n), got[n * 16 : n * 16 + 8] + got[n * 16 + 8 : n * 16 + 16], total)
        payload[g * rhs : (g + 1) * rhs, :] = total


def prep_kernel(coords, mask, row_transfer, col_transfer, left, right, heights, row_blocks, col_blocks, weights, wides):
    start = [coords[c * leaves : c * leaves + 1, 0:1] for c in range(3)]
    fill_tables(leaves, start, coords, left, right, heights, wides)
    spread_blocks(row_transfer, row_blocks)
    spread_blocks(col_transfer, col_blocks)
    diagonal = lax.broadcasted_iota(jnp.int32, (leaf_cols, leaf_cols), 0) == lax.broadcasted_iota(jnp.int32, (leaf_cols, leaf_cols), 1)
    ones = jnp.ones((leaf_cols, points), bf16)
    for k in range(9):
        for i in range(leaf_rows):
            spread = jnp.where(diagonal, mask[k, i : i + 1, :].astype(f32), 0.0).astype(bf16)
            at = k * leaves + i * leaf_cols
            weights[at : at + leaf_cols, :] = dot(spread, ones)
    weights[zero_row : zero_row + 8, :] = jnp.zeros((8, points), f32)


def halo_tables(count, coords, values, left, right, heights, halves, wides):
    start = [coords[c * leaves : c * leaves + 1, 0:1] for c in range(3)]
    fill_tables(count, start, values, left, right, heights, wides)
    for leaf in range(count):
        high, low = split(values[pl.ds(3 * count + leaf, rhs, stride=count), :])
        halves[sixteen(leaf), :] = jnp.concatenate([high, low], axis=0)


def edges_kernel(coords, edges, left, right, heights, halves, wides):
    halo_tables(edge_leaves, coords, edges, left, right, heights, halves, wides)


def sides_kernel(coords, first, second, third, fourth, left, right, heights, halves, wides, sides):
    col = lax.axis_index("col")
    odd = col % 2 == 1
    inner = (col > 0) & (col < lax.axis_size("col") - 1)
    at = slice(points, points + side_rows)
    near = first[at, :]
    far = jnp.where((col % 8 == 3) | (col % 8 == 4), third[at, :], fourth[at, :])
    far = jnp.where((col % 4 == 1) | (col % 4 == 2), second[at, :], far)
    far = jnp.where(inner, far, 0.0)
    to_left, to_right = jnp.where(odd, near, far), jnp.where(odd, far, near)
    gap = jnp.zeros((2, points), f32)
    for c in range(3 + rhs):
        at = slice(6 * c, 6 * c + 6)
        sides[c * side_leaves : (c + 1) * side_leaves, :] = jnp.concatenate([to_left[at], gap, to_right[at], gap], axis=0)
    halo_tables(side_leaves, coords, sides, left, right, heights, halves, wides)


def level(mine, theirs, blocks):
    total = None
    for value, n in ((mine, 0), (theirs, 2)):
        high, low = split(value)
        got = dot_t(jnp.concatenate([high, low], axis=0), jnp.concatenate([blocks[n], blocks[n + 1]], axis=0))
        got = got[:, :points] + got[:, points:]
        got = got[:points] + got[points:]
        total = got if total is None else total + got
    return total


def level_kernel(forward, mine, theirs, blocks, payload):
    payload[:points, :] = level(mine[:points, :], theirs[:points, :], blocks)
    payload[points:, :] = theirs[forward:, :]


def turn_kernel(mine, theirs, blocks, coords, sources, first, second, payload, edges):
    payload[:points, :] = level(mine[:points, :], theirs[:points, :], blocks)
    row, col = lax.axis_index("row"), lax.axis_index("col")
    odd = row % 2 == 1
    around = (row % 4 == 1) | (row % 4 == 2)
    inner = (row > 0) & (row < lax.axis_size("row") - 1)
    for c in range(3 + rhs):
        at = slice(points + c * leaf_cols, points + (c + 1) * leaf_cols)
        near = first[at, :]
        far = jnp.where(inner, jnp.where(around, second[at, :], theirs[at, :]), 0.0)
        edges[c * edge_leaves : c * edge_leaves + leaf_cols, :] = jnp.where(odd, near, far)
        edges[c * edge_leaves + leaf_cols : (c + 1) * edge_leaves, :] = jnp.where(odd, far, near)
    for k in range(2):
        j = (leaf_cols - 1) * (1 - col % 2 if k == 0 else col % 2)
        base = points + k * side_rows
        for c in range(3 + rhs):
            ref, at = (coords, c) if c < 3 else (sources, c - 3)
            payload[base + 6 * c : base + 6 * c + 1, :] = edges[pl.ds(c * edge_leaves + j, 1), :]
            for i in range(leaf_rows):
                payload[base + 6 * c + 1 + i : base + 6 * c + 2 + i, :] = ref[pl.ds(at * leaves + i * leaf_cols + j, 1), :]
            payload[base + 6 * c + 5 : base + 6 * c + 6, :] = edges[pl.ds(c * edge_leaves + leaf_cols + j, 1), :]
        payload[base + 66 : base + side_rows, :] = jnp.zeros((side_rows - 66, points), f32)


def near_kernel(items, batch, weights, left, source_heights, source_halves, right, heights, halves, seed, acc, gaps, splats, kerns):
    acc[...] = seed[...]

    def subtract(item, n, gap, splat):
        source, target = item[:2]
        gap[n] = dot(left[source * points : (source + 1) * points, :], right[sixteen(target), :])
        splat[n] = jnp.broadcast_to(source_heights[source : source + 1, :], (points, points)).T

    def evaluate(item, n, gap, splat, kern):
        height = heights[item[1] : item[1] + 1, :]
        for g in range(points // 32):
            at_rows = slice(32 * g, 32 * g + 32)
            dx, dy, dz = gap[n, at_rows, :points], gap[n, at_rows, points:], splat[n, at_rows] - height
            distance_sq = dx * dx + dy * dy + dz * dz
            safe = jnp.maximum(distance_sq, 1e-30)
            turn = safe * lax.rsqrt(safe)
            f = turn - jnp.round(turn)
            u = f * f
            m = f * (((u + b2) * u + b1) * u + b0)
            value = (m * m - half_gain) * lax.rsqrt(distance_sq + eps_sq)
            high, low = split(value)
            kern[n, 0, at_rows] = high
            kern[n, 1, at_rows] = low

    def receive(leaf, weight, got):
        at = slice(leaf * rhs, (leaf + 1) * rhs)
        acc[at, :] += (got[:rhs] + got[rhs:]) * weights[weight : weight + 1, :]

    def apply(item, n, kern):
        source, target, weight, back = item
        pair = jnp.concatenate([kern[n, 0], kern[n, 1]], axis=1)
        got = dot(source_halves[sixteen(source), :], pair)
        receive(target, weight, got[:, :points] + got[:, points:])
        if back is not None:
            mine = halves[sixteen(target), :]
            receive(source, back, dot_t(jnp.concatenate([mine, mine], axis=1), pair))

    stages = [items[at : at + batch] for at in range(0, len(items), batch)]
    for k in range(-1, len(stages) + 1):
        if k >= 1:
            for n, item in enumerate(stages[k - 1]):
                apply(item, n, kerns.at[(k - 1) % ring])
        if k + 1 < len(stages):
            for n, item in enumerate(stages[k + 1]):
                subtract(item, n, gaps.at[(k + 1) % ring], splats.at[(k + 1) % ring])
        if 0 <= k < len(stages):
            for n, item in enumerate(stages[k]):
                evaluate(item, n, gaps.at[k % ring], splats.at[k % ring], kerns.at[k % ring])


def near_piece(pieces, weights, source_tables, target_tables, seed):
    items = listed(pieces)
    batch = 4 if any(item[3] is not None for item in items) else 8
    left, _, source_heights, source_halves = source_tables
    _, right, heights, halves = target_tables
    return pl.pallas_call(
        functools.partial(near_kernel, items, batch),
        out_shape=jax.ShapeDtypeStruct(seed.shape, f32),
        in_specs=[vmem] * 8,
        out_specs=vmem,
        scratch_shapes=[
            pltpu.VMEM((ring, batch, points, 2 * points), f32),
            pltpu.VMEM((ring, batch, points, points), f32),
            pltpu.VMEM((ring, batch, 2, points, points), bf16),
        ],
        compiler_params=params(24),
        cost_estimate=cost(len(items) * 110),
        name="near",
    )(weights, left, source_heights, source_halves, right, heights, halves, seed)


def finish_kernel(mine, theirs, blocks, expand, acc, out):
    coeffs = level(mine[:points, :], theirs[:points, :], blocks)
    for g in range(groups):
        here = coeffs[g * rhs : (g + 1) * rhs]
        rows = jnp.concatenate([jnp.where(lane_block(n), here, 0.0) for n in range(group)], axis=0)
        high, low = split(rows)
        e_high, e_low = split(expand[g * points : (g + 1) * points, :])
        got = dot(jnp.concatenate([high, low], axis=0), jnp.concatenate([e_high, e_low], axis=1))
        got = got[:, :points] + got[:, points:]
        got = got[: group * rhs] + got[group * rhs :]
        for n in range(group):
            leaf = g * group + n
            near = acc[leaf * rhs : (leaf + 1) * rhs, :] * near_gain
            out[pl.ds(leaf, rhs, stride=leaves), :] = near + got[n * rhs : (n + 1) * rhs]


def table_shapes(count):
    return (
        jax.ShapeDtypeStruct((count * points, 16), bf16),
        jax.ShapeDtypeStruct((count * 16, 2 * points), bf16),
        jax.ShapeDtypeStruct((count, points), f32),
        jax.ShapeDtypeStruct((count * 16, points), bf16),
    )


def partner_of(block, axis, distance):
    route = [(i, i ^ (1 << distance)) for i in range(lax.axis_size(axis))]
    return lax.ppermute(block, axis, route)


def array(*shape):
    return jax.ShapeDtypeStruct(shape, f32)


def small_call(body, name, out_shape, *operands):
    single = not isinstance(out_shape, tuple)
    return pl.pallas_call(
        body,
        out_shape=out_shape,
        in_specs=[vmem] * len(operands),
        out_specs=vmem if single else (vmem,) * len(out_shape),
        compiler_params=params(16),
        cost_estimate=cost(600),
        name=name,
    )(*operands)


def far_call(body, name, out_shape, scratch, *operands):
    return pl.pallas_call(
        body,
        out_shape=out_shape,
        in_specs=[pl.BlockSpec(memory_space=pltpu.HBM)] * len(operands),
        out_specs=(vmem,) * len(out_shape),
        scratch_shapes=scratch + [pltpu.SemaphoreType.DMA((len(operands),))],
        compiler_params=params(24),
        cost_estimate=cost(2000),
        name=name,
    )(*[pltpu.with_memory_space_constraint(operand, pltpu.HBM) for operand in operands])


def tables_call(body, name, count, scratch, *operands):
    return pl.pallas_call(
        body,
        out_shape=table_shapes(count),
        in_specs=[vmem] * len(operands),
        out_specs=(vmem,) * 4,
        scratch_shapes=[pltpu.VMEM((3, count * 16, points), f32)] + scratch,
        compiler_params=params(16),
        cost_estimate=cost(1000),
        name=name,
    )(*operands)


def shards(coords, sources, neighbour_mask, compress, expand, row_transfer, col_transfer):
    coords = coords.reshape(-1, points)
    sources = sources.reshape(-1, points)
    halves, payload = far_call(
        compress_kernel,
        "compress",
        (table_shapes(leaves)[3], array(points + 2 * edge_rows, points)),
        [pltpu.VMEM(shape, f32) for shape in ((3 * leaves, points), (rhs * leaves, points), (leaves * rank, points))],
        coords, sources, compress.reshape(-1, points),
    )
    row_bits, col_bits = (lax.axis_size(axis).bit_length() - 1 for axis in ("row", "col"))
    axes = ["row"] * row_bits + ["col"] * col_bits
    bits = [*range(row_bits), *range(col_bits)]
    theirs = partner_of(payload, "row", 0)
    block_shape = jax.ShapeDtypeStruct((4, points, points), bf16)
    coords_later, payload = lax.optimization_barrier((coords, payload))
    left, right, heights, row_blocks, col_blocks, weights = pl.pallas_call(
        prep_kernel,
        out_shape=table_shapes(leaves)[:3] + (block_shape, block_shape, array(zero_row + 8, points)),
        in_specs=[vmem] * 4,
        out_specs=(vmem,) * 6,
        scratch_shapes=[pltpu.VMEM((3, leaves * 16, points), f32)],
        compiler_params=params(16),
        cost_estimate=cost(2000),
        name="prep",
    )(coords_later, neighbour_mask, row_transfer[:, 0, 0], col_transfer[:, 0, 0])
    own = left, right, heights, halves
    inner, edge, side = interior_runs(), edge_runs(), side_runs()
    counts = [sum(run.count for run in runs) for runs in (inner, edge, side)]
    windows = row_bits + col_bits - 1
    edge_windows = (row_bits, row_bits + 2)
    inner_windows = [n for n in range(1, windows + 1) if n not in edge_windows]
    cuts = [counts[0] * k // len(inner_windows) // 4 * 4 for k in range(len(inner_windows))] + [counts[0]]
    half = -(-counts[1] // 2 // 8) * 8
    acc = jnp.zeros((leaves * rhs, points), f32)
    received = [theirs]
    for n, (axis, bit) in enumerate(zip(axes, bits)):
        blocks = row_blocks if axis == "row" else col_blocks
        if n > 0:
            theirs = partner_of(payload, axis, bit)
            payload, acc = lax.optimization_barrier((payload, acc))
            if n == row_bits:
                edges, acc = lax.optimization_barrier((edges, acc))
                edge_tables = tables_call(edges_kernel, "edges", edge_leaves, [], coords, edges)
            if n in edge_windows:
                some = cut_runs(edge, 0, half) if n == row_bits else cut_runs(edge, half, counts[1])
                acc = near_piece(some, weights, edge_tables, own, acc)
            else:
                k = inner_windows.index(n)
                acc = near_piece(cut_runs(inner, cuts[k], cuts[k + 1]), weights, own, own, acc)
            theirs, acc = lax.optimization_barrier((theirs, acc))
            received.append(theirs)
        if n == row_bits - 1:
            payload, edges = small_call(
                turn_kernel,
                "turn",
                (array(points + 2 * side_rows, points), array((3 + rhs) * edge_leaves, points)),
                payload, theirs, blocks, coords, sources, received[0], received[1],
            )
        elif n < windows:
            rows = edge_rows if axis == "row" else side_rows
            skip = points + rows if bit == 0 else points
            payload = small_call(functools.partial(level_kernel, skip), "level", array(points + rows, points), payload, theirs, blocks)
    side_tables = tables_call(sides_kernel, "sides", side_leaves, [pltpu.VMEM(((3 + rhs) * side_leaves, points), f32)], coords, *received[row_bits:])
    acc = near_piece(cut_runs(side, 0, counts[2]), weights, side_tables, own, acc)
    out = pl.pallas_call(
        finish_kernel,
        out_shape=array(rhs * leaves, points),
        in_specs=[vmem] * 5,
        out_specs=vmem,
        compiler_params=params(16),
        cost_estimate=cost(2000),
        name="finish",
    )(payload, theirs, blocks, expand.reshape(-1, points), acc)
    return out.reshape(rhs, leaf_rows, leaf_cols, points)


def solution(mesh):
    in_specs = (
        P(None, "row", "col", None),
        P(None, "row", "col", None),
        P(None, "row", "col"),
        P("row", "col", None, None),
        P("row", "col", None, None),
        P(None, "row", "col", None, None),
        P(None, "row", "col", None, None),
    )
    out_specs = P(None, "row", "col", None)
    return jax.shard_map(shards, mesh=mesh, in_specs=in_specs, out_specs=out_specs, check_vma=False)
```

```python
import functools

import jax
import jax.numpy as jnp
import numpy as np
from jax import lax
from jax.experimental import pallas as pl
from jax.experimental.pallas import tpu as pltpu
from jax.sharding import PartitionSpec as P

wave_number = 6.0
softening = 0.05
near_scale = 1.0 / 32.0
highest = lax.Precision.HIGHEST
f32, bf16 = jnp.float32, jnp.bfloat16

turns = wave_number / (2.0 * np.pi)
eps_sq = (softening * turns) ** 2
sine = (3.14157435, -5.16695951, 2.54064763, -0.55204997)
b0, b1, b2 = (sine[0] / sine[3], sine[1] / sine[3], sine[2] / sine[3])
half_gain = 1.0 / (2.0 * sine[3] ** 2)
near_gain = -2.0 * sine[3] ** 2 * turns * near_scale

leaf_rows, leaf_cols, points, rank, rhs = 4, 16, 128, 32, 8
leaves = leaf_rows * leaf_cols
edge_leaves = 2 * leaf_cols
side_leaves = 16
edge_rows = (3 + rhs) * leaf_cols
side_rows = 72
group = points // rank
groups = leaves // group
ring = 2
vmem = pl.BlockSpec(memory_space=pltpu.VMEM)


def params(mib):
    return pltpu.CompilerParams(vmem_limit_bytes=mib << 20)


def cost(cycles):
    return pl.CostEstimate(flops=int(cycles * 400_000), bytes_accessed=1 << 18, transcendentals=0)


class Run:
    def __init__(self, count, skip, source, step, target, offset, both):
        self.count, self.skip, self.source, self.step, self.target = count, skip, source, step, target
        self.offset, self.both = offset, both


def interior_runs():
    across, down = leaf_rows * (leaf_cols - 1), (leaf_rows - 1) * (leaf_cols - 1)
    return [
        Run(leaves, 0, 0, 1, 0, 4, False),
        Run(across, 1, 0, 1, 1, 3, True),
        Run(leaves - leaf_cols, 0, 0, 1, leaf_cols, 1, True),
        Run(down, 1, 0, 1, leaf_cols + 1, 0, True),
        Run(down, 1, 1, 1, leaf_cols, 2, True),
    ]


def edge_runs():
    runs = []
    for first, row, di in ((0, 0, -1), (leaf_cols, leaf_rows - 1, 1)):
        for dj in (-1, 0, 1):
            start = max(0, -dj)
            at = row * leaf_cols + start
            runs.append(Run(leaf_cols - abs(dj), 0, first + start + dj, 1, at, 3 * (di + 1) + dj + 1, False))
    return runs


def side_runs():
    runs = []
    for first, column, dj in ((0, 0, -1), (8, leaf_cols - 1, 1)):
        for di in (-1, 0, 1):
            runs.append(Run(leaf_rows, 0, first + 1 + di, leaf_cols, column, 3 * (di + 1) + dj + 1, False))
    return runs


def cut_runs(runs, first, last):
    pieces, at = [], 0
    for run in runs:
        low, high = max(first - at, 0), min(last - at, run.count)
        if low < high:
            pieces.append((run, low, high))
        at += run.count
    return pieces


zero_row = 9 * leaves


def listed(pieces):
    items = []
    for run, low, high in pieces:
        for q in range(low, high):
            moved = q + run.skip * (q // (leaf_cols - 1))
            source, target = moved + run.source, run.step * moved + run.target
            back = (8 - run.offset) * leaves + source if run.both else None
            items.append((source, target, run.offset * leaves + target, back))
    return items


def split(value):
    high = value.astype(bf16)
    return high, (value - high.astype(f32)).astype(bf16)


def thirds(value):
    high = value.astype(bf16).astype(f32)
    rest = value - high
    middle = rest.astype(bf16).astype(f32)
    return high, middle, rest - middle


def dot(left, right):
    return jnp.dot(left, right, preferred_element_type=f32)


def dot_t(left, right):
    return lax.dot_general(left, right, (((1,), (1,)), ((), ())), preferred_element_type=f32)


def sixteen(leaf):
    return pl.ds(leaf * 16 if isinstance(leaf, int) else pl.multiple_of(leaf * 16, 16), 16)


def fill_tables(count, start, coords, left, right, heights, wides):
    parts = []
    for c in range(3):
        moved = (coords[pl.ds(c * count, count), :] - start[c]) * turns
        if c == 2:
            heights[...] = moved
        else:
            parts.append(thirds(moved))
    k = lax.broadcasted_iota(jnp.int32, (16, points), 0)
    ones_x = jnp.where(k < 3, 1.0, 0.0)
    ones_y = jnp.where((k >= 3) & (k < 6), 1.0, 0.0)
    ones_t = jnp.where((k >= 6) & (k < 9), 1.0, 0.0)
    for role in range(1 if right is None else 3):
        wide = wides.at[role]
        for leaf in range(count):
            wide[pl.ds(leaf * 16, 16), :] = (ones_t, ones_x, ones_y)[role]
        for first in range(0, count, 8):
            for m in range(3):
                for c in range(2):
                    part = parts[c][m][first : first + 8]
                    if role == 0:
                        wide[pl.ds(first * 16 + 3 * c + m, 8, stride=16), :] = part
                    elif role == c + 1:
                        wide[pl.ds(first * 16 + 6 + m, 8, stride=16), :] = -part
        if role == 0:
            for leaf in range(count):
                left[leaf * points : (leaf + 1) * points, :] = wide[leaf * 16 : leaf * 16 + 16, :].T.astype(bf16)
        else:
            right[:, points * (role - 1) : points * role] = wide[...].astype(bf16)


def lane_block(n):
    return lax.broadcasted_iota(jnp.int32, (rhs, points), 1) // rank == n


def spread_blocks(transfer, blocks):
    same = lax.broadcasted_iota(jnp.int32, (points, points), 0) // rank == lax.broadcasted_iota(jnp.int32, (points, points), 1) // rank
    for n in range(2):
        wide = jnp.concatenate([transfer[n]] * group, axis=1)
        wide = jnp.where(same, jnp.concatenate([wide] * group, axis=0), 0.0)
        blocks[2 * n], blocks[2 * n + 1] = split(wide)


def start_copies(fars, heres, arrived):
    copies = [pltpu.make_async_copy(far, here, arrived.at[n]) for n, (far, here) in enumerate(zip(fars, heres))]
    for copy in copies:
        copy.start()
    return copies


def compress_kernel(coords_far, sources_far, compress_far, halves, payload, coords, sources, compress, arrived):
    chunk = groups // 4 * points
    chunks = [slice(n * chunk, (n + 1) * chunk) for n in range(4)]
    copies = start_copies(
        [sources_far, coords_far] + [compress_far.at[rows] for rows in chunks], [sources, coords] + [compress.at[rows] for rows in chunks], arrived
    )
    copies[0].wait()
    for leaf in range(leaves):
        high, low = split(sources[pl.ds(leaf, rhs, stride=leaves), :])
        halves[sixteen(leaf), :] = jnp.concatenate([high, low], axis=0)
    copies[1].wait()
    odd = lax.axis_index("row") % 2
    for k in range(2):
        row = (leaf_rows - 1) * (1 - odd if k == 0 else odd)
        for c in range(3 + rhs):
            ref, at = (coords, c) if c < 3 else (sources, c - 3)
            to = points + k * edge_rows + c * leaf_cols
            payload[to : to + leaf_cols, :] = ref[pl.ds(pl.multiple_of(at * leaves + row * leaf_cols, 8), leaf_cols), :]
    for g in range(groups):
        if g % (groups // 4) == 0:
            copies[2 + g // (groups // 4)].wait()
        high, low = split(compress[g * points : (g + 1) * points, :])
        got = dot_t(halves[g * 16 * group : (g + 1) * 16 * group, :], jnp.concatenate([high, low], axis=0))
        got = got[:, :points] + got[:, points:]
        total = jnp.zeros((rhs, points), f32)
        for n in range(group):
            total = jnp.where(lane_block(n), got[n * 16 : n * 16 + 8] + got[n * 16 + 8 : n * 16 + 16], total)
        payload[g * rhs : (g + 1) * rhs, :] = total


def prep_kernel(coords, mask, row_transfer, col_transfer, left, right, heights, row_blocks, col_blocks, weights, wides):
    start = [coords[c * leaves : c * leaves + 1, 0:1] for c in range(3)]
    fill_tables(leaves, start, coords, left, right, heights, wides)
    spread_blocks(row_transfer, row_blocks)
    spread_blocks(col_transfer, col_blocks)
    diagonal = lax.broadcasted_iota(jnp.int32, (leaf_cols, leaf_cols), 0) == lax.broadcasted_iota(jnp.int32, (leaf_cols, leaf_cols), 1)
    ones = jnp.ones((leaf_cols, points), bf16)
    for k in range(9):
        for i in range(leaf_rows):
            spread = jnp.where(diagonal, mask[k, i : i + 1, :].astype(f32), 0.0).astype(bf16)
            at = k * leaves + i * leaf_cols
            weights[at : at + leaf_cols, :] = dot(spread, ones)
    weights[zero_row : zero_row + 8, :] = jnp.zeros((8, points), f32)


def halo_tables(count, coords, values, left, heights, halves, wides):
    start = [coords[c * leaves : c * leaves + 1, 0:1] for c in range(3)]
    fill_tables(count, start, values, left, None, heights, wides)
    for leaf in range(count):
        high, low = split(values[pl.ds(3 * count + leaf, rhs, stride=count), :])
        halves[sixteen(leaf), :] = jnp.concatenate([high, low], axis=0)


def edges_kernel(coords, edges, left, heights, halves, wides):
    halo_tables(edge_leaves, coords, edges, left, heights, halves, wides)


def side_tables(coords, first, second, third, fourth, left, heights, halves, wides, sides):
    col = lax.axis_index("col")
    odd = col % 2 == 1
    inner = (col > 0) & (col < lax.axis_size("col") - 1)
    at = slice(points, points + side_rows)
    near = first[at, :]
    far = jnp.where((col % 8 == 3) | (col % 8 == 4), third[at, :], fourth[at, :])
    far = jnp.where((col % 4 == 1) | (col % 4 == 2), second[at, :], far)
    far = jnp.where(inner, far, 0.0)
    to_left, to_right = jnp.where(odd, near, far), jnp.where(odd, far, near)
    gap = jnp.zeros((2, points), f32)
    for c in range(3 + rhs):
        at = slice(6 * c, 6 * c + 6)
        sides[c * side_leaves : (c + 1) * side_leaves, :] = jnp.concatenate([to_left[at], gap, to_right[at], gap], axis=0)
    halo_tables(side_leaves, coords, sides, left, heights, halves, wides)


def level(mine, theirs, blocks):
    total = None
    for value, n in ((mine, 0), (theirs, 2)):
        high, low = split(value)
        got = dot_t(jnp.concatenate([high, low], axis=0), jnp.concatenate([blocks[n], blocks[n + 1]], axis=0))
        got = got[:, :points] + got[:, points:]
        got = got[:points] + got[points:]
        total = got if total is None else total + got
    return total


def level_kernel(forward, mine, theirs, blocks, payload):
    payload[:points, :] = level(mine[:points, :], theirs[:points, :], blocks)
    payload[points:, :] = theirs[forward:, :]


def turn_kernel(mine, theirs, blocks, coords, sources, first, second, payload, edges):
    payload[:points, :] = level(mine[:points, :], theirs[:points, :], blocks)
    row, col = lax.axis_index("row"), lax.axis_index("col")
    odd = row % 2 == 1
    around = (row % 4 == 1) | (row % 4 == 2)
    inner = (row > 0) & (row < lax.axis_size("row") - 1)
    for c in range(3 + rhs):
        at = slice(points + c * leaf_cols, points + (c + 1) * leaf_cols)
        near = first[at, :]
        far = jnp.where(inner, jnp.where(around, second[at, :], theirs[at, :]), 0.0)
        edges[c * edge_leaves : c * edge_leaves + leaf_cols, :] = jnp.where(odd, near, far)
        edges[c * edge_leaves + leaf_cols : (c + 1) * edge_leaves, :] = jnp.where(odd, far, near)
    for k in range(2):
        j = (leaf_cols - 1) * (1 - col % 2 if k == 0 else col % 2)
        base = points + k * side_rows
        for c in range(3 + rhs):
            ref, at = (coords, c) if c < 3 else (sources, c - 3)
            payload[base + 6 * c : base + 6 * c + 1, :] = edges[pl.ds(c * edge_leaves + j, 1), :]
            for i in range(leaf_rows):
                payload[base + 6 * c + 1 + i : base + 6 * c + 2 + i, :] = ref[pl.ds(at * leaves + i * leaf_cols + j, 1), :]
            payload[base + 6 * c + 5 : base + 6 * c + 6, :] = edges[pl.ds(c * edge_leaves + leaf_cols + j, 1), :]
        payload[base + 66 : base + side_rows, :] = jnp.zeros((side_rows - 66, points), f32)


def near_kernel(items, batch, weights, left, source_heights, source_halves, right, heights, halves, seed, acc, gaps, splats, kerns):
    acc[...] = seed[...]

    def subtract(item, n, gap, splat):
        source, target = item[:2]
        gap[n] = dot(left[source * points : (source + 1) * points, :], right[sixteen(target), :])
        splat[n] = jnp.broadcast_to(source_heights[source : source + 1, :], (points, points)).T

    def evaluate(item, n, gap, splat, kern):
        height = heights[item[1] : item[1] + 1, :]
        for g in range(points // 32):
            at_rows = slice(32 * g, 32 * g + 32)
            dx, dy, dz = gap[n, at_rows, :points], gap[n, at_rows, points:], splat[n, at_rows] - height
            distance_sq = dx * dx + dy * dy + dz * dz
            safe = jnp.maximum(distance_sq, 1e-30)
            turn = safe * lax.rsqrt(safe)
            f = turn - jnp.round(turn)
            u = f * f
            m = f * (((u + b2) * u + b1) * u + b0)
            value = (m * m - half_gain) * lax.rsqrt(distance_sq + eps_sq)
            high, low = split(value)
            kern[n, 0, at_rows] = high
            kern[n, 1, at_rows] = low

    def receive(leaf, weight, got):
        at = slice(leaf * rhs, (leaf + 1) * rhs)
        acc[at, :] += (got[:rhs] + got[rhs:]) * weights[weight : weight + 1, :]

    def apply(item, n, kern):
        source, target, weight, back = item
        pair = jnp.concatenate([kern[n, 0], kern[n, 1]], axis=1)
        got = dot(source_halves[sixteen(source), :], pair)
        receive(target, weight, got[:, :points] + got[:, points:])
        if back is not None:
            mine = halves[sixteen(target), :]
            receive(source, back, dot_t(jnp.concatenate([mine, mine], axis=1), pair))

    stages = [items[at : at + batch] for at in range(0, len(items), batch)]
    for k in range(-1, len(stages) + 1):
        if k >= 1:
            for n, item in enumerate(stages[k - 1]):
                apply(item, n, kerns.at[(k - 1) % ring])
        if k + 1 < len(stages):
            for n, item in enumerate(stages[k + 1]):
                subtract(item, n, gaps.at[(k + 1) % ring], splats.at[(k + 1) % ring])
        if 0 <= k < len(stages):
            for n, item in enumerate(stages[k]):
                evaluate(item, n, gaps.at[k % ring], splats.at[k % ring], kerns.at[k % ring])


def near_scratch(batch):
    return [
        pltpu.VMEM((ring, batch, points, 2 * points), f32),
        pltpu.VMEM((ring, batch, points, points), f32),
        pltpu.VMEM((ring, batch, 2, points, points), bf16),
    ]


def near_piece(pieces, weights, source_tables, target_tables, seed):
    items = listed(pieces)
    batch = 4 if any(item[3] is not None for item in items) else 8
    left, source_heights, source_halves = source_tables
    right, heights, halves = target_tables
    return pl.pallas_call(
        functools.partial(near_kernel, items, batch),
        out_shape=jax.ShapeDtypeStruct(seed.shape, f32),
        in_specs=[vmem] * 8,
        out_specs=vmem,
        scratch_shapes=near_scratch(batch),
        compiler_params=params(24),
        cost_estimate=cost(len(items) * 110),
        name="near",
    )(weights, left, source_heights, source_halves, right, heights, halves, seed)


def finish_kernel(
    items, weights, coords, first, second, third, theirs, mine, blocks, expand, right, heights, halves, seed, out,
    left, source_heights, source_halves, wides, sides, acc, gaps, splats, kerns, *far,
):
    side_tables(coords, first, second, third, theirs, left, source_heights, source_halves, wides, sides)
    coeffs = level(mine[:points, :], theirs[:points, :], blocks)
    for g in range(groups):
        here = coeffs[g * rhs : (g + 1) * rhs]
        rows = jnp.concatenate([jnp.where(lane_block(n), here, 0.0) for n in range(group)], axis=0)
        high, low = split(rows)
        e_high, e_low = split(expand[g * points : (g + 1) * points, :])
        got = dot(jnp.concatenate([high, low], axis=0), jnp.concatenate([e_high, e_low], axis=1))
        got = got[:, :points] + got[:, points:]
        far[0][g * group * rhs : (g + 1) * group * rhs, :] = got[: group * rhs] + got[group * rhs :]
    near_kernel(items, 8, weights, left, source_heights, source_halves, right, heights, halves, seed, acc, gaps, splats, kerns)
    order = sorted(range(leaves), key=lambda leaf: leaf % leaf_cols in (0, leaf_cols - 1))
    for leaf in order:
        at = slice(leaf * rhs, (leaf + 1) * rhs)
        out[pl.ds(leaf, rhs, stride=leaves), :] = acc[at, :] * near_gain + far[0][at, :]


def table_shapes(count):
    return (
        jax.ShapeDtypeStruct((count * points, 16), bf16),
        jax.ShapeDtypeStruct((count * 16, 2 * points), bf16),
        jax.ShapeDtypeStruct((count, points), f32),
        jax.ShapeDtypeStruct((count * 16, points), bf16),
    )


def partner_of(block, axis, distance):
    route = [(i, i ^ (1 << distance)) for i in range(lax.axis_size(axis))]
    return lax.ppermute(block, axis, route)


def array(*shape):
    return jax.ShapeDtypeStruct(shape, f32)


def small_call(body, name, out_shape, *operands):
    single = not isinstance(out_shape, tuple)
    return pl.pallas_call(
        body,
        out_shape=out_shape,
        in_specs=[vmem] * len(operands),
        out_specs=vmem if single else (vmem,) * len(out_shape),
        compiler_params=params(16),
        cost_estimate=cost(600),
        name=name,
    )(*operands)


def far_call(body, name, out_shape, scratch, *operands):
    return pl.pallas_call(
        body,
        out_shape=out_shape,
        in_specs=[pl.BlockSpec(memory_space=pltpu.HBM)] * len(operands),
        out_specs=(vmem,) * len(out_shape),
        scratch_shapes=scratch + [pltpu.SemaphoreType.DMA((8,))],
        compiler_params=params(24),
        cost_estimate=cost(2000),
        name=name,
    )(*[pltpu.with_memory_space_constraint(operand, pltpu.HBM) for operand in operands])


def shards(coords, sources, neighbour_mask, compress, expand, row_transfer, col_transfer):
    coords = coords.reshape(-1, points)
    sources = sources.reshape(-1, points)
    halves, payload = far_call(
        compress_kernel,
        "compress",
        (table_shapes(leaves)[3], array(points + 2 * edge_rows, points)),
        [pltpu.VMEM(shape, f32) for shape in ((3 * leaves, points), (rhs * leaves, points), (leaves * rank, points))],
        coords, sources, compress.reshape(-1, points),
    )
    row_bits, col_bits = (lax.axis_size(axis).bit_length() - 1 for axis in ("row", "col"))
    axes = ["row"] * row_bits + ["col"] * col_bits
    bits = [*range(row_bits), *range(col_bits)]
    theirs = partner_of(payload, "row", 0)
    block_shape = jax.ShapeDtypeStruct((4, points, points), bf16)
    coords_later, payload = lax.optimization_barrier((coords, payload))
    left, right, heights, row_blocks, col_blocks, weights = pl.pallas_call(
        prep_kernel,
        out_shape=table_shapes(leaves)[:3] + (block_shape, block_shape, array(zero_row + 8, points)),
        in_specs=[vmem] * 4,
        out_specs=(vmem,) * 6,
        scratch_shapes=[pltpu.VMEM((3, leaves * 16, points), f32)],
        compiler_params=params(16),
        cost_estimate=cost(2000),
        name="prep",
    )(coords_later, neighbour_mask, row_transfer[:, 0, 0], col_transfer[:, 0, 0])
    own, targets = (left, heights, halves), (right, heights, halves)
    inner, edge, side = interior_runs(), edge_runs(), side_runs()
    counts = [sum(run.count for run in runs) for runs in (inner, edge, side)]
    windows = row_bits + col_bits - 1
    edge_windows = (row_bits, row_bits + 2)
    inner_windows = [n for n in range(1, windows + 1) if n not in edge_windows]
    cuts = [counts[0] * k // len(inner_windows) // 4 * 4 for k in range(len(inner_windows))] + [counts[0]]
    half = -(-counts[1] // 2 // 8) * 8
    acc = jnp.zeros((leaves * rhs, points), f32)
    received = [theirs]
    for n, (axis, bit) in enumerate(zip(axes, bits)):
        blocks = row_blocks if axis == "row" else col_blocks
        if n > 0:
            theirs = partner_of(payload, axis, bit)
            payload, acc = lax.optimization_barrier((payload, acc))
            if n == row_bits:
                edges, acc = lax.optimization_barrier((edges, acc))
                shapes = table_shapes(edge_leaves)
                edge_tables = pl.pallas_call(
                    edges_kernel,
                    out_shape=(shapes[0], shapes[2], shapes[3]),
                    in_specs=[vmem] * 2,
                    out_specs=(vmem,) * 3,
                    scratch_shapes=[pltpu.VMEM((1, edge_leaves * 16, points), f32)],
                    compiler_params=params(16),
                    cost_estimate=cost(1000),
                    name="edges",
                )(coords, edges)
            if n in edge_windows:
                some = cut_runs(edge, 0, half) if n == row_bits else cut_runs(edge, half, counts[1])
                acc = near_piece(some, weights, edge_tables, targets, acc)
            else:
                k = inner_windows.index(n)
                acc = near_piece(cut_runs(inner, cuts[k], cuts[k + 1]), weights, own, targets, acc)
            theirs, acc = lax.optimization_barrier((theirs, acc))
            received.append(theirs)
        if n == row_bits - 1:
            payload, edges = small_call(
                turn_kernel,
                "turn",
                (array(points + 2 * side_rows, points), array((3 + rhs) * edge_leaves, points)),
                payload, theirs, blocks, coords, sources, received[0], received[1],
            )
        elif n < windows:
            rows = edge_rows if axis == "row" else side_rows
            skip = points + rows if bit == 0 else points
            payload = small_call(functools.partial(level_kernel, skip), "level", array(points + rows, points), payload, theirs, blocks)
    shapes = table_shapes(side_leaves)
    operands = (weights, coords, *received[row_bits:], payload, blocks, expand.reshape(-1, points), *targets, acc)
    out = pl.pallas_call(
        functools.partial(finish_kernel, listed(cut_runs(side, 0, counts[2]))),
        out_shape=array(rhs * leaves, points),
        in_specs=[vmem] * len(operands),
        out_specs=vmem,
        scratch_shapes=[pltpu.VMEM(shape.shape, shape.dtype) for shape in (shapes[0], shapes[2], shapes[3])]
        + [
            pltpu.VMEM((1, side_leaves * 16, points), f32),
            pltpu.VMEM(((3 + rhs) * side_leaves, points), f32),
            pltpu.VMEM((rhs * leaves, points), f32),
        ]
        + near_scratch(8)
        + [pltpu.VMEM((rhs * leaves, points), f32)],
        compiler_params=params(24),
        cost_estimate=cost(5000),
        name="finish",
    )(*operands)
    return out.reshape(rhs, leaf_rows, leaf_cols, points)


def solution(mesh):
    in_specs = (
        P(None, "row", "col", None),
        P(None, "row", "col", None),
        P(None, "row", "col"),
        P("row", "col", None, None),
        P("row", "col", None, None),
        P(None, "row", "col", None, None),
        P(None, "row", "col", None, None),
    )
    out_specs = P(None, "row", "col", None)
    return jax.shard_map(shards, mesh=mesh, in_specs=in_specs, out_specs=out_specs, check_vma=False)
```

```python
import functools

import jax
import jax.numpy as jnp
import numpy as np
from jax import lax
from jax.experimental import pallas as pl
from jax.experimental.pallas import tpu as pltpu
from jax.sharding import PartitionSpec as P

wave_number = 6.0
softening = 0.05
near_scale = 1.0 / 32.0
highest = lax.Precision.HIGHEST
f32, bf16 = jnp.float32, jnp.bfloat16

turns = wave_number / (2.0 * np.pi)
eps_sq = (softening * turns) ** 2
sine = (3.14157435, -5.16695951, 2.54064763, -0.55204997)
b0, b1, b2 = (sine[0] / sine[3], sine[1] / sine[3], sine[2] / sine[3])
half_gain = 1.0 / (2.0 * sine[3] ** 2)
near_gain = -2.0 * sine[3] ** 2 * turns * near_scale

leaf_rows, leaf_cols, points, rank, rhs = 4, 16, 128, 32, 8
leaves = leaf_rows * leaf_cols
edge_leaves = 2 * leaf_cols
side_leaves = 8
edge_rows = (3 + rhs) * leaf_cols
side_rows = 72
group = points // rank
groups = leaves // group
ring = 2
vmem = pl.BlockSpec(memory_space=pltpu.VMEM)


def params(mib):
    return pltpu.CompilerParams(vmem_limit_bytes=mib << 20)


def cost(cycles):
    return pl.CostEstimate(flops=int(cycles * 400_000), bytes_accessed=1 << 18, transcendentals=0)


class Run:
    def __init__(self, count, skip, source, step, target, offset, both):
        self.count, self.skip, self.source, self.step, self.target = count, skip, source, step, target
        self.offset, self.both = offset, both


def interior_runs():
    across, down = leaf_rows * (leaf_cols - 1), (leaf_rows - 1) * (leaf_cols - 1)
    return [
        Run(leaves, 0, 0, 1, 0, 4, False),
        Run(across, 1, 0, 1, 1, 3, True),
        Run(leaves - leaf_cols, 0, 0, 1, leaf_cols, 1, True),
        Run(down, 1, 0, 1, leaf_cols + 1, 0, True),
        Run(down, 1, 1, 1, leaf_cols, 2, True),
    ]


def edge_runs():
    runs = []
    for first, row, di in ((0, 0, -1), (leaf_cols, leaf_rows - 1, 1)):
        for dj in (-1, 0, 1):
            start = max(0, -dj)
            at = row * leaf_cols + start
            runs.append(Run(leaf_cols - abs(dj), 0, first + start + dj, 1, at, 3 * (di + 1) + dj + 1, False))
    return runs


def column_items(facing):
    right = lax.axis_index("col") % 2
    right = 1 - right if facing else right
    items = []
    for di in (-1, 0, 1):
        for i in range(leaf_rows):
            target = i * leaf_cols + (leaf_cols - 1) * right
            items.append((i + 1 + di, target, (3 * (di + 1) + 2 * right) * leaves + target, None))
    return items


def cut_runs(runs, first, last):
    pieces, at = [], 0
    for run in runs:
        low, high = max(first - at, 0), min(last - at, run.count)
        if low < high:
            pieces.append((run, low, high))
        at += run.count
    return pieces


zero_row = 9 * leaves


def listed(pieces):
    items = []
    for run, low, high in pieces:
        for q in range(low, high):
            moved = q + run.skip * (q // (leaf_cols - 1))
            source, target = moved + run.source, run.step * moved + run.target
            back = (8 - run.offset) * leaves + source if run.both else None
            items.append((source, target, run.offset * leaves + target, back))
    return items


def split(value):
    high = value.astype(bf16)
    return high, (value - high.astype(f32)).astype(bf16)


def thirds(value):
    high = value.astype(bf16).astype(f32)
    rest = value - high
    middle = rest.astype(bf16).astype(f32)
    return high, middle, rest - middle


def dot(left, right):
    return jnp.dot(left, right, preferred_element_type=f32)


def dot_t(left, right):
    return lax.dot_general(left, right, (((1,), (1,)), ((), ())), preferred_element_type=f32)


def sixteen(leaf):
    return pl.ds(leaf * 16 if isinstance(leaf, int) else pl.multiple_of(leaf * 16, 16), 16)


def fill_tables(count, start, coords, left, right, heights, wides):
    parts = []
    for c in range(3):
        moved = (coords[pl.ds(c * count, count), :] - start[c]) * turns
        if c == 2:
            heights[...] = moved
        else:
            parts.append(thirds(moved))
    k = lax.broadcasted_iota(jnp.int32, (16, points), 0)
    ones_x = jnp.where(k < 3, 1.0, 0.0)
    ones_y = jnp.where((k >= 3) & (k < 6), 1.0, 0.0)
    ones_t = jnp.where((k >= 6) & (k < 9), 1.0, 0.0)
    for role in range(1 if right is None else 3):
        wide = wides.at[role]
        for leaf in range(count):
            wide[pl.ds(leaf * 16, 16), :] = (ones_t, ones_x, ones_y)[role]
        for first in range(0, count, 8):
            for m in range(3):
                for c in range(2):
                    part = parts[c][m][first : first + 8]
                    if role == 0:
                        wide[pl.ds(first * 16 + 3 * c + m, 8, stride=16), :] = part
                    elif role == c + 1:
                        wide[pl.ds(first * 16 + 6 + m, 8, stride=16), :] = -part
        if role == 0:
            for leaf in range(count):
                left[leaf * points : (leaf + 1) * points, :] = wide[leaf * 16 : leaf * 16 + 16, :].T.astype(bf16)
        else:
            right[:, points * (role - 1) : points * role] = wide[...].astype(bf16)


def lane_block(n):
    return lax.broadcasted_iota(jnp.int32, (rhs, points), 1) // rank == n


def spread_blocks(transfer, blocks):
    same = lax.broadcasted_iota(jnp.int32, (points, points), 0) // rank == lax.broadcasted_iota(jnp.int32, (points, points), 1) // rank
    for n in range(2):
        wide = jnp.concatenate([transfer[n]] * group, axis=1)
        wide = jnp.where(same, jnp.concatenate([wide] * group, axis=0), 0.0)
        blocks[2 * n], blocks[2 * n + 1] = split(wide)


def start_copies(fars, heres, arrived):
    copies = [pltpu.make_async_copy(far, here, arrived.at[n]) for n, (far, here) in enumerate(zip(fars, heres))]
    for copy in copies:
        copy.start()
    return copies


def compress_kernel(coords_far, sources_far, compress_far, halves, payload, coords, sources, compress, arrived):
    copies = start_copies((sources_far, coords_far, compress_far), (sources, coords, compress), arrived)
    copies[0].wait()
    for leaf in range(leaves):
        high, low = split(sources[pl.ds(leaf, rhs, stride=leaves), :])
        halves[sixteen(leaf), :] = jnp.concatenate([high, low], axis=0)
    copies[1].wait()
    odd = lax.axis_index("row") % 2
    for k in range(2):
        row = (leaf_rows - 1) * (1 - odd if k == 0 else odd)
        for c in range(3 + rhs):
            ref, at = (coords, c) if c < 3 else (sources, c - 3)
            to = points + k * edge_rows + c * leaf_cols
            payload[to : to + leaf_cols, :] = ref[pl.ds(pl.multiple_of(at * leaves + row * leaf_cols, 8), leaf_cols), :]
    copies[2].wait()
    for g in range(groups):
        high, low = split(compress[g * points : (g + 1) * points, :])
        got = dot_t(halves[g * 16 * group : (g + 1) * 16 * group, :], jnp.concatenate([high, low], axis=0))
        got = got[:, :points] + got[:, points:]
        total = jnp.zeros((rhs, points), f32)
        for n in range(group):
            total = jnp.where(lane_block(n), got[n * 16 : n * 16 + 8] + got[n * 16 + 8 : n * 16 + 16], total)
        payload[g * rhs : (g + 1) * rhs, :] = total


def prep_kernel(coords, mask, row_transfer, col_transfer, left, right, heights, row_blocks, col_blocks, weights, wides):
    start = [coords[c * leaves : c * leaves + 1, 0:1] for c in range(3)]
    fill_tables(leaves, start, coords, left, right, heights, wides)
    spread_blocks(row_transfer, row_blocks)
    spread_blocks(col_transfer, col_blocks)
    diagonal = lax.broadcasted_iota(jnp.int32, (leaf_cols, leaf_cols), 0) == lax.broadcasted_iota(jnp.int32, (leaf_cols, leaf_cols), 1)
    ones = jnp.ones((leaf_cols, points), bf16)
    for k in range(9):
        for i in range(leaf_rows):
            spread = jnp.where(diagonal, mask[k, i : i + 1, :].astype(f32), 0.0).astype(bf16)
            at = k * leaves + i * leaf_cols
            weights[at : at + leaf_cols, :] = dot(spread, ones)
    weights[zero_row : zero_row + 8, :] = jnp.zeros((8, points), f32)


def halo_tables(count, coords, values, left, heights, halves, wides):
    start = [coords[c * leaves : c * leaves + 1, 0:1] for c in range(3)]
    fill_tables(count, start, values, left, None, heights, wides)
    for leaf in range(count):
        high, low = split(values[pl.ds(3 * count + leaf, rhs, stride=count), :])
        halves[sixteen(leaf), :] = jnp.concatenate([high, low], axis=0)


def edges_kernel(coords, edges, left, heights, halves, wides):
    halo_tables(edge_leaves, coords, edges, left, heights, halves, wides)


def column_tables(coords, column, left, heights, halves, wides, values):
    for c in range(3 + rhs):
        values[c * side_leaves : c * side_leaves + 6, :] = column[6 * c : 6 * c + 6]
        values[c * side_leaves + 6 : (c + 1) * side_leaves, :] = jnp.zeros((2, points), f32)
    halo_tables(side_leaves, coords, values, left, heights, halves, wides)


def facing_kernel(coords, first, left, heights, halves, wides, values):
    column_tables(coords, first[points : points + side_rows, :], left, heights, halves, wides, values)


def far_column(second, third, fourth):
    col = lax.axis_index("col")
    inner = (col > 0) & (col < lax.axis_size("col") - 1)
    at = slice(points, points + side_rows)
    far = jnp.where((col % 8 == 3) | (col % 8 == 4), third[at, :], fourth[at, :])
    far = jnp.where((col % 4 == 1) | (col % 4 == 2), second[at, :], far)
    return jnp.where(inner, far, 0.0)


def level(mine, theirs, blocks):
    total = None
    for value, n in ((mine, 0), (theirs, 2)):
        high, low = split(value)
        got = dot_t(jnp.concatenate([high, low], axis=0), jnp.concatenate([blocks[n], blocks[n + 1]], axis=0))
        got = got[:, :points] + got[:, points:]
        got = got[:points] + got[points:]
        total = got if total is None else total + got
    return total


def level_kernel(forward, mine, theirs, blocks, payload):
    payload[:points, :] = level(mine[:points, :], theirs[:points, :], blocks)
    payload[points:, :] = theirs[forward:, :]


def turn_kernel(mine, theirs, blocks, coords, sources, first, second, payload, edges):
    payload[:points, :] = level(mine[:points, :], theirs[:points, :], blocks)
    row, col = lax.axis_index("row"), lax.axis_index("col")
    odd = row % 2 == 1
    around = (row % 4 == 1) | (row % 4 == 2)
    inner = (row > 0) & (row < lax.axis_size("row") - 1)
    for c in range(3 + rhs):
        at = slice(points + c * leaf_cols, points + (c + 1) * leaf_cols)
        near = first[at, :]
        far = jnp.where(inner, jnp.where(around, second[at, :], theirs[at, :]), 0.0)
        edges[c * edge_leaves : c * edge_leaves + leaf_cols, :] = jnp.where(odd, near, far)
        edges[c * edge_leaves + leaf_cols : (c + 1) * edge_leaves, :] = jnp.where(odd, far, near)
    for k in range(2):
        j = (leaf_cols - 1) * (1 - col % 2 if k == 0 else col % 2)
        base = points + k * side_rows
        for c in range(3 + rhs):
            ref, at = (coords, c) if c < 3 else (sources, c - 3)
            payload[base + 6 * c : base + 6 * c + 1, :] = edges[pl.ds(c * edge_leaves + j, 1), :]
            for i in range(leaf_rows):
                payload[base + 6 * c + 1 + i : base + 6 * c + 2 + i, :] = ref[pl.ds(at * leaves + i * leaf_cols + j, 1), :]
            payload[base + 6 * c + 5 : base + 6 * c + 6, :] = edges[pl.ds(c * edge_leaves + leaf_cols + j, 1), :]
        payload[base + 66 : base + side_rows, :] = jnp.zeros((side_rows - 66, points), f32)


def near_kernel(items, batch, weights, left, source_heights, source_halves, right, heights, halves, seed, acc, gaps, splats, kerns):
    acc[...] = seed[...]
    items = items() if callable(items) else items

    def subtract(item, n, gap, splat):
        source, target = item[:2]
        gap[n] = dot(left[source * points : (source + 1) * points, :], right[sixteen(target), :])
        splat[n] = jnp.broadcast_to(source_heights[source : source + 1, :], (points, points)).T

    def evaluate(item, n, gap, splat, kern):
        height = heights[pl.ds(item[1], 1), :]
        for g in range(points // 32):
            at_rows = slice(32 * g, 32 * g + 32)
            dx, dy, dz = gap[n, at_rows, :points], gap[n, at_rows, points:], splat[n, at_rows] - height
            distance_sq = dx * dx + dy * dy + dz * dz
            safe = jnp.maximum(distance_sq, 1e-30)
            turn = safe * lax.rsqrt(safe)
            f = turn - jnp.round(turn)
            u = f * f
            m = f * (((u + b2) * u + b1) * u + b0)
            value = (m * m - half_gain) * lax.rsqrt(distance_sq + eps_sq)
            high, low = split(value)
            kern[n, 0, at_rows] = high
            kern[n, 1, at_rows] = low

    def receive(leaf, weight, got):
        at = pl.ds(leaf * rhs if isinstance(leaf, int) else pl.multiple_of(leaf * rhs, rhs), rhs)
        acc[at, :] += (got[:rhs] + got[rhs:]) * weights[pl.ds(weight, 1), :]

    def apply(item, n, kern):
        source, target, weight, back = item
        pair = jnp.concatenate([kern[n, 0], kern[n, 1]], axis=1)
        got = dot(source_halves[sixteen(source), :], pair)
        receive(target, weight, got[:, :points] + got[:, points:])
        if back is not None:
            mine = halves[sixteen(target), :]
            receive(source, back, dot_t(jnp.concatenate([mine, mine], axis=1), pair))

    stages = [items[at : at + batch] for at in range(0, len(items), batch)]
    for k in range(-1, len(stages) + 1):
        if k >= 1:
            for n, item in enumerate(stages[k - 1]):
                apply(item, n, kerns.at[(k - 1) % ring])
        if k + 1 < len(stages):
            for n, item in enumerate(stages[k + 1]):
                subtract(item, n, gaps.at[(k + 1) % ring], splats.at[(k + 1) % ring])
        if 0 <= k < len(stages):
            for n, item in enumerate(stages[k]):
                evaluate(item, n, gaps.at[k % ring], splats.at[k % ring], kerns.at[k % ring])


def near_scratch(batch):
    return [
        pltpu.VMEM((ring, batch, points, 2 * points), f32),
        pltpu.VMEM((ring, batch, points, points), f32),
        pltpu.VMEM((ring, batch, 2, points, points), bf16),
    ]


def near_piece(items, weights, source_tables, target_tables, seed):
    if callable(items):
        count, batch = 3 * leaf_rows, 4
    else:
        count, batch = len(items), 4 if any(item[3] is not None for item in items) else 8
    left, source_heights, source_halves = source_tables
    right, heights, halves = target_tables
    return pl.pallas_call(
        functools.partial(near_kernel, items, batch),
        out_shape=jax.ShapeDtypeStruct(seed.shape, f32),
        in_specs=[vmem] * 8,
        out_specs=vmem,
        scratch_shapes=near_scratch(batch),
        compiler_params=params(24),
        cost_estimate=cost(count * 110),
        name="near",
    )(weights, left, source_heights, source_halves, right, heights, halves, seed)


def finish_kernel(
    weights, coords, second, third, theirs, mine, blocks, expand, right, heights, halves, seed, out,
    left, source_heights, source_halves, wides, sides, acc, gaps, splats, kerns, *far,
):
    column_tables(coords, far_column(second, third, theirs), left, source_heights, source_halves, wides, sides)
    coeffs = level(mine[:points, :], theirs[:points, :], blocks)
    for g in range(groups):
        here = coeffs[g * rhs : (g + 1) * rhs]
        rows = jnp.concatenate([jnp.where(lane_block(n), here, 0.0) for n in range(group)], axis=0)
        high, low = split(rows)
        e_high, e_low = split(expand[g * points : (g + 1) * points, :])
        got = dot(jnp.concatenate([high, low], axis=0), jnp.concatenate([e_high, e_low], axis=1))
        got = got[:, :points] + got[:, points:]
        far[0][g * group * rhs : (g + 1) * group * rhs, :] = got[: group * rhs] + got[group * rhs :]
    near_kernel(functools.partial(column_items, False), 4, weights, left, source_heights, source_halves, right, heights, halves, seed, acc, gaps, splats, kerns)
    order = sorted(range(leaves), key=lambda leaf: leaf % leaf_cols in (0, leaf_cols - 1))
    for leaf in order:
        at = slice(leaf * rhs, (leaf + 1) * rhs)
        out[pl.ds(leaf, rhs, stride=leaves), :] = acc[at, :] * near_gain + far[0][at, :]


def table_shapes(count):
    return (
        jax.ShapeDtypeStruct((count * points, 16), bf16),
        jax.ShapeDtypeStruct((count * 16, 2 * points), bf16),
        jax.ShapeDtypeStruct((count, points), f32),
        jax.ShapeDtypeStruct((count * 16, points), bf16),
    )


def partner_of(block, axis, distance):
    route = [(i, i ^ (1 << distance)) for i in range(lax.axis_size(axis))]
    return lax.ppermute(block, axis, route)


def array(*shape):
    return jax.ShapeDtypeStruct(shape, f32)


def small_call(body, name, out_shape, *operands):
    single = not isinstance(out_shape, tuple)
    return pl.pallas_call(
        body,
        out_shape=out_shape,
        in_specs=[vmem] * len(operands),
        out_specs=vmem if single else (vmem,) * len(out_shape),
        compiler_params=params(16),
        cost_estimate=cost(600),
        name=name,
    )(*operands)


def far_call(body, name, out_shape, scratch, *operands):
    return pl.pallas_call(
        body,
        out_shape=out_shape,
        in_specs=[pl.BlockSpec(memory_space=pltpu.HBM)] * len(operands),
        out_specs=(vmem,) * len(out_shape),
        scratch_shapes=scratch + [pltpu.SemaphoreType.DMA((8,))],
        compiler_params=params(24),
        cost_estimate=cost(2000),
        name=name,
    )(*[pltpu.with_memory_space_constraint(operand, pltpu.HBM) for operand in operands])


def tables_call(body, name, count, scratch, *operands):
    shapes = table_shapes(count)
    return pl.pallas_call(
        body,
        out_shape=(shapes[0], shapes[2], shapes[3]),
        in_specs=[vmem] * len(operands),
        out_specs=(vmem,) * 3,
        scratch_shapes=[pltpu.VMEM(shape, f32) for shape in [(1, count * 16, points)] + scratch],
        compiler_params=params(16),
        cost_estimate=cost(1000),
        name=name,
    )(*operands)


def shards(coords, sources, neighbour_mask, compress, expand, row_transfer, col_transfer):
    coords = coords.reshape(-1, points)
    sources = sources.reshape(-1, points)
    halves, payload = far_call(
        compress_kernel,
        "compress",
        (table_shapes(leaves)[3], array(points + 2 * edge_rows, points)),
        [pltpu.VMEM(shape, f32) for shape in ((3 * leaves, points), (rhs * leaves, points), (leaves * rank, points))],
        coords, sources, compress.reshape(-1, points),
    )
    row_bits, col_bits = (lax.axis_size(axis).bit_length() - 1 for axis in ("row", "col"))
    axes = ["row"] * row_bits + ["col"] * col_bits
    bits = [*range(row_bits), *range(col_bits)]
    theirs = partner_of(payload, "row", 0)
    block_shape = jax.ShapeDtypeStruct((4, points, points), bf16)
    coords_later, payload = lax.optimization_barrier((coords, payload))
    left, right, heights, row_blocks, col_blocks, weights = pl.pallas_call(
        prep_kernel,
        out_shape=table_shapes(leaves)[:3] + (block_shape, block_shape, array(zero_row + 8, points)),
        in_specs=[vmem] * 4,
        out_specs=(vmem,) * 6,
        scratch_shapes=[pltpu.VMEM((3, leaves * 16, points), f32)],
        compiler_params=params(16),
        cost_estimate=cost(2000),
        name="prep",
    )(coords_later, neighbour_mask, row_transfer[:, 0, 0], col_transfer[:, 0, 0])
    own, targets = (left, heights, halves), (right, heights, halves)
    inner, edge = interior_runs(), edge_runs()
    counts = [sum(run.count for run in runs) for runs in (inner, edge)]
    windows = row_bits + col_bits - 1
    edge_windows = (row_bits, row_bits + 2)
    inner_windows = [n for n in range(1, windows + 1) if n not in edge_windows]
    parts = (72, 72, 64, 54)
    cuts = [counts[0] * sum(parts[:k]) // sum(parts) // 4 * 4 for k in range(len(parts))] + [counts[0]]
    half = -(-counts[1] // 2 // 8) * 8
    acc = jnp.zeros((leaves * rhs, points), f32)
    received = [theirs]
    for n, (axis, bit) in enumerate(zip(axes, bits)):
        blocks = row_blocks if axis == "row" else col_blocks
        if n > 0:
            theirs = partner_of(payload, axis, bit)
            payload, acc = lax.optimization_barrier((payload, acc))
            if n == row_bits:
                edges, acc = lax.optimization_barrier((edges, acc))
                edge_tables = tables_call(edges_kernel, "edges", edge_leaves, [], coords, edges)
            if n == row_bits + 1:
                first, acc = lax.optimization_barrier((received[row_bits], acc))
                facing_tables = tables_call(facing_kernel, "facing", side_leaves, [((3 + rhs) * side_leaves, points)], coords, first)
            if n in edge_windows:
                some = cut_runs(edge, 0, half) if n == row_bits else cut_runs(edge, half, counts[1])
                acc = near_piece(listed(some), weights, edge_tables, targets, acc)
            else:
                k = inner_windows.index(n)
                acc = near_piece(listed(cut_runs(inner, cuts[k], cuts[k + 1])), weights, own, targets, acc)
            if n == windows:
                acc = near_piece(functools.partial(column_items, True), weights, facing_tables, targets, acc)
            theirs, acc = lax.optimization_barrier((theirs, acc))
            received.append(theirs)
        if n == row_bits - 1:
            payload, edges = small_call(
                turn_kernel,
                "turn",
                (array(points + 2 * side_rows, points), array((3 + rhs) * edge_leaves, points)),
                payload, theirs, blocks, coords, sources, received[0], received[1],
            )
        elif n < windows:
            rows = edge_rows if axis == "row" else side_rows
            skip = points + rows if bit == 0 else points
            payload = small_call(functools.partial(level_kernel, skip), "level", array(points + rows, points), payload, theirs, blocks)
    shapes = table_shapes(side_leaves)
    operands = (weights, coords, *received[row_bits + 1 :], payload, blocks, expand.reshape(-1, points), *targets, acc)
    out = pl.pallas_call(
        finish_kernel,
        out_shape=array(rhs * leaves, points),
        in_specs=[vmem] * len(operands),
        out_specs=vmem,
        scratch_shapes=[pltpu.VMEM(shape.shape, shape.dtype) for shape in (shapes[0], shapes[2], shapes[3])]
        + [
            pltpu.VMEM((1, side_leaves * 16, points), f32),
            pltpu.VMEM(((3 + rhs) * side_leaves, points), f32),
            pltpu.VMEM((rhs * leaves, points), f32),
        ]
        + near_scratch(4)
        + [pltpu.VMEM((rhs * leaves, points), f32)],
        compiler_params=params(24),
        cost_estimate=cost(5000),
        name="finish",
    )(*operands)
    return out.reshape(rhs, leaf_rows, leaf_cols, points)


def solution(mesh):
    in_specs = (
        P(None, "row", "col", None),
        P(None, "row", "col", None),
        P(None, "row", "col"),
        P("row", "col", None, None),
        P("row", "col", None, None),
        P(None, "row", "col", None, None),
        P(None, "row", "col", None, None),
    )
    out_specs = P(None, "row", "col", None)
    return jax.shard_map(shards, mesh=mesh, in_specs=in_specs, out_specs=out_specs, check_vma=False)
```

```python
import functools

import jax
import jax.numpy as jnp
import numpy as np
from jax import lax
from jax.experimental import pallas as pl
from jax.experimental.pallas import tpu as pltpu
from jax.sharding import PartitionSpec as P

wave_number = 6.0
softening = 0.05
near_scale = 1.0 / 32.0
highest = lax.Precision.HIGHEST
f32, bf16 = jnp.float32, jnp.bfloat16

turns = wave_number / (2.0 * np.pi)
eps_sq = (softening * turns) ** 2
sine = (3.14157435, -5.16695951, 2.54064763, -0.55204997)
b0, b1, b2 = (sine[0] / sine[3], sine[1] / sine[3], sine[2] / sine[3])
half_gain = 1.0 / (2.0 * sine[3] ** 2)
near_gain = -2.0 * sine[3] ** 2 * turns * near_scale

leaf_rows, leaf_cols, points, rank, rhs = 4, 16, 128, 32, 8
leaves = leaf_rows * leaf_cols
edge_leaves = 2 * leaf_cols
side_leaves = 16
edge_rows = (3 + rhs) * leaf_cols
side_rows = 72
group = points // rank
groups = leaves // group
ring = 2
vmem = pl.BlockSpec(memory_space=pltpu.VMEM)


def params(mib):
    return pltpu.CompilerParams(vmem_limit_bytes=mib << 20)


def cost(cycles):
    return pl.CostEstimate(flops=int(cycles * 400_000), bytes_accessed=1 << 18, transcendentals=0)


class Run:
    def __init__(self, count, skip, source, step, target, offset, both):
        self.count, self.skip, self.source, self.step, self.target = count, skip, source, step, target
        self.offset, self.both = offset, both


def interior_runs():
    across, down = leaf_rows * (leaf_cols - 1), (leaf_rows - 1) * (leaf_cols - 1)
    return [
        Run(leaves, 0, 0, 1, 0, 4, False),
        Run(across, 1, 0, 1, 1, 3, True),
        Run(leaves - leaf_cols, 0, 0, 1, leaf_cols, 1, True),
        Run(down, 1, 0, 1, leaf_cols + 1, 0, True),
        Run(down, 1, 1, 1, leaf_cols, 2, True),
    ]


def edge_runs():
    runs = []
    for first, row, di in ((0, 0, -1), (leaf_cols, leaf_rows - 1, 1)):
        for dj in (-1, 0, 1):
            start = max(0, -dj)
            at = row * leaf_cols + start
            runs.append(Run(leaf_cols - abs(dj), 0, first + start + dj, 1, at, 3 * (di + 1) + dj + 1, False))
    return runs


def side_runs():
    runs = []
    for first, column, dj in ((0, 0, -1), (8, leaf_cols - 1, 1)):
        for di in (-1, 0, 1):
            runs.append(Run(leaf_rows, 0, first + 1 + di, leaf_cols, column, 3 * (di + 1) + dj + 1, False))
    return runs


def cut_runs(runs, first, last):
    pieces, at = [], 0
    for run in runs:
        low, high = max(first - at, 0), min(last - at, run.count)
        if low < high:
            pieces.append((run, low, high))
        at += run.count
    return pieces


zero_row = 9 * leaves


def listed(pieces):
    items = []
    for run, low, high in pieces:
        for q in range(low, high):
            moved = q + run.skip * (q // (leaf_cols - 1))
            source, target = moved + run.source, run.step * moved + run.target
            back = (8 - run.offset) * leaves + source if run.both else None
            items.append((source, target, run.offset * leaves + target, back))
    return items


def split(value):
    high = value.astype(bf16)
    return high, (value - high.astype(f32)).astype(bf16)


def thirds(value):
    high = value.astype(bf16).astype(f32)
    rest = value - high
    middle = rest.astype(bf16).astype(f32)
    return high, middle, rest - middle


def dot(left, right):
    return jnp.dot(left, right, preferred_element_type=f32)


def dot_t(left, right):
    return lax.dot_general(left, right, (((1,), (1,)), ((), ())), preferred_element_type=f32)


def sixteen(leaf):
    return pl.ds(leaf * 16 if isinstance(leaf, int) else pl.multiple_of(leaf * 16, 16), 16)


def fill_tables(count, start, coords, left, right, heights, wides):
    parts = []
    for c in range(3):
        moved = (coords[pl.ds(c * count, count), :] - start[c]) * turns
        if c == 2:
            heights[...] = moved
        else:
            parts.append(thirds(moved))
    k = lax.broadcasted_iota(jnp.int32, (16, points), 0)
    ones_x = jnp.where(k < 3, 1.0, 0.0)
    ones_y = jnp.where((k >= 3) & (k < 6), 1.0, 0.0)
    ones_t = jnp.where((k >= 6) & (k < 9), 1.0, 0.0)
    for role in range(1 if right is None else 3):
        wide = wides.at[role]
        for leaf in range(count):
            wide[pl.ds(leaf * 16, 16), :] = (ones_t, ones_x, ones_y)[role]
        for first in range(0, count, 8):
            for m in range(3):
                for c in range(2):
                    part = parts[c][m][first : first + 8]
                    if role == 0:
                        wide[pl.ds(first * 16 + 3 * c + m, 8, stride=16), :] = part
                    elif role == c + 1:
                        wide[pl.ds(first * 16 + 6 + m, 8, stride=16), :] = -part
        if role == 0:
            for leaf in range(count):
                left[leaf * points : (leaf + 1) * points, :] = wide[leaf * 16 : leaf * 16 + 16, :].T.astype(bf16)
        else:
            right[:, points * (role - 1) : points * role] = wide[...].astype(bf16)


def lane_block(n):
    return lax.broadcasted_iota(jnp.int32, (rhs, points), 1) // rank == n


def spread_blocks(transfer, blocks):
    same = lax.broadcasted_iota(jnp.int32, (points, points), 0) // rank == lax.broadcasted_iota(jnp.int32, (points, points), 1) // rank
    for n in range(2):
        wide = jnp.concatenate([transfer[n]] * group, axis=1)
        wide = jnp.where(same, jnp.concatenate([wide] * group, axis=0), 0.0)
        blocks[2 * n], blocks[2 * n + 1] = split(wide)


def start_copies(fars, heres, arrived):
    copies = [pltpu.make_async_copy(far, here, arrived.at[n]) for n, (far, here) in enumerate(zip(fars, heres))]
    for copy in copies:
        copy.start()
    return copies


def compress_kernel(coords_far, sources_far, compress_far, halves, payload, outer, coords, sources, compress, arrived):
    copies = start_copies((sources_far, coords_far, compress_far), (sources, coords, compress), arrived)
    copies[0].wait()
    for leaf in range(leaves):
        high, low = split(sources[pl.ds(leaf, rhs, stride=leaves), :])
        halves[sixteen(leaf), :] = jnp.concatenate([high, low], axis=0)
    copies[1].wait()
    odd = lax.axis_index("row") % 2
    for k in range(2):
        row = (leaf_rows - 1) * (1 - odd if k == 0 else odd)
        for c in range(3 + rhs):
            ref, at = (coords, c) if c < 3 else (sources, c - 3)
            to, base = (payload, points) if k == 0 else (outer, 0)
            to[base + c * leaf_cols : base + (c + 1) * leaf_cols, :] = ref[pl.ds(pl.multiple_of(at * leaves + row * leaf_cols, 8), leaf_cols), :]
    copies[2].wait()
    for g in range(groups):
        high, low = split(compress[g * points : (g + 1) * points, :])
        got = dot_t(halves[g * 16 * group : (g + 1) * 16 * group, :], jnp.concatenate([high, low], axis=0))
        got = got[:, :points] + got[:, points:]
        total = jnp.zeros((rhs, points), f32)
        for n in range(group):
            total = jnp.where(lane_block(n), got[n * 16 : n * 16 + 8] + got[n * 16 + 8 : n * 16 + 16], total)
        payload[g * rhs : (g + 1) * rhs, :] = total


def prep_kernel(coords, mask, row_transfer, col_transfer, left, right, heights, row_blocks, col_blocks, weights, wides):
    start = [coords[c * leaves : c * leaves + 1, 0:1] for c in range(3)]
    fill_tables(leaves, start, coords, left, right, heights, wides)
    spread_blocks(row_transfer, row_blocks)
    spread_blocks(col_transfer, col_blocks)
    diagonal = lax.broadcasted_iota(jnp.int32, (leaf_cols, leaf_cols), 0) == lax.broadcasted_iota(jnp.int32, (leaf_cols, leaf_cols), 1)
    ones = jnp.ones((leaf_cols, points), bf16)
    for k in range(9):
        for i in range(leaf_rows):
            spread = jnp.where(diagonal, mask[k, i : i + 1, :].astype(f32), 0.0).astype(bf16)
            at = k * leaves + i * leaf_cols
            weights[at : at + leaf_cols, :] = dot(spread, ones)
    weights[zero_row : zero_row + 8, :] = jnp.zeros((8, points), f32)


def halo_tables(count, coords, values, left, heights, halves, wides):
    start = [coords[c * leaves : c * leaves + 1, 0:1] for c in range(3)]
    fill_tables(count, start, values, left, None, heights, wides)
    for leaf in range(count):
        high, low = split(values[pl.ds(3 * count + leaf, rhs, stride=count), :])
        halves[sixteen(leaf), :] = jnp.concatenate([high, low], axis=0)


def edges_kernel(coords, edges, left, heights, halves, wides):
    halo_tables(edge_leaves, coords, edges, left, heights, halves, wides)


def sides_kernel(coords, facing, beyond, left, heights, halves, wides, sides):
    odd = lax.axis_index("col") % 2 == 1
    near, far = facing[points : points + side_rows, :], beyond[...]
    to_left, to_right = jnp.where(odd, near, far), jnp.where(odd, far, near)
    gap = jnp.zeros((2, points), f32)
    for c in range(3 + rhs):
        at = slice(6 * c, 6 * c + 6)
        sides[c * side_leaves : (c + 1) * side_leaves, :] = jnp.concatenate([to_left[at], gap, to_right[at], gap], axis=0)
    halo_tables(side_leaves, coords, sides, left, heights, halves, wides)


def level(mine, theirs, blocks):
    total = None
    for value, n in ((mine, 0), (theirs, 2)):
        high, low = split(value)
        got = dot_t(jnp.concatenate([high, low], axis=0), jnp.concatenate([blocks[n], blocks[n + 1]], axis=0))
        got = got[:, :points] + got[:, points:]
        got = got[:points] + got[points:]
        total = got if total is None else total + got
    return total


def level_kernel(mine, theirs, blocks, payload):
    payload[...] = level(mine[:points, :], theirs[:points, :], blocks)


def turn_kernel(mine, theirs, blocks, coords, sources, facing, beyond, payload, outer, edges):
    payload[:points, :] = level(mine[:points, :], theirs[:points, :], blocks)
    odd = lax.axis_index("row") % 2 == 1
    col = lax.axis_index("col")
    for c in range(3 + rhs):
        near = facing[points + c * leaf_cols : points + (c + 1) * leaf_cols, :]
        far = beyond[c * leaf_cols : (c + 1) * leaf_cols, :]
        edges[c * edge_leaves : c * edge_leaves + leaf_cols, :] = jnp.where(odd, near, far)
        edges[c * edge_leaves + leaf_cols : (c + 1) * edge_leaves, :] = jnp.where(odd, far, near)
    for k in range(2):
        j = (leaf_cols - 1) * (1 - col % 2 if k == 0 else col % 2)
        to, base = (payload, points) if k == 0 else (outer, 0)
        for c in range(3 + rhs):
            ref, at = (coords, c) if c < 3 else (sources, c - 3)
            to[base + 6 * c : base + 6 * c + 1, :] = edges[pl.ds(c * edge_leaves + j, 1), :]
            for i in range(leaf_rows):
                to[base + 6 * c + 1 + i : base + 6 * c + 2 + i, :] = ref[pl.ds(at * leaves + i * leaf_cols + j, 1), :]
            to[base + 6 * c + 5 : base + 6 * c + 6, :] = edges[pl.ds(c * edge_leaves + leaf_cols + j, 1), :]
        to[base + 66 : base + side_rows, :] = jnp.zeros((side_rows - 66, points), f32)


def near_kernel(items, batch, weights, left, source_heights, source_halves, right, heights, halves, seed, acc, gaps, splats, kerns):
    acc[...] = seed[...]

    def subtract(item, n, gap, splat):
        source, target = item[:2]
        gap[n] = dot(left[source * points : (source + 1) * points, :], right[sixteen(target), :])
        splat[n] = jnp.broadcast_to(source_heights[source : source + 1, :], (points, points)).T

    def evaluate(item, n, gap, splat, kern):
        height = heights[pl.ds(item[1], 1), :]
        for g in range(points // 32):
            at_rows = slice(32 * g, 32 * g + 32)
            dx, dy, dz = gap[n, at_rows, :points], gap[n, at_rows, points:], splat[n, at_rows] - height
            distance_sq = dx * dx + dy * dy + dz * dz
            safe = jnp.maximum(distance_sq, 1e-30)
            turn = safe * lax.rsqrt(safe)
            f = turn - jnp.round(turn)
            u = f * f
            m = f * (((u + b2) * u + b1) * u + b0)
            value = (m * m - half_gain) * lax.rsqrt(distance_sq + eps_sq)
            high, low = split(value)
            kern[n, 0, at_rows] = high
            kern[n, 1, at_rows] = low

    def receive(leaf, weight, got):
        at = pl.ds(leaf * rhs if isinstance(leaf, int) else pl.multiple_of(leaf * rhs, rhs), rhs)
        acc[at, :] += (got[:rhs] + got[rhs:]) * weights[pl.ds(weight, 1), :]

    def apply(item, n, kern):
        source, target, weight, back = item
        pair = jnp.concatenate([kern[n, 0], kern[n, 1]], axis=1)
        got = dot(source_halves[sixteen(source), :], pair)
        receive(target, weight, got[:, :points] + got[:, points:])
        if back is not None:
            mine = halves[sixteen(target), :]
            receive(source, back, dot_t(jnp.concatenate([mine, mine], axis=1), pair))

    stages = [items[at : at + batch] for at in range(0, len(items), batch)]
    for k in range(-1, len(stages) + 1):
        if k >= 1:
            for n, item in enumerate(stages[k - 1]):
                apply(item, n, kerns.at[(k - 1) % ring])
        if k + 1 < len(stages):
            for n, item in enumerate(stages[k + 1]):
                subtract(item, n, gaps.at[(k + 1) % ring], splats.at[(k + 1) % ring])
        if 0 <= k < len(stages):
            for n, item in enumerate(stages[k]):
                evaluate(item, n, gaps.at[k % ring], splats.at[k % ring], kerns.at[k % ring])


def near_scratch(batch):
    return [
        pltpu.VMEM((ring, batch, points, 2 * points), f32),
        pltpu.VMEM((ring, batch, points, points), f32),
        pltpu.VMEM((ring, batch, 2, points, points), bf16),
    ]


def near_piece(items, weights, source_tables, target_tables, seed):
    batch = 4 if any(item[3] is not None for item in items) else 8
    left, source_heights, source_halves = source_tables
    right, heights, halves = target_tables
    return pl.pallas_call(
        functools.partial(near_kernel, items, batch),
        out_shape=jax.ShapeDtypeStruct(seed.shape, f32),
        in_specs=[vmem] * 8,
        out_specs=vmem,
        scratch_shapes=near_scratch(batch),
        compiler_params=params(24),
        cost_estimate=cost(len(items) * 110),
        name="near",
    )(weights, left, source_heights, source_halves, right, heights, halves, seed)


def finish_kernel(mine, theirs, blocks, expand, acc, out):
    coeffs = level(mine[:points, :], theirs[:points, :], blocks)
    for g in range(groups):
        here = coeffs[g * rhs : (g + 1) * rhs]
        rows = jnp.concatenate([jnp.where(lane_block(n), here, 0.0) for n in range(group)], axis=0)
        high, low = split(rows)
        e_high, e_low = split(expand[g * points : (g + 1) * points, :])
        got = dot(jnp.concatenate([high, low], axis=0), jnp.concatenate([e_high, e_low], axis=1))
        got = got[:, :points] + got[:, points:]
        got = got[: group * rhs] + got[group * rhs :]
        for n in range(group):
            leaf = g * group + n
            near = acc[leaf * rhs : (leaf + 1) * rhs, :] * near_gain
            out[pl.ds(leaf, rhs, stride=leaves), :] = near + got[n * rhs : (n + 1) * rhs]


def table_shapes(count):
    return (
        jax.ShapeDtypeStruct((count * points, 16), bf16),
        jax.ShapeDtypeStruct((count * 16, 2 * points), bf16),
        jax.ShapeDtypeStruct((count, points), f32),
        jax.ShapeDtypeStruct((count * 16, points), bf16),
    )


def partner_of(block, axis, distance):
    route = [(i, i ^ (1 << distance)) for i in range(lax.axis_size(axis))]
    return lax.ppermute(block, axis, route)


def array(*shape):
    return jax.ShapeDtypeStruct(shape, f32)


def small_call(body, name, out_shape, *operands):
    single = not isinstance(out_shape, tuple)
    return pl.pallas_call(
        body,
        out_shape=out_shape,
        in_specs=[vmem] * len(operands),
        out_specs=vmem if single else (vmem,) * len(out_shape),
        compiler_params=params(16),
        cost_estimate=cost(600),
        name=name,
    )(*operands)


def far_call(body, name, out_shape, scratch, *operands):
    return pl.pallas_call(
        body,
        out_shape=out_shape,
        in_specs=[pl.BlockSpec(memory_space=pltpu.HBM)] * len(operands),
        out_specs=(vmem,) * len(out_shape),
        scratch_shapes=scratch + [pltpu.SemaphoreType.DMA((8,))],
        compiler_params=params(24),
        cost_estimate=cost(2000),
        name=name,
    )(*[pltpu.with_memory_space_constraint(operand, pltpu.HBM) for operand in operands])


def tables_call(body, name, count, scratch, *operands):
    shapes = table_shapes(count)
    return pl.pallas_call(
        body,
        out_shape=(shapes[0], shapes[2], shapes[3]),
        in_specs=[vmem] * len(operands),
        out_specs=(vmem,) * 3,
        scratch_shapes=[pltpu.VMEM(shape, f32) for shape in [(1, count * 16, points)] + scratch],
        compiler_params=params(16),
        cost_estimate=cost(1000),
        name=name,
    )(*operands)


def outward(block, axis):
    size = lax.axis_size(axis)
    return lax.ppermute(block, axis, [(i, i + 1 if i % 2 else i - 1) for i in range(1, size - 1)])


def shards(coords, sources, neighbour_mask, compress, expand, row_transfer, col_transfer):
    coords = coords.reshape(-1, points)
    sources = sources.reshape(-1, points)
    halves, payload, outer = far_call(
        compress_kernel,
        "compress",
        (table_shapes(leaves)[3], array(points + edge_rows, points), array(edge_rows, points)),
        [pltpu.VMEM(shape, f32) for shape in ((3 * leaves, points), (rhs * leaves, points), (leaves * rank, points))],
        coords, sources, compress.reshape(-1, points),
    )
    facing_row = partner_of(payload, "row", 0)
    block_shape = jax.ShapeDtypeStruct((4, points, points), bf16)
    coords_later, payload = lax.optimization_barrier((coords, payload))
    left, right, heights, row_blocks, col_blocks, weights = pl.pallas_call(
        prep_kernel,
        out_shape=table_shapes(leaves)[:3] + (block_shape, block_shape, array(zero_row + 8, points)),
        in_specs=[vmem] * 4,
        out_specs=(vmem,) * 6,
        scratch_shapes=[pltpu.VMEM((3, leaves * 16, points), f32)],
        compiler_params=params(16),
        cost_estimate=cost(2000),
        name="prep",
    )(coords_later, neighbour_mask, row_transfer[:, 0, 0], col_transfer[:, 0, 0])
    own, targets = (left, heights, halves), (right, heights, halves)
    acc = jnp.zeros((leaves * rhs, points), f32)
    facing_row, acc, outer, weights = lax.optimization_barrier((facing_row, acc, outer, weights))

    inner, edge, side = interior_runs(), edge_runs(), side_runs()
    taken = {"inner": 0, "edge": 0, "side": 0}

    def some(kind, count):
        runs = {"inner": inner, "edge": edge, "side": side}[kind]
        first = taken[kind]
        taken[kind] = min(first + count, sum(run.count for run in runs))
        return listed(cut_runs(runs, first, taken[kind]))

    def window(sent, arriving, acc, *work):
        sent, acc = lax.optimization_barrier((sent, acc))
        for make, kind, count in work:
            acc = near_piece(some(kind, count), weights, make(acc), targets, acc)
        arriving, acc = lax.optimization_barrier((arriving, acc))
        return sent, arriving, acc

    def mine(acc):
        return own

    def next_level(payload, theirs, blocks):
        return small_call(level_kernel, "level", array(points, points), payload, theirs, blocks)

    outer, beyond_row, acc = window(outer, outward(outer, "row"), acc, (mine, "inner", 36))
    facing_row, beyond_row = lax.optimization_barrier((facing_row, beyond_row))
    payload = next_level(payload, facing_row, row_blocks)
    for bit, count in ((1, 52), (2, 60)):
        payload, theirs, acc = window(payload, partner_of(payload, "row", bit), acc, (mine, "inner", count))
        if bit == 1:
            payload = next_level(payload, theirs, row_blocks)
    payload, outer, edges = small_call(
        turn_kernel,
        "turn",
        (array(points + side_rows, points), array(side_rows, points), array((3 + rhs) * edge_leaves, points)),
        payload, theirs, row_blocks, coords, sources, facing_row, beyond_row,
    )
    tables = {}

    def around(acc):
        if "edge" not in tables:
            values, _ = lax.optimization_barrier((edges, acc))
            tables["edge"] = tables_call(edges_kernel, "edges", edge_leaves, [], coords, values)
        return tables["edge"]

    def beside(acc):
        values, _ = lax.optimization_barrier((beyond_col, acc))
        return tables_call(sides_kernel, "sides", side_leaves, [((3 + rhs) * side_leaves, points)], coords, facing_col, values)

    payload, facing_col, acc = window(payload, partner_of(payload, "col", 0), acc, (around, "edge", 48))
    outer, acc = lax.optimization_barrier((outer, acc))
    outer, beyond_col, acc = window(outer, outward(outer, "col"), acc, (mine, "inner", 36))
    facing_col, beyond_col = lax.optimization_barrier((facing_col, beyond_col))
    payload = next_level(payload, facing_col, col_blocks)
    works = {1: ((around, "edge", 48),), 2: ((beside, "side", 24), (mine, "inner", 16)), 3: ((mine, "inner", leaves * 9),)}
    for bit in range(1, lax.axis_size("col").bit_length() - 1):
        payload, theirs, acc = window(payload, partner_of(payload, "col", bit), acc, *works[bit])
        if bit < max(works):
            payload = next_level(payload, theirs, col_blocks)
    out = pl.pallas_call(
        finish_kernel,
        out_shape=array(rhs * leaves, points),
        in_specs=[vmem] * 5,
        out_specs=vmem,
        compiler_params=params(16),
        cost_estimate=cost(2000),
        name="finish",
    )(payload, theirs, col_blocks, expand.reshape(-1, points), acc)
    return out.reshape(rhs, leaf_rows, leaf_cols, points)


def solution(mesh):
    in_specs = (
        P(None, "row", "col", None),
        P(None, "row", "col", None),
        P(None, "row", "col"),
        P("row", "col", None, None),
        P("row", "col", None, None),
        P(None, "row", "col", None, None),
        P(None, "row", "col", None, None),
    )
    out_specs = P(None, "row", "col", None)
    return jax.shard_map(shards, mesh=mesh, in_specs=in_specs, out_specs=out_specs, check_vma=False)
```

```python
import functools

import jax
import jax.numpy as jnp
import numpy as np
from jax import lax
from jax.experimental import pallas as pl
from jax.experimental.pallas import tpu as pltpu
from jax.sharding import PartitionSpec as P

wave_number = 6.0
softening = 0.05
near_scale = 1.0 / 32.0
highest = lax.Precision.HIGHEST
f32, bf16 = jnp.float32, jnp.bfloat16

turns = wave_number / (2.0 * np.pi)
eps_sq = (softening * turns) ** 2
sine = (3.14157435, -5.16695951, 2.54064763, -0.55204997)
b0, b1, b2 = (sine[0] / sine[3], sine[1] / sine[3], sine[2] / sine[3])
half_gain = 1.0 / (2.0 * sine[3] ** 2)
near_gain = -2.0 * sine[3] ** 2 * turns * near_scale

leaf_rows, leaf_cols, points, rank, rhs = 4, 16, 128, 32, 8
leaves = leaf_rows * leaf_cols
edge_leaves = 2 * leaf_cols
side_leaves = 16
edge_rows = (3 + rhs) * leaf_cols
side_rows = 72
group = points // rank
groups = leaves // group
ring = 2
vmem = pl.BlockSpec(memory_space=pltpu.VMEM)


def params(mib):
    return pltpu.CompilerParams(vmem_limit_bytes=mib << 20)


def cost(cycles):
    return pl.CostEstimate(flops=int(cycles * 400_000), bytes_accessed=1 << 18, transcendentals=0)


class Run:
    def __init__(self, count, skip, source, step, target, offset, both):
        self.count, self.skip, self.source, self.step, self.target = count, skip, source, step, target
        self.offset, self.both = offset, both


def interior_runs():
    across, down = leaf_rows * (leaf_cols - 1), (leaf_rows - 1) * (leaf_cols - 1)
    return [
        Run(leaves, 0, 0, 1, 0, 4, False),
        Run(across, 1, 0, 1, 1, 3, True),
        Run(leaves - leaf_cols, 0, 0, 1, leaf_cols, 1, True),
        Run(down, 1, 0, 1, leaf_cols + 1, 0, True),
        Run(down, 1, 1, 1, leaf_cols, 2, True),
    ]


def edge_runs():
    runs = []
    for first, row, di in ((0, 0, -1), (leaf_cols, leaf_rows - 1, 1)):
        for dj in (-1, 0, 1):
            start = max(0, -dj)
            at = row * leaf_cols + start
            runs.append(Run(leaf_cols - abs(dj), 0, first + start + dj, 1, at, 3 * (di + 1) + dj + 1, False))
    return runs


def side_runs():
    runs = []
    for first, column, dj in ((0, 0, -1), (8, leaf_cols - 1, 1)):
        for di in (-1, 0, 1):
            runs.append(Run(leaf_rows, 0, first + 1 + di, leaf_cols, column, 3 * (di + 1) + dj + 1, False))
    return runs


def cut_runs(runs, first, last):
    pieces, at = [], 0
    for run in runs:
        low, high = max(first - at, 0), min(last - at, run.count)
        if low < high:
            pieces.append((run, low, high))
        at += run.count
    return pieces


zero_row = 9 * leaves


def listed(pieces):
    items = []
    for run, low, high in pieces:
        for q in range(low, high):
            moved = q + run.skip * (q // (leaf_cols - 1))
            source, target = moved + run.source, run.step * moved + run.target
            back = (8 - run.offset) * leaves + source if run.both else None
            items.append((source, target, run.offset * leaves + target, back))
    return items


def split(value):
    high = value.astype(bf16)
    return high, (value - high.astype(f32)).astype(bf16)


def thirds(value):
    high = value.astype(bf16).astype(f32)
    rest = value - high
    middle = rest.astype(bf16).astype(f32)
    return high, middle, rest - middle


def dot(left, right):
    return jnp.dot(left, right, preferred_element_type=f32)


def dot_t(left, right):
    return lax.dot_general(left, right, (((1,), (1,)), ((), ())), preferred_element_type=f32)


def sixteen(leaf):
    return pl.ds(leaf * 16 if isinstance(leaf, int) else pl.multiple_of(leaf * 16, 16), 16)


def fill_tables(count, start, coords, left, right, heights, wides):
    parts = []
    for c in range(3):
        moved = (coords[pl.ds(c * count, count), :] - start[c]) * turns
        if c == 2:
            heights[...] = moved
        parts.append(thirds(moved))
    k = lax.broadcasted_iota(jnp.int32, (16, points), 0)
    ones_x = jnp.where(k < 3, 1.0, 0.0)
    ones_y = jnp.where((k >= 3) & (k < 6), 1.0, 0.0)
    ones_t = jnp.where((k >= 6) & (k < 9), 1.0, 0.0)
    ones_z = jnp.where((k >= 9) & (k < 12), 1.0, 0.0)
    base = (0, 3, 9)
    for role in range(1 if right is None else 4):
        wide = wides.at[role]
        for leaf in range(count):
            wide[pl.ds(leaf * 16, 16), :] = (ones_t, ones_x, ones_y, ones_z)[role]
        for first in range(0, count, 8):
            for m in range(3):
                for c in range(3):
                    part = parts[c][m][first : first + 8]
                    if role == 0:
                        wide[pl.ds(first * 16 + base[c] + m, 8, stride=16), :] = part
                    elif role == c + 1:
                        wide[pl.ds(first * 16 + 6 + m, 8, stride=16), :] = -part
        if role == 0:
            for leaf in range(count):
                left[leaf * points : (leaf + 1) * points, :] = wide[leaf * 16 : leaf * 16 + 16, :].T.astype(bf16)
        else:
            right[:, points * (role - 1) : points * role] = wide[...].astype(bf16)


def lane_block(n):
    return lax.broadcasted_iota(jnp.int32, (rhs, points), 1) // rank == n


def spread_blocks(transfer, blocks):
    same = lax.broadcasted_iota(jnp.int32, (points, points), 0) // rank == lax.broadcasted_iota(jnp.int32, (points, points), 1) // rank
    for n in range(2):
        wide = jnp.concatenate([transfer[n]] * group, axis=1)
        wide = jnp.where(same, jnp.concatenate([wide] * group, axis=0), 0.0)
        blocks[2 * n], blocks[2 * n + 1] = split(wide)


def start_copies(fars, heres, arrived):
    copies = [pltpu.make_async_copy(far, here, arrived.at[n]) for n, (far, here) in enumerate(zip(fars, heres))]
    for copy in copies:
        copy.start()
    return copies


def compress_kernel(coords_far, sources_far, compress_far, halves, payload, coords, sources, compress, arrived):
    copies = start_copies((sources_far, coords_far, compress_far), (sources, coords, compress), arrived)
    copies[0].wait()
    for leaf in range(leaves):
        high, low = split(sources[pl.ds(leaf, rhs, stride=leaves), :])
        halves[sixteen(leaf), :] = jnp.concatenate([high, low], axis=0)
    copies[1].wait()
    odd = lax.axis_index("row") % 2
    for k in range(2):
        row = (leaf_rows - 1) * (1 - odd if k == 0 else odd)
        for c in range(3 + rhs):
            ref, at = (coords, c) if c < 3 else (sources, c - 3)
            to = points + k * edge_rows + c * leaf_cols
            payload[to : to + leaf_cols, :] = ref[pl.ds(pl.multiple_of(at * leaves + row * leaf_cols, 8), leaf_cols), :]
    copies[2].wait()
    for g in range(groups):
        high, low = split(compress[g * points : (g + 1) * points, :])
        got = dot_t(halves[g * 16 * group : (g + 1) * 16 * group, :], jnp.concatenate([high, low], axis=0))
        got = got[:, :points] + got[:, points:]
        total = jnp.zeros((rhs, points), f32)
        for n in range(group):
            total = jnp.where(lane_block(n), got[n * 16 : n * 16 + 8] + got[n * 16 + 8 : n * 16 + 16], total)
        payload[g * rhs : (g + 1) * rhs, :] = total


def prep_kernel(coords, mask, row_transfer, col_transfer, left, right, heights, row_blocks, col_blocks, weights, wides):
    start = [coords[c * leaves : c * leaves + 1, 0:1] for c in range(3)]
    fill_tables(leaves, start, coords, left, right, heights, wides)
    spread_blocks(row_transfer, row_blocks)
    spread_blocks(col_transfer, col_blocks)
    diagonal = lax.broadcasted_iota(jnp.int32, (leaf_cols, leaf_cols), 0) == lax.broadcasted_iota(jnp.int32, (leaf_cols, leaf_cols), 1)
    ones = jnp.ones((leaf_cols, points), bf16)
    for k in range(9):
        for i in range(leaf_rows):
            spread = jnp.where(diagonal, mask[k, i : i + 1, :].astype(f32), 0.0).astype(bf16)
            at = k * leaves + i * leaf_cols
            weights[at : at + leaf_cols, :] = dot(spread, ones)
    weights[zero_row : zero_row + 8, :] = jnp.zeros((8, points), f32)


def halo_tables(count, coords, values, left, heights, halves, wides):
    start = [coords[c * leaves : c * leaves + 1, 0:1] for c in range(3)]
    fill_tables(count, start, values, left, None, heights, wides)
    for leaf in range(count):
        high, low = split(values[pl.ds(3 * count + leaf, rhs, stride=count), :])
        halves[sixteen(leaf), :] = jnp.concatenate([high, low], axis=0)


def edges_kernel(coords, edges, left, heights, halves, wides):
    halo_tables(edge_leaves, coords, edges, left, heights, halves, wides)


def side_tables(coords, first, second, third, fourth, left, heights, halves, wides, sides):
    col = lax.axis_index("col")
    odd = col % 2 == 1
    inner = (col > 0) & (col < lax.axis_size("col") - 1)
    at = slice(points, points + side_rows)
    near = first[at, :]
    far = jnp.where((col % 8 == 3) | (col % 8 == 4), third[at, :], fourth[at, :])
    far = jnp.where((col % 4 == 1) | (col % 4 == 2), second[at, :], far)
    far = jnp.where(inner, far, 0.0)
    to_left, to_right = jnp.where(odd, near, far), jnp.where(odd, far, near)
    gap = jnp.zeros((2, points), f32)
    for c in range(3 + rhs):
        at = slice(6 * c, 6 * c + 6)
        sides[c * side_leaves : (c + 1) * side_leaves, :] = jnp.concatenate([to_left[at], gap, to_right[at], gap], axis=0)
    halo_tables(side_leaves, coords, sides, left, heights, halves, wides)


def level(mine, theirs, blocks):
    total = None
    for value, n in ((mine, 0), (theirs, 2)):
        high, low = split(value)
        got = dot_t(jnp.concatenate([high, low], axis=0), jnp.concatenate([blocks[n], blocks[n + 1]], axis=0))
        got = got[:, :points] + got[:, points:]
        got = got[:points] + got[points:]
        total = got if total is None else total + got
    return total


def level_kernel(forward, mine, theirs, blocks, payload):
    payload[:points, :] = level(mine[:points, :], theirs[:points, :], blocks)
    payload[points:, :] = theirs[forward:, :]


def turn_kernel(mine, theirs, blocks, coords, sources, first, second, payload, edges):
    payload[:points, :] = level(mine[:points, :], theirs[:points, :], blocks)
    row, col = lax.axis_index("row"), lax.axis_index("col")
    odd = row % 2 == 1
    around = (row % 4 == 1) | (row % 4 == 2)
    inner = (row > 0) & (row < lax.axis_size("row") - 1)
    for c in range(3 + rhs):
        at = slice(points + c * leaf_cols, points + (c + 1) * leaf_cols)
        near = first[at, :]
        far = jnp.where(inner, jnp.where(around, second[at, :], theirs[at, :]), 0.0)
        edges[c * edge_leaves : c * edge_leaves + leaf_cols, :] = jnp.where(odd, near, far)
        edges[c * edge_leaves + leaf_cols : (c + 1) * edge_leaves, :] = jnp.where(odd, far, near)
    for k in range(2):
        j = (leaf_cols - 1) * (1 - col % 2 if k == 0 else col % 2)
        base = points + k * side_rows
        for c in range(3 + rhs):
            ref, at = (coords, c) if c < 3 else (sources, c - 3)
            payload[base + 6 * c : base + 6 * c + 1, :] = edges[pl.ds(c * edge_leaves + j, 1), :]
            for i in range(leaf_rows):
                payload[base + 6 * c + 1 + i : base + 6 * c + 2 + i, :] = ref[pl.ds(at * leaves + i * leaf_cols + j, 1), :]
            payload[base + 6 * c + 5 : base + 6 * c + 6, :] = edges[pl.ds(c * edge_leaves + leaf_cols + j, 1), :]
        payload[base + 66 : base + side_rows, :] = jnp.zeros((side_rows - 66, points), f32)


def near_kernel(items, batch, weights, left, source_heights, source_halves, right, heights, halves, seed, acc, gaps, splats, kerns):
    acc[...] = seed[...]
    one_way = all(item[3] is None for item in items)

    def subtract(item, n, gap, splat):
        source, target = item[:2]
        here = left[source * points : (source + 1) * points, :]
        if one_way:
            gap[n] = dot(here, right[sixteen(target), :])
            return
        gap[n, :, : 2 * points] = dot(here, right[sixteen(target), : 2 * points])
        splat[n] = jnp.broadcast_to(source_heights[source : source + 1, :], (points, points)).T

    def evaluate(item, n, gap, splat, kern):
        height = heights[item[1] : item[1] + 1, :]
        for g in range(points // 32):
            at_rows = slice(32 * g, 32 * g + 32)
            dx, dy = gap[n, at_rows, :points], gap[n, at_rows, points : 2 * points]
            dz = gap[n, at_rows, 2 * points :] if one_way else splat[n, at_rows] - height
            distance_sq = dx * dx + dy * dy + dz * dz
            safe = jnp.maximum(distance_sq, 1e-30)
            turn = safe * lax.rsqrt(safe)
            f = turn - jnp.round(turn)
            u = f * f
            m = f * (((u + b2) * u + b1) * u + b0)
            value = (m * m - half_gain) * lax.rsqrt(distance_sq + eps_sq)
            high, low = split(value)
            kern[n, 0, at_rows] = high
            kern[n, 1, at_rows] = low

    def receive(leaf, weight, got):
        at = slice(leaf * rhs, (leaf + 1) * rhs)
        acc[at, :] += (got[:rhs] + got[rhs:]) * weights[weight : weight + 1, :]

    def apply(item, n, kern):
        source, target, weight, back = item
        pair = jnp.concatenate([kern[n, 0], kern[n, 1]], axis=1)
        got = dot(source_halves[sixteen(source), :], pair)
        receive(target, weight, got[:, :points] + got[:, points:])
        if back is not None:
            mine = halves[sixteen(target), :]
            receive(source, back, dot_t(jnp.concatenate([mine, mine], axis=1), pair))

    stages = [items[at : at + batch] for at in range(0, len(items), batch)]
    for k in range(-1, len(stages) + 1):
        if k >= 1:
            for n, item in enumerate(stages[k - 1]):
                apply(item, n, kerns.at[(k - 1) % ring])
        if k + 1 < len(stages):
            for n, item in enumerate(stages[k + 1]):
                subtract(item, n, gaps.at[(k + 1) % ring], splats.at[(k + 1) % ring])
        if 0 <= k < len(stages):
            for n, item in enumerate(stages[k]):
                evaluate(item, n, gaps.at[k % ring], splats.at[k % ring], kerns.at[k % ring])


def near_scratch(batch):
    return [
        pltpu.VMEM((ring, batch, points, 3 * points), f32),
        pltpu.VMEM((ring, batch, points, points), f32),
        pltpu.VMEM((ring, batch, 2, points, points), bf16),
    ]


def near_piece(pieces, weights, source_tables, target_tables, seed):
    items = listed(pieces)
    batch = 4 if any(item[3] is not None for item in items) else 8
    left, source_heights, source_halves = source_tables
    right, heights, halves = target_tables
    return pl.pallas_call(
        functools.partial(near_kernel, items, batch),
        out_shape=jax.ShapeDtypeStruct(seed.shape, f32),
        in_specs=[vmem] * 8,
        out_specs=vmem,
        scratch_shapes=near_scratch(batch),
        compiler_params=params(24),
        cost_estimate=cost(len(items) * 110),
        name="near",
    )(weights, left, source_heights, source_halves, right, heights, halves, seed)


def finish_kernel(
    items, weights, coords, first, second, third, theirs, mine, blocks, expand, right, heights, halves, seed, out,
    left, source_heights, source_halves, wides, sides, acc, gaps, splats, kerns, *far,
):
    side_tables(coords, first, second, third, theirs, left, source_heights, source_halves, wides, sides)
    coeffs = level(mine[:points, :], theirs[:points, :], blocks)
    for g in range(groups):
        here = coeffs[g * rhs : (g + 1) * rhs]
        rows = jnp.concatenate([jnp.where(lane_block(n), here, 0.0) for n in range(group)], axis=0)
        high, low = split(rows)
        e_high, e_low = split(expand[g * points : (g + 1) * points, :])
        got = dot(jnp.concatenate([high, low], axis=0), jnp.concatenate([e_high, e_low], axis=1))
        got = got[:, :points] + got[:, points:]
        far[0][g * group * rhs : (g + 1) * group * rhs, :] = got[: group * rhs] + got[group * rhs :]
    near_kernel(items, 8, weights, left, source_heights, source_halves, right, heights, halves, seed, acc, gaps, splats, kerns)
    order = sorted(range(leaves), key=lambda leaf: leaf % leaf_cols in (0, leaf_cols - 1))
    for leaf in order:
        at = slice(leaf * rhs, (leaf + 1) * rhs)
        out[pl.ds(leaf, rhs, stride=leaves), :] = acc[at, :] * near_gain + far[0][at, :]


def table_shapes(count):
    return (
        jax.ShapeDtypeStruct((count * points, 16), bf16),
        jax.ShapeDtypeStruct((count * 16, 3 * points), bf16),
        jax.ShapeDtypeStruct((count, points), f32),
        jax.ShapeDtypeStruct((count * 16, points), bf16),
    )


def partner_of(block, axis, distance):
    route = [(i, i ^ (1 << distance)) for i in range(lax.axis_size(axis))]
    return lax.ppermute(block, axis, route)


def array(*shape):
    return jax.ShapeDtypeStruct(shape, f32)


def small_call(body, name, out_shape, *operands):
    single = not isinstance(out_shape, tuple)
    return pl.pallas_call(
        body,
        out_shape=out_shape,
        in_specs=[vmem] * len(operands),
        out_specs=vmem if single else (vmem,) * len(out_shape),
        compiler_params=params(16),
        cost_estimate=cost(600),
        name=name,
    )(*operands)


def far_call(body, name, out_shape, scratch, *operands):
    return pl.pallas_call(
        body,
        out_shape=out_shape,
        in_specs=[pl.BlockSpec(memory_space=pltpu.HBM)] * len(operands),
        out_specs=(vmem,) * len(out_shape),
        scratch_shapes=scratch + [pltpu.SemaphoreType.DMA((8,))],
        compiler_params=params(24),
        cost_estimate=cost(2000),
        name=name,
    )(*[pltpu.with_memory_space_constraint(operand, pltpu.HBM) for operand in operands])


def shards(coords, sources, neighbour_mask, compress, expand, row_transfer, col_transfer):
    coords = coords.reshape(-1, points)
    sources = sources.reshape(-1, points)
    halves, payload = far_call(
        compress_kernel,
        "compress",
        (table_shapes(leaves)[3], array(points + 2 * edge_rows, points)),
        [pltpu.VMEM(shape, f32) for shape in ((3 * leaves, points), (rhs * leaves, points), (leaves * rank, points))],
        coords, sources, compress.reshape(-1, points),
    )
    row_bits, col_bits = (lax.axis_size(axis).bit_length() - 1 for axis in ("row", "col"))
    axes = ["row"] * row_bits + ["col"] * col_bits
    bits = [*range(row_bits), *range(col_bits)]
    theirs = partner_of(payload, "row", 0)
    block_shape = jax.ShapeDtypeStruct((4, points, points), bf16)
    coords_later, payload = lax.optimization_barrier((coords, payload))
    left, right, heights, row_blocks, col_blocks, weights = pl.pallas_call(
        prep_kernel,
        out_shape=table_shapes(leaves)[:3] + (block_shape, block_shape, array(zero_row + 8, points)),
        in_specs=[vmem] * 4,
        out_specs=(vmem,) * 6,
        scratch_shapes=[pltpu.VMEM((4, leaves * 16, points), f32)],
        compiler_params=params(16),
        cost_estimate=cost(2000),
        name="prep",
    )(coords_later, neighbour_mask, row_transfer[:, 0, 0], col_transfer[:, 0, 0])
    own, targets = (left, heights, halves), (right, heights, halves)
    inner, edge, side = interior_runs(), edge_runs(), side_runs()
    counts = [sum(run.count for run in runs) for runs in (inner, edge, side)]
    windows = row_bits + col_bits - 1
    edge_windows = (row_bits, row_bits + 2)
    inner_windows = [n for n in range(1, windows + 1) if n not in edge_windows]
    cuts = [counts[0] * k // len(inner_windows) // 4 * 4 for k in range(len(inner_windows))] + [counts[0]]
    half = -(-counts[1] // 2 // 8) * 8
    acc = jnp.zeros((leaves * rhs, points), f32)
    received = [theirs]
    for n, (axis, bit) in enumerate(zip(axes, bits)):
        blocks = row_blocks if axis == "row" else col_blocks
        if n > 0:
            theirs = partner_of(payload, axis, bit)
            payload, acc = lax.optimization_barrier((payload, acc))
            if n == row_bits:
                edges, acc = lax.optimization_barrier((edges, acc))
                shapes = table_shapes(edge_leaves)
                edge_tables = pl.pallas_call(
                    edges_kernel,
                    out_shape=(shapes[0], shapes[2], shapes[3]),
                    in_specs=[vmem] * 2,
                    out_specs=(vmem,) * 3,
                    scratch_shapes=[pltpu.VMEM((1, edge_leaves * 16, points), f32)],
                    compiler_params=params(16),
                    cost_estimate=cost(1000),
                    name="edges",
                )(coords, edges)
            if n in edge_windows:
                some = cut_runs(edge, 0, half) if n == row_bits else cut_runs(edge, half, counts[1])
                acc = near_piece(some, weights, edge_tables, targets, acc)
            else:
                k = inner_windows.index(n)
                acc = near_piece(cut_runs(inner, cuts[k], cuts[k + 1]), weights, own, targets, acc)
            theirs, acc = lax.optimization_barrier((theirs, acc))
            received.append(theirs)
        if n == row_bits - 1:
            payload, edges = small_call(
                turn_kernel,
                "turn",
                (array(points + 2 * side_rows, points), array((3 + rhs) * edge_leaves, points)),
                payload, theirs, blocks, coords, sources, received[0], received[1],
            )
        elif n < windows:
            rows = edge_rows if axis == "row" else side_rows
            skip = points + rows if bit == 0 else points
            payload = small_call(functools.partial(level_kernel, skip), "level", array(points + rows, points), payload, theirs, blocks)
    shapes = table_shapes(side_leaves)
    operands = (weights, coords, *received[row_bits:], payload, blocks, expand.reshape(-1, points), *targets, acc)
    out = pl.pallas_call(
        functools.partial(finish_kernel, listed(cut_runs(side, 0, counts[2]))),
        out_shape=array(rhs * leaves, points),
        in_specs=[vmem] * len(operands),
        out_specs=vmem,
        scratch_shapes=[pltpu.VMEM(shape.shape, shape.dtype) for shape in (shapes[0], shapes[2], shapes[3])]
        + [
            pltpu.VMEM((1, side_leaves * 16, points), f32),
            pltpu.VMEM(((3 + rhs) * side_leaves, points), f32),
            pltpu.VMEM((rhs * leaves, points), f32),
        ]
        + near_scratch(8)
        + [pltpu.VMEM((rhs * leaves, points), f32)],
        compiler_params=params(24),
        cost_estimate=cost(5000),
        name="finish",
    )(*operands)
    return out.reshape(rhs, leaf_rows, leaf_cols, points)


def solution(mesh):
    in_specs = (
        P(None, "row", "col", None),
        P(None, "row", "col", None),
        P(None, "row", "col"),
        P("row", "col", None, None),
        P("row", "col", None, None),
        P(None, "row", "col", None, None),
        P(None, "row", "col", None, None),
    )
    out_specs = P(None, "row", "col", None)
    return jax.shard_map(shards, mesh=mesh, in_specs=in_specs, out_specs=out_specs, check_vma=False)
```

```python
import functools

import jax
import jax.numpy as jnp
import numpy as np
from jax import lax
from jax.experimental import pallas as pl
from jax.experimental.pallas import tpu as pltpu
from jax.sharding import PartitionSpec as P

wave_number = 6.0
softening = 0.05
near_scale = 1.0 / 32.0
highest = lax.Precision.HIGHEST
f32, bf16 = jnp.float32, jnp.bfloat16

turns = wave_number / (2.0 * np.pi)
eps_sq = (softening * turns) ** 2
sine = (3.14157435, -5.16695951, 2.54064763, -0.55204997)
b0, b1, b2 = (sine[0] / sine[3], sine[1] / sine[3], sine[2] / sine[3])
half_gain = 1.0 / (2.0 * sine[3] ** 2)
near_gain = -2.0 * sine[3] ** 2 * turns * near_scale

leaf_rows, leaf_cols, points, rank, rhs = 4, 16, 128, 32, 8
leaves = leaf_rows * leaf_cols
edge_leaves = 2 * leaf_cols
side_leaves = 8
edge_rows = (3 + rhs) * leaf_cols
side_rows = 72
group = points // rank
groups = leaves // group
ring = 2
vmem = pl.BlockSpec(memory_space=pltpu.VMEM)


def params(mib):
    return pltpu.CompilerParams(vmem_limit_bytes=mib << 20)


def cost(cycles):
    return pl.CostEstimate(flops=int(cycles * 400_000), bytes_accessed=1 << 18, transcendentals=0)


class Run:
    def __init__(self, count, skip, source, step, target, offset, both):
        self.count, self.skip, self.source, self.step, self.target = count, skip, source, step, target
        self.offset, self.both = offset, both


def interior_runs():
    across, down = leaf_rows * (leaf_cols - 1), (leaf_rows - 1) * (leaf_cols - 1)
    return [
        Run(leaves, 0, 0, 1, 0, 4, False),
        Run(across, 1, 0, 1, 1, 3, True),
        Run(leaves - leaf_cols, 0, 0, 1, leaf_cols, 1, True),
        Run(down, 1, 0, 1, leaf_cols + 1, 0, True),
        Run(down, 1, 1, 1, leaf_cols, 2, True),
    ]


def edge_runs():
    runs = []
    for first, row, di in ((0, 0, -1), (leaf_cols, leaf_rows - 1, 1)):
        for dj in (-1, 0, 1):
            start = max(0, -dj)
            at = row * leaf_cols + start
            runs.append(Run(leaf_cols - abs(dj), 0, first + start + dj, 1, at, 3 * (di + 1) + dj + 1, False))
    return runs


def column_items(facing):
    right = lax.axis_index("col") % 2
    right = 1 - right if facing else right
    items = []
    for di in (-1, 0, 1):
        for i in range(leaf_rows):
            target = i * leaf_cols + (leaf_cols - 1) * right
            items.append((i + 1 + di, target, (3 * (di + 1) + 2 * right) * leaves + target, None))
    return items


def cut_runs(runs, first, last):
    pieces, at = [], 0
    for run in runs:
        low, high = max(first - at, 0), min(last - at, run.count)
        if low < high:
            pieces.append((run, low, high))
        at += run.count
    return pieces


zero_row = 9 * leaves


def listed(pieces):
    items = []
    for run, low, high in pieces:
        for q in range(low, high):
            moved = q + run.skip * (q // (leaf_cols - 1))
            source, target = moved + run.source, run.step * moved + run.target
            back = (8 - run.offset) * leaves + source if run.both else None
            items.append((source, target, run.offset * leaves + target, back))
    return items


def split(value):
    high = value.astype(bf16)
    return high, (value - high.astype(f32)).astype(bf16)


def thirds(value):
    high = value.astype(bf16).astype(f32)
    rest = value - high
    middle = rest.astype(bf16).astype(f32)
    return high, middle, rest - middle


def dot(left, right):
    return jnp.dot(left, right, preferred_element_type=f32)


def dot_t(left, right):
    return lax.dot_general(left, right, (((1,), (1,)), ((), ())), preferred_element_type=f32)


def sixteen(leaf):
    return pl.ds(leaf * 16 if isinstance(leaf, int) else pl.multiple_of(leaf * 16, 16), 16)


def fill_tables(count, start, coords, left, right, heights, wides):
    parts = []
    for c in range(3):
        moved = (coords[pl.ds(c * count, count), :] - start[c]) * turns
        if c == 2:
            heights[...] = moved
        else:
            parts.append(thirds(moved))
    k = lax.broadcasted_iota(jnp.int32, (16, points), 0)
    ones_x = jnp.where(k < 3, 1.0, 0.0)
    ones_y = jnp.where((k >= 3) & (k < 6), 1.0, 0.0)
    ones_t = jnp.where((k >= 6) & (k < 9), 1.0, 0.0)
    for role in range(1 if right is None else 3):
        wide = wides.at[role]
        for leaf in range(count):
            wide[pl.ds(leaf * 16, 16), :] = (ones_t, ones_x, ones_y)[role]
        for first in range(0, count, 8):
            for m in range(3):
                for c in range(2):
                    part = parts[c][m][first : first + 8]
                    if role == 0:
                        wide[pl.ds(first * 16 + 3 * c + m, 8, stride=16), :] = part
                    elif role == c + 1:
                        wide[pl.ds(first * 16 + 6 + m, 8, stride=16), :] = -part
        if role == 0:
            for leaf in range(count):
                left[leaf * points : (leaf + 1) * points, :] = wide[leaf * 16 : leaf * 16 + 16, :].T.astype(bf16)
        else:
            right[:, points * (role - 1) : points * role] = wide[...].astype(bf16)


def lane_block(n):
    return lax.broadcasted_iota(jnp.int32, (rhs, points), 1) // rank == n


def spread_blocks(transfer, blocks):
    same = lax.broadcasted_iota(jnp.int32, (points, points), 0) // rank == lax.broadcasted_iota(jnp.int32, (points, points), 1) // rank
    for n in range(2):
        wide = jnp.concatenate([transfer[n]] * group, axis=1)
        wide = jnp.where(same, jnp.concatenate([wide] * group, axis=0), 0.0)
        blocks[2 * n], blocks[2 * n + 1] = split(wide)


def start_copies(fars, heres, arrived):
    copies = [pltpu.make_async_copy(far, here, arrived.at[n]) for n, (far, here) in enumerate(zip(fars, heres))]
    for copy in copies:
        copy.start()
    return copies


def compress_kernel(coords_far, sources_far, compress_far, halves, payload, coords, sources, compress, arrived):
    copies = start_copies((sources_far, coords_far, compress_far), (sources, coords, compress), arrived)
    copies[0].wait()
    for leaf in range(leaves):
        high, low = split(sources[pl.ds(leaf, rhs, stride=leaves), :])
        halves[sixteen(leaf), :] = jnp.concatenate([high, low], axis=0)
    copies[1].wait()
    odd = lax.axis_index("row") % 2
    for k in range(2):
        row = (leaf_rows - 1) * (1 - odd if k == 0 else odd)
        for c in range(3 + rhs):
            ref, at = (coords, c) if c < 3 else (sources, c - 3)
            to = points + k * edge_rows + c * leaf_cols
            payload[to : to + leaf_cols, :] = ref[pl.ds(pl.multiple_of(at * leaves + row * leaf_cols, 8), leaf_cols), :]
    copies[2].wait()
    for g in range(groups):
        high, low = split(compress[g * points : (g + 1) * points, :])
        got = dot_t(halves[g * 16 * group : (g + 1) * 16 * group, :], jnp.concatenate([high, low], axis=0))
        got = got[:, :points] + got[:, points:]
        total = jnp.zeros((rhs, points), f32)
        for n in range(group):
            total = jnp.where(lane_block(n), got[n * 16 : n * 16 + 8] + got[n * 16 + 8 : n * 16 + 16], total)
        payload[g * rhs : (g + 1) * rhs, :] = total


def prep_kernel(coords, mask, row_transfer, col_transfer, left, right, heights, row_blocks, col_blocks, weights, wides):
    start = [coords[c * leaves : c * leaves + 1, 0:1] for c in range(3)]
    fill_tables(leaves, start, coords, left, right, heights, wides)
    spread_blocks(row_transfer, row_blocks)
    spread_blocks(col_transfer, col_blocks)
    diagonal = lax.broadcasted_iota(jnp.int32, (leaf_cols, leaf_cols), 0) == lax.broadcasted_iota(jnp.int32, (leaf_cols, leaf_cols), 1)
    ones = jnp.ones((leaf_cols, points), bf16)
    for k in range(9):
        for i in range(leaf_rows):
            spread = jnp.where(diagonal, mask[k, i : i + 1, :].astype(f32), 0.0).astype(bf16)
            at = k * leaves + i * leaf_cols
            weights[at : at + leaf_cols, :] = dot(spread, ones)
    weights[zero_row : zero_row + 8, :] = jnp.zeros((8, points), f32)


def halo_tables(count, coords, values, left, heights, halves, wides):
    start = [coords[c * leaves : c * leaves + 1, 0:1] for c in range(3)]
    fill_tables(count, start, values, left, None, heights, wides)
    for leaf in range(count):
        high, low = split(values[pl.ds(3 * count + leaf, rhs, stride=count), :])
        halves[sixteen(leaf), :] = jnp.concatenate([high, low], axis=0)


def edges_kernel(coords, edges, left, heights, halves, wides):
    halo_tables(edge_leaves, coords, edges, left, heights, halves, wides)


def column_tables(coords, column, left, heights, halves, wides, values):
    for c in range(3 + rhs):
        values[c * side_leaves : c * side_leaves + 6, :] = column[6 * c : 6 * c + 6]
        values[c * side_leaves + 6 : (c + 1) * side_leaves, :] = jnp.zeros((2, points), f32)
    halo_tables(side_leaves, coords, values, left, heights, halves, wides)


def facing_kernel(coords, first, left, heights, halves, wides, values):
    column_tables(coords, first[points : points + side_rows, :], left, heights, halves, wides, values)


def far_column(second, third, fourth):
    col = lax.axis_index("col")
    inner = (col > 0) & (col < lax.axis_size("col") - 1)
    at = slice(points, points + side_rows)
    far = jnp.where((col % 8 == 3) | (col % 8 == 4), third[at, :], fourth[at, :])
    far = jnp.where((col % 4 == 1) | (col % 4 == 2), second[at, :], far)
    return jnp.where(inner, far, 0.0)


def level(mine, theirs, blocks):
    total = None
    for value, n in ((mine, 0), (theirs, 2)):
        high, low = split(value)
        got = dot_t(jnp.concatenate([high, low], axis=0), jnp.concatenate([blocks[n], blocks[n + 1]], axis=0))
        got = got[:, :points] + got[:, points:]
        got = got[:points] + got[points:]
        total = got if total is None else total + got
    return total


def level_kernel(forward, mine, theirs, blocks, payload):
    payload[:points, :] = level(mine[:points, :], theirs[:points, :], blocks)
    payload[points:, :] = theirs[forward:, :]


def turn_kernel(mine, theirs, blocks, coords, sources, first, second, payload, edges):
    payload[:points, :] = level(mine[:points, :], theirs[:points, :], blocks)
    row, col = lax.axis_index("row"), lax.axis_index("col")
    odd = row % 2 == 1
    around = (row % 4 == 1) | (row % 4 == 2)
    inner = (row > 0) & (row < lax.axis_size("row") - 1)
    for c in range(3 + rhs):
        at = slice(points + c * leaf_cols, points + (c + 1) * leaf_cols)
        near = first[at, :]
        far = jnp.where(inner, jnp.where(around, second[at, :], theirs[at, :]), 0.0)
        edges[c * edge_leaves : c * edge_leaves + leaf_cols, :] = jnp.where(odd, near, far)
        edges[c * edge_leaves + leaf_cols : (c + 1) * edge_leaves, :] = jnp.where(odd, far, near)
    for k in range(2):
        j = (leaf_cols - 1) * (1 - col % 2 if k == 0 else col % 2)
        base = points + k * side_rows
        for c in range(3 + rhs):
            ref, at = (coords, c) if c < 3 else (sources, c - 3)
            payload[base + 6 * c : base + 6 * c + 1, :] = edges[pl.ds(c * edge_leaves + j, 1), :]
            for i in range(leaf_rows):
                payload[base + 6 * c + 1 + i : base + 6 * c + 2 + i, :] = ref[pl.ds(at * leaves + i * leaf_cols + j, 1), :]
            payload[base + 6 * c + 5 : base + 6 * c + 6, :] = edges[pl.ds(c * edge_leaves + leaf_cols + j, 1), :]
        payload[base + 66 : base + side_rows, :] = jnp.zeros((side_rows - 66, points), f32)


def near_kernel(items, batch, weights, left, source_heights, source_halves, right, heights, halves, seed, acc, gaps, splats, kerns):
    acc[...] = seed[...]
    items = items() if callable(items) else items

    def subtract(item, n, gap, splat):
        source, target = item[:2]
        gap[n] = dot(left[source * points : (source + 1) * points, :], right[sixteen(target), :])
        splat[n] = jnp.broadcast_to(source_heights[source : source + 1, :], (points, points)).T

    def evaluate(item, n, gap, splat, kern):
        height = heights[pl.ds(item[1], 1), :]
        for g in range(points // 32):
            at_rows = slice(32 * g, 32 * g + 32)
            dx, dy, dz = gap[n, at_rows, :points], gap[n, at_rows, points:], splat[n, at_rows] - height
            distance_sq = dx * dx + dy * dy + dz * dz
            safe = jnp.maximum(distance_sq, 1e-30)
            turn = safe * lax.rsqrt(safe)
            f = turn - jnp.round(turn)
            u = f * f
            m = f * (((u + b2) * u + b1) * u + b0)
            value = (m * m - half_gain) * lax.rsqrt(distance_sq + eps_sq)
            high, low = split(value)
            kern[n, 0, at_rows] = high
            kern[n, 1, at_rows] = low

    def receive(leaf, weight, got):
        at = pl.ds(leaf * rhs if isinstance(leaf, int) else pl.multiple_of(leaf * rhs, rhs), rhs)
        acc[at, :] += (got[:rhs] + got[rhs:]) * weights[pl.ds(weight, 1), :]

    def apply(item, n, kern):
        source, target, weight, back = item
        pair = jnp.concatenate([kern[n, 0], kern[n, 1]], axis=1)
        got = dot(source_halves[sixteen(source), :], pair)
        receive(target, weight, got[:, :points] + got[:, points:])
        if back is not None:
            mine = halves[sixteen(target), :]
            receive(source, back, dot_t(jnp.concatenate([mine, mine], axis=1), pair))

    stages = [items[at : at + batch] for at in range(0, len(items), batch)]
    for k in range(-1, len(stages) + 1):
        if k >= 1:
            for n, item in enumerate(stages[k - 1]):
                apply(item, n, kerns.at[(k - 1) % ring])
        if k + 1 < len(stages):
            for n, item in enumerate(stages[k + 1]):
                subtract(item, n, gaps.at[(k + 1) % ring], splats.at[(k + 1) % ring])
        if 0 <= k < len(stages):
            for n, item in enumerate(stages[k]):
                evaluate(item, n, gaps.at[k % ring], splats.at[k % ring], kerns.at[k % ring])


def near_scratch(batch):
    return [
        pltpu.VMEM((ring, batch, points, 2 * points), f32),
        pltpu.VMEM((ring, batch, points, points), f32),
        pltpu.VMEM((ring, batch, 2, points, points), bf16),
    ]


def near_piece(items, weights, source_tables, target_tables, seed):
    if callable(items):
        count, batch = 3 * leaf_rows, 4
    else:
        count, batch = len(items), 4 if any(item[3] is not None for item in items) else 8
    left, source_heights, source_halves = source_tables
    right, heights, halves = target_tables
    return pl.pallas_call(
        functools.partial(near_kernel, items, batch),
        out_shape=jax.ShapeDtypeStruct(seed.shape, f32),
        in_specs=[vmem] * 8,
        out_specs=vmem,
        scratch_shapes=near_scratch(batch),
        compiler_params=params(24),
        cost_estimate=cost(count * 110),
        name="near",
    )(weights, left, source_heights, source_halves, right, heights, halves, seed)


def finish_kernel(
    weights, coords, second, third, theirs, mine, blocks, expand, right, heights, halves, seed, out,
    left, source_heights, source_halves, wides, sides, acc, gaps, splats, kerns, *far,
):
    column_tables(coords, far_column(second, third, theirs), left, source_heights, source_halves, wides, sides)
    coeffs = level(mine[:points, :], theirs[:points, :], blocks)
    for g in range(groups):
        here = coeffs[g * rhs : (g + 1) * rhs]
        rows = jnp.concatenate([jnp.where(lane_block(n), here, 0.0) for n in range(group)], axis=0)
        high, low = split(rows)
        e_high, e_low = split(expand[g * points : (g + 1) * points, :])
        got = dot(jnp.concatenate([high, low], axis=0), jnp.concatenate([e_high, e_low], axis=1))
        got = got[:, :points] + got[:, points:]
        far[0][g * group * rhs : (g + 1) * group * rhs, :] = got[: group * rhs] + got[group * rhs :]
    near_kernel(functools.partial(column_items, False), 4, weights, left, source_heights, source_halves, right, heights, halves, seed, acc, gaps, splats, kerns)
    order = sorted(range(leaves), key=lambda leaf: leaf % leaf_cols in (0, leaf_cols - 1))
    for leaf in order:
        at = slice(leaf * rhs, (leaf + 1) * rhs)
        out[pl.ds(leaf, rhs, stride=leaves), :] = acc[at, :] * near_gain + far[0][at, :]


def table_shapes(count):
    return (
        jax.ShapeDtypeStruct((count * points, 16), bf16),
        jax.ShapeDtypeStruct((count * 16, 2 * points), bf16),
        jax.ShapeDtypeStruct((count, points), f32),
        jax.ShapeDtypeStruct((count * 16, points), bf16),
    )


def partner_of(block, axis, distance):
    route = [(i, i ^ (1 << distance)) for i in range(lax.axis_size(axis))]
    return lax.ppermute(block, axis, route)


def array(*shape):
    return jax.ShapeDtypeStruct(shape, f32)


def small_call(body, name, out_shape, *operands):
    single = not isinstance(out_shape, tuple)
    return pl.pallas_call(
        body,
        out_shape=out_shape,
        in_specs=[vmem] * len(operands),
        out_specs=vmem if single else (vmem,) * len(out_shape),
        compiler_params=params(16),
        cost_estimate=cost(600),
        name=name,
    )(*operands)


def far_call(body, name, out_shape, scratch, *operands):
    return pl.pallas_call(
        body,
        out_shape=out_shape,
        in_specs=[pl.BlockSpec(memory_space=pltpu.HBM)] * len(operands),
        out_specs=(vmem,) * len(out_shape),
        scratch_shapes=scratch + [pltpu.SemaphoreType.DMA((8,))],
        compiler_params=params(24),
        cost_estimate=cost(2000),
        name=name,
    )(*[pltpu.with_memory_space_constraint(operand, pltpu.HBM) for operand in operands])


def tables_call(body, name, count, scratch, *operands):
    shapes = table_shapes(count)
    return pl.pallas_call(
        body,
        out_shape=(shapes[0], shapes[2], shapes[3]),
        in_specs=[vmem] * len(operands),
        out_specs=(vmem,) * 3,
        scratch_shapes=[pltpu.VMEM(shape, f32) for shape in [(1, count * 16, points)] + scratch],
        compiler_params=params(16),
        cost_estimate=cost(1000),
        name=name,
    )(*operands)


def shards(coords, sources, neighbour_mask, compress, expand, row_transfer, col_transfer):
    coords = coords.reshape(-1, points)
    sources = sources.reshape(-1, points)
    halves, payload = far_call(
        compress_kernel,
        "compress",
        (table_shapes(leaves)[3], array(points + 2 * edge_rows, points)),
        [pltpu.VMEM(shape, f32) for shape in ((3 * leaves, points), (rhs * leaves, points), (leaves * rank, points))],
        coords, sources, compress.reshape(-1, points),
    )
    row_bits, col_bits = (lax.axis_size(axis).bit_length() - 1 for axis in ("row", "col"))
    axes = ["row"] * row_bits + ["col"] * col_bits
    bits = [*range(row_bits), *range(col_bits)]
    theirs = partner_of(payload, "row", 0)
    block_shape = jax.ShapeDtypeStruct((4, points, points), bf16)
    coords_later, payload = lax.optimization_barrier((coords, payload))
    left, right, heights, row_blocks, col_blocks, weights = pl.pallas_call(
        prep_kernel,
        out_shape=table_shapes(leaves)[:3] + (block_shape, block_shape, array(zero_row + 8, points)),
        in_specs=[vmem] * 4,
        out_specs=(vmem,) * 6,
        scratch_shapes=[pltpu.VMEM((3, leaves * 16, points), f32)],
        compiler_params=params(16),
        cost_estimate=cost(2000),
        name="prep",
    )(coords_later, neighbour_mask, row_transfer[:, 0, 0], col_transfer[:, 0, 0])
    own, targets = (left, heights, halves), (right, heights, halves)
    inner, edge = interior_runs(), edge_runs()
    counts = [sum(run.count for run in runs) for runs in (inner, edge)]
    windows = row_bits + col_bits - 1
    edge_windows = (row_bits, row_bits + 2)
    inner_windows = [n for n in range(1, windows + 1) if n not in edge_windows]
    parts = (64, 66, 64, 68)
    cuts = [counts[0] * sum(parts[:k]) // sum(parts) // 4 * 4 for k in range(len(parts))] + [counts[0]]
    half = counts[1] // 2 // 8 * 8 + 12
    acc = jnp.zeros((leaves * rhs, points), f32)
    received = [theirs]
    for n, (axis, bit) in enumerate(zip(axes, bits)):
        blocks = row_blocks if axis == "row" else col_blocks
        if n > 0:
            theirs = partner_of(payload, axis, bit)
            payload, acc = lax.optimization_barrier((payload, acc))
            if n == row_bits:
                edges, acc = lax.optimization_barrier((edges, acc))
                edge_tables = tables_call(edges_kernel, "edges", edge_leaves, [], coords, edges)
            if n == row_bits + 1:
                first, acc = lax.optimization_barrier((received[row_bits], acc))
                facing_tables = tables_call(facing_kernel, "facing", side_leaves, [((3 + rhs) * side_leaves, points)], coords, first)
            if n in edge_windows:
                some = cut_runs(edge, 0, half) if n == row_bits else cut_runs(edge, half, counts[1])
                acc = near_piece(listed(some), weights, edge_tables, targets, acc)
            else:
                k = inner_windows.index(n)
                acc = near_piece(listed(cut_runs(inner, cuts[k], cuts[k + 1])), weights, own, targets, acc)
            if n == edge_windows[1]:
                acc = near_piece(functools.partial(column_items, True), weights, facing_tables, targets, acc)
            theirs, acc = lax.optimization_barrier((theirs, acc))
            received.append(theirs)
        if n == row_bits - 1:
            payload, edges = small_call(
                turn_kernel,
                "turn",
                (array(points + 2 * side_rows, points), array((3 + rhs) * edge_leaves, points)),
                payload, theirs, blocks, coords, sources, received[0], received[1],
            )
        elif n < windows:
            rows = edge_rows if axis == "row" else side_rows
            skip = points + rows if bit == 0 else points
            payload = small_call(functools.partial(level_kernel, skip), "level", array(points + rows, points), payload, theirs, blocks)
    shapes = table_shapes(side_leaves)
    operands = (weights, coords, *received[row_bits + 1 :], payload, blocks, expand.reshape(-1, points), *targets, acc)
    out = pl.pallas_call(
        finish_kernel,
        out_shape=array(rhs * leaves, points),
        in_specs=[vmem] * len(operands),
        out_specs=vmem,
        scratch_shapes=[pltpu.VMEM(shape.shape, shape.dtype) for shape in (shapes[0], shapes[2], shapes[3])]
        + [
            pltpu.VMEM((1, side_leaves * 16, points), f32),
            pltpu.VMEM(((3 + rhs) * side_leaves, points), f32),
            pltpu.VMEM((rhs * leaves, points), f32),
        ]
        + near_scratch(4)
        + [pltpu.VMEM((rhs * leaves, points), f32)],
        compiler_params=params(24),
        cost_estimate=cost(5000),
        name="finish",
    )(*operands)
    return out.reshape(rhs, leaf_rows, leaf_cols, points)


def solution(mesh):
    in_specs = (
        P(None, "row", "col", None),
        P(None, "row", "col", None),
        P(None, "row", "col"),
        P("row", "col", None, None),
        P("row", "col", None, None),
        P(None, "row", "col", None, None),
        P(None, "row", "col", None, None),
    )
    out_specs = P(None, "row", "col", None)
    return jax.shard_map(shards, mesh=mesh, in_specs=in_specs, out_specs=out_specs, check_vma=False)
```
